32 devices in a mesh: dp: 8 (over z, x), head: 4 (over y, core).
Axes of the slice: x: 2, y: 2, z: 4, core: 2. Of those that a mesh axis runs over, the one named last changes fastest.
Arguments:
- tokens: bfloat16 [48, 512, 768], P('dp'), may hold values from -6 to 6
- query_weight: bfloat16 [768, 768], P('dp', 'head'), may hold values from -0.21875 to 0.21875
- query_bias: float32 [768], P('head'), may hold values from -3 to 3
- key_weight: bfloat16 [768, 768], P('dp', 'head'), may hold values from -0.21875 to 0.21875
- value_weight: bfloat16 [768, 768], P('dp', 'head'), may hold values from -0.21875 to 0.21875
- value_bias: float32 [768], P('head'), may hold values from -0.3125 to 0.3125
- out_weight: bfloat16 [768, 768], P('head', 'dp'), may hold values from -2.5 to 2.5
- out_bias: float32 [768], replicated, may hold values from -1.75 to 1.75
- first_gain: float32 [768], replicated, may hold values from 0.25 to 1.75
- first_shift: float32 [768], replicated, may hold values from -1.75 to 1.75
- up_weight: bfloat16 [768, 3072], P('dp', 'head'), may hold values from -0.21875 to 0.21875
- up_bias: float32 [3072], P('head'), may hold values from -1.75 to 1.75
- down_weight: bfloat16 [3072, 768], P('head', 'dp'), may hold values from -0.109375 to 0.109375
- down_bias: float32 [768], replicated, may hold values from -1.75 to 1.75
- second_gain: float32 [768], replicated, may hold values from 0.25 to 1.75
- second_shift: float32 [768], replicated, may hold values from -1.75 to 1.75
- block_order: int32 [12], P('head'), may hold values from 0 to 1, as said below
- masked_rows: int32 [48, 128], P('dp'), may hold values from -1 to 511, as said below
- out_grad: bfloat16 [48, 128, 768], P('dp'), may hold values from -6 to 6
Outputs:
- out_y: bfloat16 [48, 512, 768], P('dp', 'head')
- grad_x: bfloat16 [48, 512, 768], P('dp', 'head')
- grad_query_weight: float32 [768, 768], P('dp', 'head')
- grad_query_bias: float32 [768], replicated
- grad_key_weight: float32 [768, 768], P('dp', 'head')
- grad_value_weight: float32 [768, 768], P('dp', 'head')
- grad_value_bias: float32 [768], replicated
- grad_out_weight: float32 [768, 768], P('head', 'dp')
- grad_out_bias: float32 [768], replicated
- grad_first_gain: float32 [768], replicated
- grad_first_shift: float32 [768], replicated
- grad_up_weight: float32 [768, 3072], P('dp', 'head')
- grad_up_bias: float32 [3072], replicated
- grad_down_weight: float32 [3072, 768], P('head', 'dp')
- grad_down_bias: float32 [768], replicated
- grad_second_gain: float32 [768], replicated
- grad_second_shift: float32 [768], replicated
The draws below stay inside these ranges and needn't reach their ends.
Inputs may be any that keep to these rules, and one draw needn't show every extreme that they name: `block_order`: exactly 6 entries are 1, the others 0. `masked_rows`: each row lists distinct positions of its query block in any order, -1 marking an empty slot. Of each aligned run of 128 positions of a block at least one and at most 32 are listed, and some run lists exactly 32.
All inputs are finite; a program needn't handle non-finite values.
Results may differ from the reference program's by a relative error of at most 0.015.
The reference program's roundings to bfloat16 on the way count: a program that leaves them out, or rounds other values in their place, can miss the bound.
Values may be sent and summed in bfloat16 or wider, within the bound.
A program may use at most 128 MiB of HBM per device.

```python
import jax
import jax.numpy as jnp
from jax import lax

D = 768
HEADS = 12
HD = 64
FF = 3072
QB = 512
BLOCKS = 48
SHARE = 128
CAP = 32
MMAX = 128


def draw_block_order(key, part):
    scores = jax.random.randint(key, (HEADS,), 0, 1 << 20) * HEADS + jnp.arange(HEADS)
    ranking = jnp.argsort(jnp.argsort(scores))
    return (ranking < HEADS // 2).astype(jnp.int32)


def draw_masked_rows(key, part):
    run_total = MMAX // CAP
    key_first, key_second, key_order, key_mix = jax.random.split(key, 4)
    least = max(1, SHARE // 20)
    spread = CAP - least + 1
    first_draw = jax.random.randint(key_first, (BLOCKS, run_total), 0, spread)
    second_draw = jax.random.randint(key_second, (BLOCKS, run_total), 0, spread)
    counts = least + first_draw * second_draw // spread
    counts = counts.at[0, 0].set(CAP)
    scores = jax.random.randint(key_order, (BLOCKS, run_total, SHARE), 0, 1 << 16) * SHARE + jnp.arange(SHARE)
    ordering = jnp.argsort(scores, axis=-1)[:, :, :CAP]
    positions = ordering + (jnp.arange(run_total) * SHARE)[None, :, None]
    alive = jnp.arange(CAP)[None, None, :] < counts[:, :, None]
    listing = jnp.where(alive, positions, -1).reshape(BLOCKS, MMAX)
    mixing = jax.random.randint(key_mix, (BLOCKS, MMAX), 0, 1 << 16) * MMAX + jnp.arange(MMAX)
    shuffle = jnp.argsort(mixing, axis=-1)
    return jnp.take_along_axis(listing, shuffle, axis=-1).astype(jnp.int32)


def strengthened(values, own_key, source, target, parts, factor):
    owner, partner = [(jnp.arange(values.shape[position]) // (values.shape[position] // parts)).reshape([-1 if axis == position else 1 for axis in range(values.ndim)]) for position in (source, target)]
    chosen = jax.random.permutation(own_key, parts)[partner]
    strong = (owner == chosen) | (owner == (partner + parts // 2) % parts)
    return jnp.where(strong, factor * values, values)


def block_levels(own_key, shape, cuts, low, top_value):
    def one(position, parts):
        draws = jax.random.uniform(jax.random.fold_in(jax.random.fold_in(own_key, 6), position), (parts,), jnp.float32, low / len(cuts), top_value / len(cuts))
        return jnp.repeat(jnp.exp(draws), shape[position] // parts).reshape((-1,) + (1,) * (len(shape) - position - 1))

    factor_of = one(*cuts[0])
    for cut in cuts[1:]:
        factor_of = factor_of * one(*cut)
    return factor_of


def gaussian(own_key, shape, scale, reach, cuts=(), held_as=jnp.bfloat16):
    loudness = block_levels(own_key, shape, cuts, -0.22, 0.18) if cuts else 1.0
    entries = jax.random.normal(own_key, shape, jnp.float32) * scale * loudness
    return jnp.minimum(jnp.maximum(entries, -reach), reach).astype(held_as)


def noise_with(rng, shape, scale, bound, cuts, heavy, dtype=jnp.bfloat16):
    drawn = scale * jax.random.normal(rng, shape, jnp.float32)
    if cuts:
        drawn = drawn * block_levels(rng, shape, cuts, -0.22, 0.18)
    return jnp.clip(strengthened(drawn, jax.random.fold_in(rng, 3), *heavy), -bound, bound).astype(dtype)


def setup_inputs(seed: int = 0) -> dict:
    splits = jax.random.split(jax.random.key(seed), 20)
    return {
        "tokens": noise_with(splits[0], (BLOCKS, QB, D), 1.0, 6.0, ((0, 8),), (0, 2, 8, 2.0)),
        "query_weight": gaussian(splits[1], (D, HEADS * HD), D ** -0.5, 0.21875, ((0, 8), (1, 4))),
        "query_bias": gaussian(splits[2], (HEADS * HD,), 0.5, 3.0, ((0, 4),), jnp.float32),
        "key_weight": gaussian(splits[3], (D, HEADS * HD), D ** -0.5, 0.21875, ((0, 8), (1, 4))),
        "value_weight": gaussian(splits[4], (D, HEADS * HD), D ** -0.5, 0.21875, ((0, 8), (1, 4))),
        "value_bias": gaussian(splits[5], (HEADS * HD,), 0.05, 0.3125, ((0, 4),), jnp.float32),
        "out_weight": gaussian(splits[6], (HEADS * HD, D), (HEADS * HD * 4 // QB) ** -0.5, 2.5, ((0, 4), (1, 8))),
        "out_bias": gaussian(splits[7], (D,), 0.3, 1.75, (), jnp.float32),
        "first_gain": jnp.clip(1.0 + 0.15 * jax.random.normal(splits[8], (D,), jnp.float32), 0.25, 1.75),
        "first_shift": gaussian(splits[9], (D,), 0.3, 1.75, (), jnp.float32),
        "up_weight": gaussian(splits[10], (D, FF), D ** -0.5, 0.21875, ((0, 8), (1, 4))),
        "up_bias": gaussian(splits[11], (FF,), 0.3, 1.75, ((0, 4),), jnp.float32),
        "down_weight": gaussian(splits[12], (FF, D), FF ** -0.5, 0.109375, ((0, 4), (1, 8))),
        "down_bias": gaussian(splits[13], (D,), 0.3, 1.75, (), jnp.float32),
        "second_gain": jnp.clip(1.0 + 0.15 * jax.random.normal(splits[14], (D,), jnp.float32), 0.25, 1.75),
        "second_shift": gaussian(splits[15], (D,), 0.3, 1.75, (), jnp.float32),
        "block_order": draw_block_order(jax.random.fold_in(splits[19], 71), 0),
        "masked_rows": draw_masked_rows(jax.random.fold_in(splits[19], 71), 0),
        "out_grad": noise_with(splits[18], (BLOCKS, MMAX, D), 1.0, 6.0, ((0, 8),), (0, 2, 8, 2.0)),
    }


@jax.custom_vjp
def low(v):
    return lax.optimization_barrier(v.astype(jnp.bfloat16)).astype(jnp.float32)

@jax.custom_vjp
def low_back(v):
    return v

def low_keep(v):
    return (low(v), None)

def low_pass(kept, grad):
    return (grad,)

def back_keep(v):
    return (v, None)

def back_low(kept, grad):
    return (low(grad),)
low.defvjp(low_keep, low_pass)
low_back.defvjp(back_keep, back_low)
EPSILON = 1e-12
HIGHEST_PRECISION = lax.Precision.HIGHEST

def normalize(row_sums, norm_gain, norm_shift):
    centered = row_sums - lax.optimization_barrier(jnp.mean(row_sums, axis=-1, keepdims=True))
    inverse = lax.rsqrt(lax.optimization_barrier(jnp.mean(centered * centered, axis=-1, keepdims=True)) + EPSILON)
    return centered * inverse * norm_gain + norm_shift

def product(operand, weights):
    return jnp.dot(operand, weights, precision=HIGHEST_PRECISION)

def layer(params, block_x, swapped):
    w_query, b_query, w_key, w_value, b_value, w_out, b_out, gain_one, shift_one, w_up, b_up, w_down, b_down, gain_two, shift_two = params
    token_rows = block_x.reshape(-1, D)
    head_shape = block_x.shape[:3] + (HEADS, HD)
    queries = low_back(low(product(token_rows, w_query) + b_query)).reshape(head_shape)
    keys_all = low_back(low(product(token_rows, w_key))).reshape(head_shape)
    values_all = low_back(low(product(token_rows, w_value) + b_value)).reshape(head_shape)
    flipped = swapped[None, None, None, :, None]
    keys_used = jnp.where(flipped, keys_all[::-1], keys_all)
    values_used = jnp.where(flipped, values_all[::-1], values_all)
    score_scale = HD ** (-0.5)

    def attend(block_items):
        query_rows, key_rows, value_rows = block_items
        scores = low_back(jnp.einsum('qhd,khd->hqk', query_rows, key_rows, precision=HIGHEST_PRECISION) * score_scale)
        probs = low(jax.nn.softmax(scores, axis=-1))
        return low_back(low(jnp.einsum('hqk,khd->qhd', probs, value_rows, precision=HIGHEST_PRECISION)))
    packed = (-1, QB, HEADS, HD)
    mixed = lax.map(jax.checkpoint(attend), (queries.reshape(packed), keys_used.reshape(packed), values_used.reshape(packed)))
    attention = mixed.reshape(-1, HEADS * HD)
    branch_out = low_back(product(attention, w_out) + b_out)
    hidden = normalize(token_rows + branch_out, gain_one, shift_one)
    hidden_low = low(hidden)
    pre_gelu = low_back(product(hidden_low, w_up) + b_up)
    activated = low(jax.nn.gelu(pre_gelu, approximate=False))
    feed_out = low_back(product(activated, w_down) + b_down)
    return normalize(hidden + feed_out, gain_two, shift_two).reshape(block_x.shape)

def to_groups(array):
    shaped = array.reshape((2, array.shape[0] // 4, 2) + array.shape[1:])
    return jnp.moveaxis(shaped, 1, 0)

def from_groups(array):
    shaped = jnp.moveaxis(array, 0, 1)
    return shaped.reshape((-1,) + shaped.shape[3:])

def add_pair(first_term, second_term):
    return first_term + second_term

def reference(tokens, query_weight, query_bias, key_weight, value_weight, value_bias, out_weight, out_bias, first_gain, first_shift, up_weight, up_bias, down_weight, down_bias, second_gain, second_shift, block_order, masked_rows, out_grad):
    weights = (query_weight, query_bias, key_weight, value_weight, value_bias, out_weight, out_bias, first_gain, first_shift, up_weight, up_bias, down_weight, down_bias, second_gain, second_shift)
    params = tuple((entry.astype(jnp.float32) for entry in weights))
    swapped = block_order == 1
    row_index = jnp.arange(QB).astype(jnp.int32)

    def run_layer(param_tuple, block_x):
        return layer(param_tuple, block_x, swapped)

    def step(totals, block_items):
        block_x, listed_rows, grad_slots = block_items
        matches = (listed_rows[..., :, None] == row_index).astype(jnp.float32)
        dense_grad = jnp.einsum('bsmq,bsmd->bsqd', matches, grad_slots, precision=HIGHEST_PRECISION)
        output, backward = jax.vjp(run_layer, params, block_x)
        gradients, grad_tokens = backward(dense_grad)
        totals = jax.tree.map(add_pair, totals, gradients)
        return (totals, (output.astype(jnp.bfloat16), grad_tokens.astype(jnp.bfloat16)))
    zero_grads = tuple((jnp.zeros_like(entry) for entry in params))
    totals, (outputs, grad_inputs) = lax.scan(step, zero_grads, (to_groups(tokens.astype(jnp.float32)), to_groups(masked_rows), to_groups(out_grad.astype(jnp.float32))))
    return (from_groups(outputs), from_groups(grad_inputs), totals[0], totals[1], totals[2], totals[3], totals[4], totals[5], totals[6], totals[7], totals[8], totals[9], totals[10], totals[11], totals[12], totals[13], totals[14])
```

```python
import functools

import jax
import jax.numpy as jnp
from jax import lax
from jax.experimental import pallas as pl
from jax.experimental.pallas import tpu as pltpu
from jax.sharding import PartitionSpec as P

HEADS = 12
HD = 64
FF = 3072
EPSILON = 1e-12
F32 = jnp.float32
BF16 = jnp.bfloat16
SCALE = HD ** (-0.5)


def flip(block, axis, bit):
    n = lax.axis_size(axis)
    return lax.ppermute(block, axis, [(i, i ^ bit) for i in range(n)])


def shift(block, axis, distance):
    n = lax.axis_size(axis)
    return lax.ppermute(block, axis, [(i, (i + distance) % n) for i in range(n)])


def sibling(block):
    return flip(block, "head", 1)


def across(block):
    return flip(block, "head", 2)


def partner(block):
    return shift(block, "dp", lax.axis_size("dp") // 2)


def pick(array, index, axis=0):
    return lax.dynamic_index_in_dim(array, index, axis, keepdims=False)


def ordered(low, own, other, axis=0):
    return jnp.stack(
        (jnp.where(low == 0, own, other), jnp.where(low == 0, other, own)), axis=axis
    )


def mm(a, b):
    return jnp.dot(a, b, preferred_element_type=F32)


def mm_t(a, b):
    return lax.dot_general(a, b, (((1,), (1,)), ((), ())), preferred_element_type=F32)


def t_mm(a, b):
    return lax.dot_general(a, b, (((0,), (0,)), ((), ())), preferred_element_type=F32)


def norm_parts(rows):
    centered = rows - jnp.mean(rows, axis=-1, keepdims=True)
    inverse = lax.rsqrt(jnp.mean(centered * centered, axis=-1, keepdims=True) + EPSILON)
    return centered * inverse, inverse


def norm_back(incoming, normed, inverse, gain):
    scaled = incoming * gain
    return inverse * (
        scaled
        - jnp.mean(scaled, axis=-1, keepdims=True)
        - normed * jnp.mean(scaled * normed, axis=-1, keepdims=True)
    )


def gather(piece, x_first):
    n = lax.axis_size("dp")
    if n != 8:
        mine = lax.all_gather(piece, "dp", axis=0, tiled=False)
        return jnp.stack((mine, across(mine)))
    index = lax.axis_index("dp")
    z, x = index // 2, index % 2
    column = jnp.zeros((4,) + piece.shape, piece.dtype)
    column = lax.dynamic_update_index_in_dim(column, piece, z, 0)
    for k in (1, 2, 3):
        column = lax.dynamic_update_index_in_dim(
            column, shift(piece, "dp", 2 * k), (z - k) % 4, 0
        )
    if x_first:
        plane = ordered(x, column, flip(column, "dp", 1), axis=1)
        both = jnp.stack((plane, across(plane)))
    else:
        both = jnp.stack((column, across(column)))
        both = ordered(x, both, flip(both, "dp", 1), axis=2)
    return both.reshape((2, 8) + piece.shape)


def reduce_scatter(terms, x_last):
    n = lax.axis_size("dp")
    if n != 8:
        total = terms[0].astype(F32) + across(terms[1].astype(BF16)).astype(F32)
        return lax.psum_scatter(total, "dp", scatter_dimension=0, tiled=False)
    index = lax.axis_index("dp")
    z, x = index // 2, index % 2
    terms = terms.reshape((2, 4, 2) + terms.shape[2:])
    if x_last:
        arrived = across(terms[1])
        plane = (terms[0].astype(F32) + arrived.astype(F32)).astype(BF16)
        arrived = flip(pick(plane, 1 - x, 1), "dp", 1)
        column = pick(plane, x, 1).astype(F32) + arrived.astype(F32)
    else:
        arrived = flip(pick(terms, 1 - x, 2), "dp", 1)
        both = (pick(terms, x, 2).astype(F32) + arrived.astype(F32)).astype(BF16)
        column = both[0].astype(F32) + across(both[1]).astype(F32)
    column = column.astype(BF16)
    total = pick(column, z).astype(F32)
    for k in (1, 2, 3):
        total = total + shift(pick(column, (z + k) % 4), "dp", 2 * k).astype(F32)
    return total


def sum_all(vector):
    n = lax.axis_size("dp")
    if n != 8:
        return lax.psum(vector, ("dp", "head"))
    vector = vector + sibling(vector)
    vector = vector + across(vector)
    vector = vector + flip(vector, "dp", 1)
    return (vector + shift(vector, "dp", 4)) + (
        shift(vector, "dp", 2) + shift(vector, "dp", 6)
    )


def lane_masks(scale):
    lane = lax.broadcasted_iota(jnp.int32, (1, 2 * HD), 1)
    first = jnp.where(lane < HD, 1.0, 0.0)
    return [(first * scale).astype(BF16), ((1.0 - first) * scale).astype(BF16)]


def rows_of(ref):
    a, b, w = ref.shape
    return ref[...].reshape(a * b, w)


def pair_lanes(halves):
    lane = lax.broadcasted_iota(jnp.int32, halves[0].shape, 1)
    return jnp.where(lane < HD, halves[0], halves[1])


def attend_kernel(q_ref, k_ref, v_ref, o_ref):
    q, k, v = rows_of(q_ref), rows_of(k_ref), rows_of(v_ref)
    outs = []
    for mask in lane_masks(SCALE):
        s = mm_t(q * mask, k)
        raised = jnp.exp(s - jnp.max(s, axis=-1, keepdims=True))
        total = jnp.sum(raised, axis=-1, keepdims=True)
        outs.append(mm(raised.astype(BF16), v) / total)
    o_ref[...] = pair_lanes(outs).astype(BF16).reshape(o_ref.shape)


def query_back_kernel(q_ref, g_ref, k_ref, v_ref, dq_ref):
    q, g, k, v = rows_of(q_ref), rows_of(g_ref), rows_of(k_ref), rows_of(v_ref)
    outs = []
    for mask, one in zip(lane_masks(SCALE), lane_masks(1.0)):
        s = mm_t(q * mask, k)
        raised = jnp.exp(s - jnp.max(s, axis=-1, keepdims=True))
        probs = raised / jnp.sum(raised, axis=-1, keepdims=True)
        d_probs = mm_t(g * one, v)
        inner = jnp.sum(d_probs * probs, axis=-1, keepdims=True)
        d_scores = (probs * (d_probs - inner)).astype(BF16)
        outs.append(mm(d_scores, k) * SCALE)
    dq_ref[...] = pair_lanes(outs).astype(BF16).reshape(dq_ref.shape)


def key_back_kernel(q_ref, g_ref, k_ref, v_ref, dk_ref, dv_ref):
    q, g, k, v = rows_of(q_ref), rows_of(g_ref), rows_of(k_ref), rows_of(v_ref)
    d_keys, d_values = [], []
    for mask, one in zip(lane_masks(SCALE), lane_masks(1.0)):
        s = mm_t(k, q * mask)
        raised = jnp.exp(s - jnp.max(s, axis=0, keepdims=True))
        probs = raised / jnp.sum(raised, axis=0, keepdims=True)
        d_probs = mm_t(v, g * one)
        inner = jnp.sum(d_probs * probs, axis=0, keepdims=True)
        d_scores = (probs * (d_probs - inner)).astype(BF16)
        d_keys.append(mm(d_scores, q) * SCALE)
        d_values.append(mm(probs.astype(BF16), g))
    dk_ref[...] = pair_lanes(d_keys).astype(BF16).reshape(dk_ref.shape)
    dv_ref[...] = pair_lanes(d_values).astype(BF16).reshape(dv_ref.shape)


def per_head_pair(kernel, arrays, out_count, out_like, flops):
    _, blocks, _, width = arrays[0].shape

    def spec(array):
        return pl.BlockSpec(
            (2, None, array.shape[2], 2 * HD), lambda b, t: (0, b, 0, t)
        )

    shape = jax.ShapeDtypeStruct(out_like.shape, BF16)
    out = pl.pallas_call(
        kernel,
        grid=(blocks, width // (2 * HD)),
        in_specs=[spec(a) for a in arrays],
        out_specs=[spec(out_like)] * out_count,
        out_shape=[shape] * out_count,
        cost_estimate=pl.CostEstimate(
            flops=flops,
            transcendentals=0,
            bytes_accessed=2 * (sum(a.size for a in arrays) + out_count * out_like.size),
        ),
    )(*arrays)
    return out


def per_device(
    tokens,
    query_weight,
    query_bias,
    key_weight,
    value_weight,
    value_bias,
    out_weight,
    out_bias,
    first_gain,
    first_shift,
    up_weight,
    up_bias,
    down_weight,
    down_bias,
    second_gain,
    second_shift,
    block_order,
    masked_rows,
    out_grad,
):
    block_count, block_rows, width = tokens.shape
    quarter = block_rows // 4
    slots = masked_rows.shape[1]
    cap = slots // 4
    blocks = block_count // 2
    piece_rows = query_weight.shape[0]
    local = query_weight.shape[1]
    columns = 2 * local
    hidden_piece = up_weight.shape[1]
    head = lax.axis_index("head")
    c, p = head % 2, head // 2

    piece = jnp.concatenate((query_weight, key_weight, value_weight, out_weight.T), axis=1)
    half = piece_rows // 2
    w_one = gather(piece[:half], True)
    w_two = gather(piece[half:], False)
    w_attn = jnp.stack((w_one, w_two), axis=2).reshape(2, width, 4, local)
    w_attn = jnp.transpose(w_attn, (2, 1, 0, 3)).reshape(4, width, columns)
    w_query, w_key, w_value, w_out_t = (w_attn[i] for i in range(4))
    w_out_other = sibling(w_out_t)
    w_up = gather(up_weight, True).reshape(2, width, hidden_piece)
    w_down = gather(down_weight.T, False).reshape(2, width, hidden_piece)

    small = jnp.concatenate(
        (query_bias, value_bias, up_bias, block_order.astype(F32))
    )
    small_other = across(small)

    def both(start, size):
        return jnp.concatenate(
            (small[start : start + size], small_other[start : start + size])
        )

    b_query = both(0, local)
    b_value = both(local, local)
    b_up = jnp.stack((up_bias, small_other[2 * local : 2 * local + hidden_piece]))
    swapped = jnp.repeat(both(2 * local + hidden_piece, local // HD) > 0.5, HD)

    mine = pick(tokens.reshape(2, blocks, 2, 2, quarter, width), p)
    x_rows = jnp.stack((pick(mine, c, 2), pick(mine, 1 - c, 2)))
    x_flat = x_rows.reshape(-1, width)
    x_other = partner(x_rows).reshape(-1, width)
    own_count = x_flat.shape[0] // 2
    attn_shape = (2, blocks, 2 * quarter, columns)
    compact_shape = (2, blocks, 2 * cap, columns)

    listed = pick(masked_rows.reshape(2, blocks, slots), p)
    run = jnp.where(listed >= 0, listed // quarter, -1)
    earlier = jnp.arange(slots)[:, None] > jnp.arange(slots)[None, :]
    rank = jnp.sum((run[:, :, None] == run[:, None, :]) & earlier, axis=-1)
    which = jnp.stack((c, c + 2, 1 - c, 3 - c)).reshape(2, 1, 2, 1, 1)
    picks = (
        (run[None, :, None, None, :] == which)
        & (rank[None, :, None, None, :] == jnp.arange(cap)[:, None])
    ).astype(BF16)
    places = (listed[:, :, None] % quarter == jnp.arange(quarter)).astype(BF16)
    select = jnp.einsum(
        "sbeki,bir->sbekr", picks, places, preferred_element_type=F32
    ).astype(BF16)
    select = select.reshape(-1, cap, quarter)
    runs_own = 2 * blocks

    def compact(rows, which=slice(None), **kw):
        source = select[which]
        out = jnp.einsum(
            "ukr,urw->ukw",
            source.astype(rows.dtype),
            rows.reshape(source.shape[0], quarter, -1),
            preferred_element_type=F32,
            **kw,
        )
        return out.reshape(-1, rows.shape[-1])

    def spread(rows, which=slice(None), **kw):
        source = select[which]
        out = jnp.einsum(
            "ukr,ukw->urw",
            source.astype(rows.dtype),
            rows.reshape(source.shape[0], cap, -1),
            preferred_element_type=F32,
            **kw,
        )
        return out.reshape(-1, rows.shape[-1])

    own_runs, other_runs = slice(0, runs_own), slice(runs_own, None)
    exact = {"precision": lax.Precision.HIGHEST}
    grads_in = pick(out_grad.reshape(2, blocks, slots, width), p)
    grad_y = jnp.einsum(
        "beki,biw->bekw", picks[0], grads_in, preferred_element_type=F32
    ).reshape(-1, width)

    queries = (mm(x_flat, w_query) + b_query).astype(BF16)
    keys = mm(x_flat, w_key).astype(BF16)
    values = (mm(x_flat, w_value) + b_value).astype(BF16)
    keys_used = jnp.where(swapped, mm(x_other, w_key).astype(BF16), keys)
    values_used = jnp.where(
        swapped, (mm(x_other, w_value) + b_value).astype(BF16), values
    )
    unit_flops = 4 * block_rows * block_rows * columns * blocks
    (attention,) = per_head_pair(
        attend_kernel,
        [a.reshape(attn_shape) for a in (queries, keys_used, values_used)],
        1,
        queries.reshape(attn_shape),
        unit_flops,
    )
    q_compact = compact(queries).astype(BF16).reshape(compact_shape)
    q_far = partner(q_compact)
    swapped_lanes = swapped[None, None, None, :]
    attn_other = sibling(attention[1]).reshape(own_count, columns)
    branch = mm_t(attention[0].reshape(own_count, columns), w_out_t) + mm_t(
        attn_other, w_out_other
    )
    sum_one = x_flat[:own_count].astype(F32) + branch + out_bias
    hidden = norm_parts(sum_one)[0] * first_gain + first_shift
    hidden_low = hidden.astype(BF16)
    hidden_other = sibling(hidden_low)
    hidden_all = jnp.concatenate((hidden_low, hidden_other))

    def feed(i):
        pre = mm(hidden_all, w_up[i]) + b_up[i]
        activated = jax.nn.gelu(pre, approximate=False).astype(BF16)
        return mm_t(activated, w_down[i])

    feed_term = feed(0) + feed(1)
    feed_out = (
        feed_term[:own_count]
        + sibling(feed_term[own_count:].astype(BF16)).astype(F32)
        + down_bias
    )
    sum_two = hidden + feed_out
    out_rows = (norm_parts(sum_two)[0] * second_gain + second_shift).astype(BF16)

    def to_output(rows):
        rows = rows.reshape(blocks, 2, quarter, width)
        kept = pick(rows, p, 1)
        moved = across(pick(rows, 1 - p, 1))
        return ordered(p, kept, moved).reshape(block_count, quarter, width)

    out_y = to_output(out_rows)

    one_c = compact(sum_one, own_runs, **exact)
    two_c = compact(sum_two, own_runs, **exact)
    normed_two, inverse_two = norm_parts(two_c)
    normed_one, inverse_one = norm_parts(one_c)
    hidden_c = (normed_one * first_gain + first_shift).astype(BF16)
    d_second = norm_back(grad_y, normed_two, inverse_two, second_gain)
    g_second_gain = jnp.sum(grad_y * normed_two, axis=0)
    g_second_shift = jnp.sum(grad_y, axis=0)
    d_feed = d_second.astype(BF16)
    g_down_bias = jnp.sum(d_feed.astype(F32), axis=0)
    d_feed_all = jnp.concatenate((d_feed, sibling(d_feed)))
    hidden_c_all = jnp.concatenate(
        (hidden_c, compact(hidden_other, other_runs).astype(BF16))
    )
    g_up, g_down, g_up_bias, d_hidden_term = [], [], [], 0.0
    for i in range(2):
        pre = mm(hidden_c_all, w_up[i]) + b_up[i]
        cdf = 0.5 * (1.0 + lax.erf(pre * (0.5**0.5)))
        density = jnp.exp(-0.5 * pre * pre) * (0.5 / jnp.pi) ** 0.5
        activated = (pre * cdf).astype(BF16)
        d_pre = (mm(d_feed_all, w_down[i]) * (cdf + pre * density)).astype(BF16)
        g_up_bias.append(jnp.sum(d_pre.astype(F32), axis=0))
        g_up.append(t_mm(hidden_c_all, d_pre).astype(BF16))
        g_down.append(t_mm(d_feed_all, activated).astype(BF16))
        d_hidden_term = d_hidden_term + mm_t(d_pre, w_up[i])
    compact_own = d_feed.shape[0]
    d_hidden = (
        d_second
        + d_hidden_term[:compact_own]
        + sibling(d_hidden_term[compact_own:].astype(BF16)).astype(F32)
    )
    pieces = (2, width // piece_rows, piece_rows, hidden_piece)
    s_up = reduce_scatter(jnp.stack(g_up).reshape(pieces), True)
    s_down = reduce_scatter(jnp.stack(g_down).reshape(pieces), False).T
    g_first_gain = jnp.sum(d_hidden * normed_one, axis=0)
    g_first_shift = jnp.sum(d_hidden, axis=0)
    d_first = norm_back(d_hidden, normed_one, inverse_one, first_gain)
    d_branch = d_first.astype(BF16)
    g_out_bias = jnp.sum(d_branch.astype(F32), axis=0)
    d_branch_all = jnp.concatenate((d_branch, sibling(d_branch)))
    d_attention = mm(d_branch_all, w_out_t).astype(BF16).reshape(compact_shape)
    d_attention_far = partner(d_attention)

    (d_queries_c,) = per_head_pair(
        query_back_kernel,
        [
            q_compact,
            d_attention,
            keys_used.reshape(attn_shape),
            values_used.reshape(attn_shape),
        ],
        1,
        q_compact,
        6 * slots * block_rows * columns * blocks,
    )
    d_keys, d_values = per_head_pair(
        key_back_kernel,
        [
            jnp.where(swapped_lanes, q_far, q_compact),
            jnp.where(swapped_lanes, d_attention_far, d_attention),
            keys.reshape(attn_shape),
            values.reshape(attn_shape),
        ],
        2,
        keys.reshape(attn_shape),
        8 * slots * block_rows * columns * blocks,
    )
    d_queries_c = d_queries_c.reshape(-1, columns)
    d_queries = spread(d_queries_c).astype(BF16)
    d_keys = d_keys.reshape(-1, columns)
    d_values = d_values.reshape(-1, columns)
    term = mm_t(d_queries, w_query) + mm_t(d_keys, w_key) + mm_t(d_values, w_value)
    grad_rows = (
        term[:own_count]
        + sibling(term[own_count:].astype(BF16)).astype(F32)
        + spread(d_first, own_runs, **exact)
    ).astype(BF16)
    grad_x = to_output(grad_rows)

    g_query_bias = jnp.sum(d_queries_c.astype(F32), axis=0)
    g_value_bias = jnp.sum(d_values.astype(F32), axis=0)
    g_attn = jnp.stack(
        (
            t_mm(x_flat, d_queries).astype(BF16),
            t_mm(x_flat, d_keys).astype(BF16),
            t_mm(x_flat, d_values).astype(BF16),
            t_mm(d_branch_all, compact(attention.reshape(-1, columns)).astype(BF16)).astype(BF16),
        ),
        axis=1,
    )
    g_attn = jnp.transpose(g_attn.reshape(width, 4, 2, local), (2, 0, 1, 3)).reshape(
        2, width // piece_rows, 2, half, 4 * local
    )
    s_attn = jnp.concatenate(
        (
            reduce_scatter(g_attn[:, :, 0], True),
            reduce_scatter(g_attn[:, :, 1], False),
        )
    )

    def widen(own_first, size):
        own_first = own_first.reshape(2, -1)
        by_p = ordered(p, own_first[0], own_first[1])
        zero = jnp.zeros_like(by_p)
        return jnp.where(
            c == 0,
            jnp.stack((by_p, zero), axis=1),
            jnp.stack((zero, by_p), axis=1),
        ).reshape(size)

    vectors = [
        widen(g_query_bias, HEADS * HD),
        widen(g_value_bias, HEADS * HD),
        g_out_bias,
        g_first_gain,
        g_first_shift,
        widen(jnp.stack(g_up_bias), 4 * hidden_piece),
        g_down_bias,
        g_second_gain,
        g_second_shift,
    ]
    summed = sum_all(jnp.concatenate(vectors))
    ends, start = [], 0
    for vector in vectors:
        ends.append(summed[start : start + vector.shape[0]])
        start += vector.shape[0]
    (
        v_query_bias,
        v_value_bias,
        v_out_bias,
        v_first_gain,
        v_first_shift,
        v_up_bias,
        v_down_bias,
        v_second_gain,
        v_second_shift,
    ) = ends
    return (
        out_y,
        grad_x,
        s_attn[:, :local],
        v_query_bias,
        s_attn[:, local : 2 * local],
        s_attn[:, 2 * local : 3 * local],
        v_value_bias,
        s_attn[:, 3 * local :].T,
        v_out_bias,
        v_first_gain,
        v_first_shift,
        s_up,
        v_up_bias,
        s_down,
        v_down_bias,
        v_second_gain,
        v_second_shift,
    )


def solution(mesh):
    in_specs = (
        P("dp", None, None),
        P("dp", "head"),
        P("head"),
        P("dp", "head"),
        P("dp", "head"),
        P("head"),
        P("head", "dp"),
        P(),
        P(),
        P(),
        P("dp", "head"),
        P("head"),
        P("head", "dp"),
        P(),
        P(),
        P(),
        P("head"),
        P("dp", None),
        P("dp", None, None),
    )
    out_specs = (
        P("dp", "head", None),
        P("dp", "head", None),
        P("dp", "head"),
        P(),
        P("dp", "head"),
        P("dp", "head"),
        P(),
        P("head", "dp"),
        P(),
        P(),
        P(),
        P("dp", "head"),
        P(),
        P("head", "dp"),
        P(),
        P(),
        P(),
    )
    return jax.shard_map(
        per_device, mesh=mesh, in_specs=in_specs, out_specs=out_specs, check_vma=False
    )
```

```python
import functools

import jax
import jax.numpy as jnp
from jax import lax
from jax.experimental import pallas as pl
from jax.experimental.pallas import tpu as pltpu
from jax.sharding import PartitionSpec as P

HEADS = 12
HD = 64
FF = 3072
EPSILON = 1e-12
F32 = jnp.float32
BF16 = jnp.bfloat16
SCALE = HD ** (-0.5)
MESH = pl.DeviceIdType.MESH


def flip(block, axis, bit):
    n = lax.axis_size(axis)
    return lax.ppermute(block, axis, [(i, i ^ bit) for i in range(n)])


def shift(block, axis, distance):
    n = lax.axis_size(axis)
    return lax.ppermute(block, axis, [(i, (i + distance) % n) for i in range(n)])


def sibling(block):
    return flip(block, "head", 1)


def across(block):
    return flip(block, "head", 2)


def partner(block):
    return shift(block, "dp", lax.axis_size("dp") // 2)


def pick(array, index, axis=0):
    return lax.dynamic_index_in_dim(array, index, axis, keepdims=False)


def ordered(low, own, other, axis=0):
    return jnp.stack(
        (jnp.where(low == 0, own, other), jnp.where(low == 0, other, own)), axis=axis
    )


def mm(a, b):
    return jnp.dot(a, b, preferred_element_type=F32)


def mm_t(a, b):
    return lax.dot_general(a, b, (((1,), (1,)), ((), ())), preferred_element_type=F32)


def t_mm(a, b):
    return lax.dot_general(a, b, (((0,), (0,)), ((), ())), preferred_element_type=F32)


def norm_parts(rows):
    centered = rows - jnp.mean(rows, axis=-1, keepdims=True)
    inverse = lax.rsqrt(jnp.mean(centered * centered, axis=-1, keepdims=True) + EPSILON)
    return centered * inverse, inverse


def norm_back(incoming, normed, inverse, gain):
    scaled = incoming * gain
    return inverse * (
        scaled
        - jnp.mean(scaled, axis=-1, keepdims=True)
        - normed * jnp.mean(scaled * normed, axis=-1, keepdims=True)
    )


def gather(piece, x_first):
    n = lax.axis_size("dp")
    if n != 8:
        mine = lax.all_gather(piece, "dp", axis=0, tiled=False)
        return jnp.stack((mine, across(mine)))
    index = lax.axis_index("dp")
    z, x = index // 2, index % 2
    column = jnp.zeros((4,) + piece.shape, piece.dtype)
    column = lax.dynamic_update_index_in_dim(column, piece, z, 0)
    for k in (1, 2, 3):
        column = lax.dynamic_update_index_in_dim(
            column, shift(piece, "dp", 2 * k), (z - k) % 4, 0
        )
    if x_first:
        plane = ordered(x, column, flip(column, "dp", 1), axis=1)
        both = jnp.stack((plane, across(plane)))
    else:
        both = jnp.stack((column, across(column)))
        both = ordered(x, both, flip(both, "dp", 1), axis=2)
    return both.reshape((2, 8) + piece.shape)


def reduce_scatter(terms, x_last):
    n = lax.axis_size("dp")
    if n != 8:
        total = terms[0].astype(F32) + across(terms[1].astype(BF16)).astype(F32)
        return lax.psum_scatter(total, "dp", scatter_dimension=0, tiled=False)
    index = lax.axis_index("dp")
    z, x = index // 2, index % 2
    terms = terms.reshape((2, 4, 2) + terms.shape[2:])
    if x_last:
        arrived = across(terms[1])
        plane = (terms[0].astype(F32) + arrived.astype(F32)).astype(BF16)
        arrived = flip(pick(plane, 1 - x, 1), "dp", 1)
        column = pick(plane, x, 1).astype(F32) + arrived.astype(F32)
    else:
        arrived = flip(pick(terms, 1 - x, 2), "dp", 1)
        both = (pick(terms, x, 2).astype(F32) + arrived.astype(F32)).astype(BF16)
        column = both[0].astype(F32) + across(both[1]).astype(F32)
    column = column.astype(BF16)
    total = pick(column, z).astype(F32)
    for k in (1, 2, 3):
        total = total + shift(pick(column, (z + k) % 4), "dp", 2 * k).astype(F32)
    return total


def sum_all(vector):
    n = lax.axis_size("dp")
    if n != 8:
        return lax.psum(vector, ("dp", "head"))
    vector = vector + sibling(vector)
    vector = vector + across(vector)
    vector = vector + flip(vector, "dp", 1)
    return (vector + shift(vector, "dp", 4)) + (
        shift(vector, "dp", 2) + shift(vector, "dp", 6)
    )


def lane_masks(scale):
    lane = lax.broadcasted_iota(jnp.int32, (1, 2 * HD), 1)
    first = jnp.where(lane < HD, 1.0, 0.0)
    return [(first * scale).astype(BF16), ((1.0 - first) * scale).astype(BF16)]


def rows_of(ref):
    a, b, w = ref.shape
    return ref[...].reshape(a * b, w)


def pair_lanes(halves):
    lane = lax.broadcasted_iota(jnp.int32, halves[0].shape, 1)
    return jnp.where(lane < HD, halves[0], halves[1])


def attend_kernel(q_ref, k_ref, v_ref, o_ref):
    q, k, v = rows_of(q_ref), rows_of(k_ref), rows_of(v_ref)
    outs = []
    for mask in lane_masks(SCALE):
        s = mm_t(q * mask, k)
        raised = jnp.exp(s - jnp.max(s, axis=-1, keepdims=True))
        total = jnp.sum(raised, axis=-1, keepdims=True)
        outs.append(mm(raised.astype(BF16), v) / total)
    o_ref[...] = pair_lanes(outs).astype(BF16).reshape(o_ref.shape)


def query_back_kernel(q_ref, g_ref, k_ref, v_ref, dq_ref):
    q, g, k, v = rows_of(q_ref), rows_of(g_ref), rows_of(k_ref), rows_of(v_ref)
    outs = []
    for mask, one in zip(lane_masks(SCALE), lane_masks(1.0)):
        s = mm_t(q * mask, k)
        raised = jnp.exp(s - jnp.max(s, axis=-1, keepdims=True))
        probs = raised / jnp.sum(raised, axis=-1, keepdims=True)
        d_probs = mm_t(g * one, v)
        inner = jnp.sum(d_probs * probs, axis=-1, keepdims=True)
        d_scores = (probs * (d_probs - inner)).astype(BF16)
        outs.append(mm(d_scores, k) * SCALE)
    dq_ref[...] = pair_lanes(outs).astype(BF16).reshape(dq_ref.shape)


def key_back_kernel(q_ref, g_ref, k_ref, v_ref, dk_ref, dv_ref):
    q, g, k, v = rows_of(q_ref), rows_of(g_ref), rows_of(k_ref), rows_of(v_ref)
    d_keys, d_values = [], []
    for mask, one in zip(lane_masks(SCALE), lane_masks(1.0)):
        s = mm_t(k, q * mask)
        raised = jnp.exp(s - jnp.max(s, axis=0, keepdims=True))
        probs = raised / jnp.sum(raised, axis=0, keepdims=True)
        d_probs = mm_t(v, g * one)
        inner = jnp.sum(d_probs * probs, axis=0, keepdims=True)
        d_scores = (probs * (d_probs - inner)).astype(BF16)
        d_keys.append(mm(d_scores, q) * SCALE)
        d_values.append(mm(probs.astype(BF16), g))
    dk_ref[...] = pair_lanes(d_keys).astype(BF16).reshape(dk_ref.shape)
    dv_ref[...] = pair_lanes(d_values).astype(BF16).reshape(dv_ref.shape)


def halves_joined(low, high):
    lane = lax.broadcasted_iota(jnp.int32, low.shape, 1)
    return jnp.where(lane < HD, low, pltpu.roll(high, HD, 1))


def highs_joined(low, high):
    lane = lax.broadcasted_iota(jnp.int32, low.shape, 1)
    return jnp.where(lane < HD, pltpu.roll(low, HD, 1), high)


def head_tiles(row_own, row_other):
    return (
        row_own[:, :128],
        row_other[:, :128],
        halves_joined(row_own[:, 128:256], row_other[:, 128:256]),
    )


def project(x, wa_ref, count):
    width = x.shape[1]
    tiles = []
    for p in range(2):
        w = wa_ref[p].reshape(width, wa_ref.shape[-1])
        out = mm(x, w[:, count[0] : count[1]])
        tiles.append([out[:, 128 * i : 128 * (i + 1)] for i in range(out.shape[1] // 128)])
    return tiles


def forward_own(b, x_ref, wa_ref, bias, q_ref, k_ref, v_ref):
    rows = x_ref.shape[2] * x_ref.shape[3] * 2
    x = x_ref[:, b].reshape(rows, x_ref.shape[-1])
    one, two = project(x, wa_ref, (0, 640))
    b_query, b_value = bias
    parts = (
        (q_ref, (one[0], two[0], halves_joined(one[3], two[3])), b_query),
        (k_ref, (one[1], two[1], highs_joined(one[3], two[3])), None),
        (v_ref, (one[2], two[2], halves_joined(one[4], two[4])), b_value),
    )
    for ref, tiles, added in parts:
        for t in range(3):
            tile = tiles[t] if added is None else tiles[t] + added[t]
            ref[:, b, :, 128 * t : 128 * (t + 1)] = tile.astype(BF16).reshape(2, rows // 2, 128)


def forward_attend(b, xp_ref, wa_ref, bias, swapped, q_ref, k_ref, v_ref, ku_ref, vu_ref, o_ref):
    rows = xp_ref.shape[2] * xp_ref.shape[3] * 2
    x = xp_ref[:, b].reshape(rows, xp_ref.shape[-1])
    one, two = project(x, wa_ref, (128, 640))
    far_keys = (one[0], two[0], highs_joined(one[2], two[2]))
    far_values = (one[1], two[1], halves_joined(one[3], two[3]))
    masks = lane_masks(SCALE)
    for t in range(3):
        lanes = slice(128 * t, 128 * (t + 1))

        def load(ref):
            return ref[:, b, :, lanes].reshape(rows, 128)

        take_far = swapped[t] > 0.5
        k = jnp.where(take_far, far_keys[t], load(k_ref).astype(F32)).astype(BF16)
        v = jnp.where(
            take_far, far_values[t] + bias[1][t], load(v_ref).astype(F32)
        ).astype(BF16)
        ku_ref[:, b, :, lanes] = k.reshape(2, rows // 2, 128)
        vu_ref[:, b, :, lanes] = v.reshape(2, rows // 2, 128)
        q = load(q_ref)
        outs = []
        for mask in masks:
            s = mm_t(q * mask, k)
            raised = jnp.exp(s - jnp.max(s, axis=-1, keepdims=True))
            total = jnp.sum(raised, axis=-1, keepdims=True)
            outs.append(mm(raised.astype(BF16), v) / total)
        o_ref[:, b, :, lanes] = pair_lanes(outs).astype(BF16).reshape(2, rows // 2, 128)


def forward_listed(b, member, row_ref, col_ref, q_ref, picks_ref, select_ref, qc_ref):
    slots = row_ref.shape[-1]
    quarter = q_ref.shape[2] // 2
    cap = slots // 4
    row, col = row_ref[b], col_ref[b]
    bits = quarter.bit_length() - 1
    run_row = lax.shift_right_arithmetic(row, bits)
    run_col = lax.shift_right_arithmetic(col, bits)
    before = lax.broadcasted_iota(jnp.int32, (slots, slots), 0) < lax.broadcasted_iota(
        jnp.int32, (slots, slots), 1
    )
    same = jnp.where(run_col == run_row, jnp.where(before, 1.0, 0.0), 0.0)
    rank = jnp.sum(same, axis=0, keepdims=True)
    line = lax.broadcasted_iota(jnp.int32, (slots, 1), 0)
    place = line // cap
    wanted_run = jnp.where(
        place == 0, member, jnp.where(place == 1, member + 2, jnp.where(place == 2, 1 - member, 3 - member))
    )
    wanted_rank = (line % cap).astype(F32)
    picks = jnp.where(run_row == wanted_run, jnp.where(rank == wanted_rank, 1.0, 0.0), 0.0).astype(BF16)
    lane = lax.broadcasted_iota(jnp.int32, (slots, quarter), 1)
    places = jnp.where(jnp.bitwise_and(col, quarter - 1) == lane, 1.0, 0.0).astype(BF16)
    select = mm(picks, places).astype(BF16)
    picks_ref[b] = picks
    select_ref[b] = select
    for s in range(2):
        for e in range(2):
            at = (2 * s + e) * cap
            rows = q_ref[s, b, quarter * e : quarter * (e + 1), :]
            qc_ref[s, b, cap * e : cap * (e + 1), :] = mm(select[at : at + cap], rows).astype(BF16)


def forward_kernel(comm, *refs):
    if comm:
        (
            a_ref, b_ref, t_ref, small_ref, row_ref, col_ref,
            wa_ref, wb_ref, x_ref, o_ref, k_ref, v_ref, ku_ref, vu_ref, qc_ref, picks_ref, select_ref, far_ref,
            xp_ref, q_ref, local_sem, send_sem, recv_sem,
        ) = refs
    else:
        (
            wa_ref, x_ref, xp_ref, small_ref, far_ref, row_ref, col_ref,
            o_ref, k_ref, v_ref, ku_ref, vu_ref, qc_ref, picks_ref, select_ref,
            q_ref,
        ) = refs
    blocks = x_ref.shape[1]
    head = lax.axis_index("head")
    member, pair = lax.rem(head, 2), lax.div(head, 2)

    def listed(b, carry):
        forward_listed(b, member, row_ref, col_ref, q_ref, picks_ref, select_ref, qc_ref)
        return carry

    def bias_of():
        own, other = small_ref[...], far_ref[...]
        rows = [head_tiles(own[i : i + 1], other[i : i + 1]) for i in range(3)]
        return (rows[0], rows[1]), rows[2]

    if not comm:
        bias, swapped = bias_of()

        def own_block(b, carry):
            forward_own(b, x_ref, wa_ref, bias, q_ref, k_ref, v_ref)
            return carry
    if comm:
        index = lax.axis_index("dp")
        z, x = lax.div(index, 2), lax.rem(index, 2)
        x_peer = {"dp": 2 * z + 1 - x}
        y_peer = {"head": lax.rem(head + 2, 4)}
        sibling_peer = {"head": 2 * pair + 1 - member}
        z_peers = [{"dp": lax.rem(index + 2 * k, 8)} for k in (1, 2, 3)]
        barrier = pltpu.get_barrier_semaphore()
        for peer in [x_peer, y_peer, sibling_peer] + z_peers:
            pl.semaphore_signal(barrier, inc=1, device_id=peer, device_id_type=MESH)
        counter = [0]

        def local(src, dst, i):
            copy = pltpu.make_async_copy(src, dst, local_sem.at[i])
            copy.start()
            return copy

        def send(src, dst, peer):
            i = counter[0]
            counter[0] += 1
            copy = pltpu.make_async_remote_copy(
                src_ref=src,
                dst_ref=dst,
                send_sem=send_sem.at[i],
                recv_sem=recv_sem.at[i],
                device_id=peer,
                device_id_type=MESH,
            )
            copy.start()
            sent.append(copy)
            return copy

        def far_copy(b):
            return pltpu.make_async_remote_copy(
                src_ref=x_ref.at[0, b],
                dst_ref=xp_ref.at[0, b],
                send_sem=send_sem.at[15 + b],
                recv_sem=recv_sem.at[15 + b],
                device_id=z_peers[1],
                device_id_type=MESH,
            )

        def near_copy(b):
            return pltpu.make_async_remote_copy(
                src_ref=xp_ref.at[0, b],
                dst_ref=xp_ref.at[1, b],
                send_sem=send_sem.at[15 + blocks + b],
                recv_sem=recv_sem.at[15 + blocks + b],
                device_id=sibling_peer,
                device_id_type=MESH,
            )

        sent = []
        quarters = (member, member + 2, 1 - member, 3 - member)
        fills = [
            local(t_ref.at[pl.ds(blocks * pair, blocks), quarters[2 * s + e]], x_ref.at[s, :, e], 2 * s + e)
            for s in range(2)
            for e in range(2)
        ]
        fill_a = local(a_ref, wa_ref.at[0, z, x], 4)
        fill_b = local(b_ref, wb_ref.at[0, :, z, x], 5)
        pl.semaphore_wait(barrier, 6)
        a_z = [send(a_ref, wa_ref.at[0, z, x], peer) for peer in z_peers]
        far = send(small_ref, far_ref, y_peer)
        b_z = [send(b_ref, wb_ref.at[0, :, z, x], peer) for peer in z_peers]
        for fill in fills:
            fill.wait()
        for b in range(blocks):
            far_copy(b).start()
        half = a_ref.shape[0] // 2
        up, low = pl.ds(0, half), pl.ds(half, half)
        fill_a.wait()
        for copy in a_z:
            copy.wait_recv()
        a_x = send(wa_ref.at[0, :, x, up], wa_ref.at[0, :, x, up], x_peer)
        a_y = send(wa_ref.at[0, :, x, low], wa_ref.at[1, :, x, low], y_peer)
        a_x.wait_recv()
        a_xy = send(wa_ref.at[0, :, :, up], wa_ref.at[1, :, :, up], y_peer)
        a_y.wait_recv()
        a_yx = send(wa_ref.at[:, :, x, low], wa_ref.at[:, :, x, low], x_peer)
        fill_b.wait()
        for copy in b_z:
            copy.wait_recv()
        b_x = send(wb_ref.at[0, 0, :, x], wb_ref.at[0, 0, :, x], x_peer)
        b_y = send(wb_ref.at[0, 1, :, x], wb_ref.at[1, 1, :, x], y_peer)
        far.wait_recv()
        a_xy.wait_recv()
        a_yx.wait_recv()
        bias, swapped = bias_of()

        def own_block(b, carry):
            forward_own(b, x_ref, wa_ref, bias, q_ref, k_ref, v_ref)
            return carry

    lax.fori_loop(0, blocks, own_block, 0)
    lax.fori_loop(0, blocks, listed, 0)
    if comm:
        b_x.wait_recv()
        b_xy = send(wb_ref.at[0, 0], wb_ref.at[1, 0], y_peer)
        b_y.wait_recv()
        b_yx = send(wb_ref.at[:, 1, :, x], wb_ref.at[:, 1, :, x], x_peer)
        def attend_block(b, carry):
            far_copy(b).wait_recv()
            near = near_copy(b)
            near.start()
            near.wait_recv()
            forward_attend(b, xp_ref, wa_ref, bias, swapped, q_ref, k_ref, v_ref, ku_ref, vu_ref, o_ref)
            return carry

        lax.fori_loop(0, blocks, attend_block, 0)
        b_xy.wait_recv()
        b_yx.wait_recv()
        for copy in sent:
            copy.wait_send()
        for b in range(blocks):
            far_copy(b).wait_send()
            near_copy(b).wait_send()
    else:

        def attend_block(b, carry):
            forward_attend(b, xp_ref, wa_ref, bias, swapped, q_ref, k_ref, v_ref, ku_ref, vu_ref, o_ref)
            return carry

        lax.fori_loop(0, blocks, attend_block, 0)


def vmem_spec():
    return pl.BlockSpec(memory_space=pltpu.VMEM)


def any_spec():
    return pl.BlockSpec(memory_space=pl.ANY)


def forward(tokens, piece_a, piece_b, small, listed, member, pair):
    n = lax.axis_size("dp")
    block_count, block_rows, width = tokens.shape
    blocks, quarter = block_count // 2, block_rows // 4
    slots = listed.shape[1]
    cap = slots // 4
    lanes = 6 * HD
    tokens = tokens.reshape(block_count, 4, quarter, width)
    row, col = listed[:, None, :], listed[:, :, None]
    rows_shape = (2, blocks, 2, quarter, width)

    def out(*shape, dtype=BF16):
        return jax.ShapeDtypeStruct(shape, dtype)

    dense = (2, blocks, 2 * quarter, lanes)
    tail = [out(*dense)] * 5 + [
        out(2, blocks, 2 * cap, lanes),
        out(blocks, slots, slots),
        out(blocks, slots, quarter),
    ]
    params = dict(vmem_limit_bytes=60 * 2**20, has_side_effects=True)
    if n == 8:
        shapes = [
            out(2, 4, 2, *piece_a.shape),
            out(2, 2, 4, 2, *piece_b.shape[1:]),
            out(*rows_shape),
            *tail,
            out(*small.shape, dtype=F32),
        ]
        specs = [vmem_spec()] * len(shapes)
        specs[1] = any_spec()
        results = pl.pallas_call(
            functools.partial(forward_kernel, True),
            out_shape=shapes,
            in_specs=[vmem_spec(), vmem_spec(), any_spec()] + [vmem_spec()] * 3,
            out_specs=specs,
            scratch_shapes=[
                pltpu.VMEM(rows_shape, BF16),
                pltpu.VMEM(dense, BF16),
                pltpu.SemaphoreType.DMA((6,)),
                pltpu.SemaphoreType.DMA((15 + 2 * blocks,)),
                pltpu.SemaphoreType.DMA((15 + 2 * blocks,)),
            ],
            compiler_params=pltpu.CompilerParams(collective_id=1, **params),
        )(piece_a, piece_b, tokens, small, row, col)
        w_attn, w_feed, rows, *rest, far = results
    else:
        mine = pick(tokens.reshape(2, blocks, 2, 2, quarter, width), pair)
        rows = jnp.stack((pick(mine, member, 2), pick(mine, 1 - member, 2)))
        w_attn = gather(piece_a, True)
        w_feed = jnp.stack([gather(piece_b[i], True) for i in range(2)], axis=1)
        far = across(small)
        shapes = tail
        rest = pl.pallas_call(
            functools.partial(forward_kernel, False),
            out_shape=shapes,
            in_specs=[vmem_spec()] * 7,
            out_specs=[vmem_spec()] * len(shapes),
            scratch_shapes=[pltpu.VMEM(dense, BF16)],
            compiler_params=pltpu.CompilerParams(vmem_limit_bytes=60 * 2**20),
        )(w_attn.reshape(2, width, -1), rows, partner(rows), small, far, row, col)
    w_attn = w_attn.reshape(2, width, -1)
    w_feed = w_feed.reshape(2, 2, width, -1)
    return (w_attn, w_feed, rows, *rest, far)


def per_head_pair(kernel, arrays, out_count, out_like, flops):
    _, blocks, _, width = arrays[0].shape

    def spec(array):
        return pl.BlockSpec(
            (2, None, array.shape[2], 2 * HD), lambda b, t: (0, b, 0, t)
        )

    shape = jax.ShapeDtypeStruct(out_like.shape, BF16)
    out = pl.pallas_call(
        kernel,
        grid=(blocks, width // (2 * HD)),
        in_specs=[spec(a) for a in arrays],
        out_specs=[spec(out_like)] * out_count,
        out_shape=[shape] * out_count,
        cost_estimate=pl.CostEstimate(
            flops=flops,
            transcendentals=0,
            bytes_accessed=2 * (sum(a.size for a in arrays) + out_count * out_like.size),
        ),
    )(*arrays)
    return out


def per_device(
    tokens,
    query_weight,
    query_bias,
    key_weight,
    value_weight,
    value_bias,
    out_weight,
    out_bias,
    first_gain,
    first_shift,
    up_weight,
    up_bias,
    down_weight,
    down_bias,
    second_gain,
    second_shift,
    block_order,
    masked_rows,
    out_grad,
):
    block_count, block_rows, width = tokens.shape
    quarter = block_rows // 4
    slots = masked_rows.shape[1]
    cap = slots // 4
    blocks = block_count // 2
    piece_rows = query_weight.shape[0]
    local = query_weight.shape[1]
    columns = 2 * local
    hidden_piece = up_weight.shape[1]
    head = lax.axis_index("head")
    c, p = head % 2, head // 2

    out_t = out_weight.T
    first, last = slice(0, 2 * HD), slice(2 * HD, 3 * HD)
    piece = jnp.concatenate(
        (
            query_weight[:, first],
            key_weight[:, first],
            value_weight[:, first],
            query_weight[:, last],
            key_weight[:, last],
            value_weight[:, last],
            out_t[:, last],
            out_t[:, first],
        ),
        axis=1,
    )
    half = piece_rows // 2

    def line(vector, size):
        return jnp.pad(vector, (0, size - vector.shape[0]))

    small = jnp.stack(
        [
            line(row, hidden_piece)
            for row in (
                query_bias,
                value_bias,
                jnp.repeat(block_order.astype(F32), HD),
                up_bias,
            )
        ]
        + [jnp.zeros((hidden_piece,), F32)] * 4
    )
    listed = pick(masked_rows.reshape(2, blocks, slots), p)
    (
        w_attn, w_feed, x_rows, attention, keys, values, keys_used, values_used, q_compact, picks_b, select_b, small_far,
    ) = forward(tokens, piece, jnp.stack((up_weight, down_weight.T)), small, listed, c, p)

    def tiles(i, second, j):
        return jnp.concatenate(
            (
                w_attn[0][:, 128 * i : 128 * i + 128],
                w_attn[1][:, 128 * i : 128 * i + 128],
                w_attn[0][:, 128 * j + 64 * second : 128 * j + 64 * second + 64],
                w_attn[1][:, 128 * j + 64 * second : 128 * j + 64 * second + 64],
            ),
            axis=1,
        )

    w_query, w_key, w_value, w_out_t = tiles(0, 0, 3), tiles(1, 1, 3), tiles(2, 0, 4), tiles(5, 1, 4)
    w_out_other = sibling(w_out_t)
    w_up, w_down = w_feed[:, 0], w_feed[:, 1]
    b_up = jnp.stack((up_bias, small_far[3]))
    order, order_far = small[2, :local], small_far[2, :local]
    swapped = (
        jnp.concatenate((order[:128], order_far[:128], order[128:], order_far[128:])) > 0.5
    )
    x_flat = x_rows.reshape(-1, width)
    own_count = x_flat.shape[0] // 2
    attn_shape = (2, blocks, 2 * quarter, columns)
    compact_shape = (2, blocks, 2 * cap, columns)
    picks = jnp.transpose(picks_b.reshape(blocks, 2, 2, cap, slots), (1, 0, 2, 3, 4))
    select = jnp.transpose(
        select_b.reshape(blocks, 2, 2, cap, quarter), (1, 0, 2, 3, 4)
    ).reshape(-1, cap, quarter)
    runs_own = 2 * blocks

    def compact(rows, which=slice(None), **kw):
        source = select[which]
        out = jnp.einsum(
            "ukr,urw->ukw",
            source.astype(rows.dtype),
            rows.reshape(source.shape[0], quarter, -1),
            preferred_element_type=F32,
            **kw,
        )
        return out.reshape(-1, rows.shape[-1])

    def spread(rows, which=slice(None), **kw):
        source = select[which]
        out = jnp.einsum(
            "ukr,ukw->urw",
            source.astype(rows.dtype),
            rows.reshape(source.shape[0], cap, -1),
            preferred_element_type=F32,
            **kw,
        )
        return out.reshape(-1, rows.shape[-1])

    own_runs, other_runs = slice(0, runs_own), slice(runs_own, None)
    exact = {"precision": lax.Precision.HIGHEST}
    grads_in = pick(out_grad.reshape(2, blocks, slots, width), p)
    grad_y = jnp.einsum(
        "beki,biw->bekw", picks[0], grads_in, preferred_element_type=F32
    ).reshape(-1, width)

    q_far = partner(q_compact)
    swapped_lanes = swapped[None, None, None, :]
    attn_other = sibling(attention[1]).reshape(own_count, columns)
    branch = mm_t(attention[0].reshape(own_count, columns), w_out_t) + mm_t(
        attn_other, w_out_other
    )
    sum_one = x_flat[:own_count].astype(F32) + branch + out_bias
    hidden = norm_parts(sum_one)[0] * first_gain + first_shift
    hidden_low = hidden.astype(BF16)
    hidden_other = sibling(hidden_low)
    hidden_all = jnp.concatenate((hidden_low, hidden_other))

    def feed(i):
        pre = mm(hidden_all, w_up[i]) + b_up[i]
        activated = jax.nn.gelu(pre, approximate=False).astype(BF16)
        return mm_t(activated, w_down[i])

    feed_term = feed(0) + feed(1)
    feed_out = (
        feed_term[:own_count]
        + sibling(feed_term[own_count:].astype(BF16)).astype(F32)
        + down_bias
    )
    sum_two = hidden + feed_out
    out_rows = (norm_parts(sum_two)[0] * second_gain + second_shift).astype(BF16)

    def to_output(rows):
        rows = rows.reshape(blocks, 2, quarter, width)
        kept = pick(rows, p, 1)
        moved = across(pick(rows, 1 - p, 1))
        return ordered(p, kept, moved).reshape(block_count, quarter, width)

    out_y = to_output(out_rows)

    one_c = compact(sum_one, own_runs, **exact)
    two_c = compact(sum_two, own_runs, **exact)
    normed_two, inverse_two = norm_parts(two_c)
    normed_one, inverse_one = norm_parts(one_c)
    hidden_c = (normed_one * first_gain + first_shift).astype(BF16)
    d_second = norm_back(grad_y, normed_two, inverse_two, second_gain)
    g_second_gain = jnp.sum(grad_y * normed_two, axis=0)
    g_second_shift = jnp.sum(grad_y, axis=0)
    d_feed = d_second.astype(BF16)
    g_down_bias = jnp.sum(d_feed.astype(F32), axis=0)
    d_feed_all = jnp.concatenate((d_feed, sibling(d_feed)))
    hidden_c_all = jnp.concatenate(
        (hidden_c, compact(hidden_other, other_runs).astype(BF16))
    )
    g_up, g_down, g_up_bias, d_hidden_term = [], [], [], 0.0
    for i in range(2):
        pre = mm(hidden_c_all, w_up[i]) + b_up[i]
        cdf = 0.5 * (1.0 + lax.erf(pre * (0.5**0.5)))
        density = jnp.exp(-0.5 * pre * pre) * (0.5 / jnp.pi) ** 0.5
        activated = (pre * cdf).astype(BF16)
        d_pre = (mm(d_feed_all, w_down[i]) * (cdf + pre * density)).astype(BF16)
        g_up_bias.append(jnp.sum(d_pre.astype(F32), axis=0))
        g_up.append(t_mm(hidden_c_all, d_pre).astype(BF16))
        g_down.append(t_mm(d_feed_all, activated).astype(BF16))
        d_hidden_term = d_hidden_term + mm_t(d_pre, w_up[i])
    compact_own = d_feed.shape[0]
    d_hidden = (
        d_second
        + d_hidden_term[:compact_own]
        + sibling(d_hidden_term[compact_own:].astype(BF16)).astype(F32)
    )
    pieces = (2, width // piece_rows, piece_rows, hidden_piece)
    s_up = reduce_scatter(jnp.stack(g_up).reshape(pieces), True)
    s_down = reduce_scatter(jnp.stack(g_down).reshape(pieces), False).T
    g_first_gain = jnp.sum(d_hidden * normed_one, axis=0)
    g_first_shift = jnp.sum(d_hidden, axis=0)
    d_first = norm_back(d_hidden, normed_one, inverse_one, first_gain)
    d_branch = d_first.astype(BF16)
    g_out_bias = jnp.sum(d_branch.astype(F32), axis=0)
    d_branch_all = jnp.concatenate((d_branch, sibling(d_branch)))
    d_attention = mm(d_branch_all, w_out_t).astype(BF16).reshape(compact_shape)
    d_attention_far = partner(d_attention)

    (d_queries_c,) = per_head_pair(
        query_back_kernel,
        [
            q_compact,
            d_attention,
            keys_used.reshape(attn_shape),
            values_used.reshape(attn_shape),
        ],
        1,
        q_compact,
        6 * slots * block_rows * columns * blocks,
    )
    d_keys, d_values = per_head_pair(
        key_back_kernel,
        [
            jnp.where(swapped_lanes, q_far, q_compact),
            jnp.where(swapped_lanes, d_attention_far, d_attention),
            keys.reshape(attn_shape),
            values.reshape(attn_shape),
        ],
        2,
        keys.reshape(attn_shape),
        8 * slots * block_rows * columns * blocks,
    )
    d_queries_c = d_queries_c.reshape(-1, columns)
    d_queries = spread(d_queries_c).astype(BF16)
    d_keys = d_keys.reshape(-1, columns)
    d_values = d_values.reshape(-1, columns)
    term = mm_t(d_queries, w_query) + mm_t(d_keys, w_key) + mm_t(d_values, w_value)
    grad_rows = (
        term[:own_count]
        + sibling(term[own_count:].astype(BF16)).astype(F32)
        + spread(d_first, own_runs, **exact)
    ).astype(BF16)
    grad_x = to_output(grad_rows)

    g_query_bias = jnp.sum(d_queries_c.astype(F32), axis=0)
    g_value_bias = jnp.sum(d_values.astype(F32), axis=0)
    g_attn = jnp.stack(
        (
            t_mm(x_flat, d_queries).astype(BF16),
            t_mm(x_flat, d_keys).astype(BF16),
            t_mm(x_flat, d_values).astype(BF16),
            t_mm(d_branch_all, compact(attention.reshape(-1, columns)).astype(BF16)).astype(BF16),
        ),
        axis=1,
    )
    g_attn = jnp.stack(
        (
            jnp.concatenate((g_attn[..., 0:128], g_attn[..., 256:320]), axis=-1),
            jnp.concatenate((g_attn[..., 128:256], g_attn[..., 320:384]), axis=-1),
        )
    ).reshape(
        2, width // piece_rows, 2, half, 4 * local
    )
    s_attn = jnp.concatenate(
        (
            reduce_scatter(g_attn[:, :, 0], True),
            reduce_scatter(g_attn[:, :, 1], False),
        )
    )

    def widen(own_first, size):
        if own_first.shape[0] != 2:
            own_first = jnp.stack(
                (
                    jnp.concatenate((own_first[0:128], own_first[256:320])),
                    jnp.concatenate((own_first[128:256], own_first[320:384])),
                )
            )
        by_p = ordered(p, own_first[0], own_first[1])
        zero = jnp.zeros_like(by_p)
        return jnp.where(
            c == 0,
            jnp.stack((by_p, zero), axis=1),
            jnp.stack((zero, by_p), axis=1),
        ).reshape(size)

    vectors = [
        widen(g_query_bias, HEADS * HD),
        widen(g_value_bias, HEADS * HD),
        g_out_bias,
        g_first_gain,
        g_first_shift,
        widen(jnp.stack(g_up_bias), 4 * hidden_piece),
        g_down_bias,
        g_second_gain,
        g_second_shift,
    ]
    summed = sum_all(jnp.concatenate(vectors))
    ends, start = [], 0
    for vector in vectors:
        ends.append(summed[start : start + vector.shape[0]])
        start += vector.shape[0]
    (
        v_query_bias,
        v_value_bias,
        v_out_bias,
        v_first_gain,
        v_first_shift,
        v_up_bias,
        v_down_bias,
        v_second_gain,
        v_second_shift,
    ) = ends
    return (
        out_y,
        grad_x,
        s_attn[:, :local],
        v_query_bias,
        s_attn[:, local : 2 * local],
        s_attn[:, 2 * local : 3 * local],
        v_value_bias,
        s_attn[:, 3 * local :].T,
        v_out_bias,
        v_first_gain,
        v_first_shift,
        s_up,
        v_up_bias,
        s_down,
        v_down_bias,
        v_second_gain,
        v_second_shift,
    )


def solution(mesh):
    in_specs = (
        P("dp", None, None),
        P("dp", "head"),
        P("head"),
        P("dp", "head"),
        P("dp", "head"),
        P("head"),
        P("head", "dp"),
        P(),
        P(),
        P(),
        P("dp", "head"),
        P("head"),
        P("head", "dp"),
        P(),
        P(),
        P(),
        P("head"),
        P("dp", None),
        P("dp", None, None),
    )
    out_specs = (
        P("dp", "head", None),
        P("dp", "head", None),
        P("dp", "head"),
        P(),
        P("dp", "head"),
        P("dp", "head"),
        P(),
        P("head", "dp"),
        P(),
        P(),
        P(),
        P("dp", "head"),
        P(),
        P("head", "dp"),
        P(),
        P(),
        P(),
    )
    return jax.shard_map(
        per_device, mesh=mesh, in_specs=in_specs, out_specs=out_specs, check_vma=False
    )
```

```python
import functools

import jax
import jax.numpy as jnp
from jax import lax
from jax.experimental import pallas as pl
from jax.experimental.pallas import tpu as pltpu
from jax.sharding import PartitionSpec as P

HEADS = 12
HD = 64
FF = 3072
EPSILON = 1e-12
F32 = jnp.float32
BF16 = jnp.bfloat16
SCALE = HD ** (-0.5)
MESH = pl.DeviceIdType.MESH


def flip(block, axis, bit):
    n = lax.axis_size(axis)
    return lax.ppermute(block, axis, [(i, i ^ bit) for i in range(n)])


def shift(block, axis, distance):
    n = lax.axis_size(axis)
    return lax.ppermute(block, axis, [(i, (i + distance) % n) for i in range(n)])


def sibling(block):
    return flip(block, "head", 1)


def across(block):
    return flip(block, "head", 2)


def partner(block):
    return shift(block, "dp", lax.axis_size("dp") // 2)


def pick(array, index, axis=0):
    return lax.dynamic_index_in_dim(array, index, axis, keepdims=False)


def ordered(low, own, other, axis=0):
    return jnp.stack(
        (jnp.where(low == 0, own, other), jnp.where(low == 0, other, own)), axis=axis
    )


def mm(a, b):
    return jnp.dot(a, b, preferred_element_type=F32)


def mm_t(a, b):
    return lax.dot_general(a, b, (((1,), (1,)), ((), ())), preferred_element_type=F32)


def t_mm(a, b):
    return lax.dot_general(a, b, (((0,), (0,)), ((), ())), preferred_element_type=F32)


def norm_parts(rows):
    centered = rows - jnp.mean(rows, axis=-1, keepdims=True)
    inverse = lax.rsqrt(jnp.mean(centered * centered, axis=-1, keepdims=True) + EPSILON)
    return centered * inverse, inverse


def norm_back(incoming, normed, inverse, gain):
    scaled = incoming * gain
    return inverse * (
        scaled
        - jnp.mean(scaled, axis=-1, keepdims=True)
        - normed * jnp.mean(scaled * normed, axis=-1, keepdims=True)
    )


def gather(piece, x_first):
    n = lax.axis_size("dp")
    if n != 8:
        mine = lax.all_gather(piece, "dp", axis=0, tiled=False)
        return jnp.stack((mine, across(mine)))
    index = lax.axis_index("dp")
    z, x = index // 2, index % 2
    column = jnp.zeros((4,) + piece.shape, piece.dtype)
    column = lax.dynamic_update_index_in_dim(column, piece, z, 0)
    for k in (1, 2, 3):
        column = lax.dynamic_update_index_in_dim(
            column, shift(piece, "dp", 2 * k), (z - k) % 4, 0
        )
    if x_first:
        plane = ordered(x, column, flip(column, "dp", 1), axis=1)
        both = jnp.stack((plane, across(plane)))
    else:
        both = jnp.stack((column, across(column)))
        both = ordered(x, both, flip(both, "dp", 1), axis=2)
    return both.reshape((2, 8) + piece.shape)


def reduce_scatter(terms, x_last):
    n = lax.axis_size("dp")
    if n != 8:
        total = terms[0].astype(F32) + across(terms[1].astype(BF16)).astype(F32)
        return lax.psum_scatter(total, "dp", scatter_dimension=0, tiled=False)
    index = lax.axis_index("dp")
    z, x = index // 2, index % 2
    terms = terms.reshape((2, 4, 2) + terms.shape[2:])
    if x_last:
        arrived = across(terms[1])
        plane = (terms[0].astype(F32) + arrived.astype(F32)).astype(BF16)
        arrived = flip(pick(plane, 1 - x, 1), "dp", 1)
        column = pick(plane, x, 1).astype(F32) + arrived.astype(F32)
    else:
        arrived = flip(pick(terms, 1 - x, 2), "dp", 1)
        both = (pick(terms, x, 2).astype(F32) + arrived.astype(F32)).astype(BF16)
        column = both[0].astype(F32) + across(both[1]).astype(F32)
    column = column.astype(BF16)
    total = pick(column, z).astype(F32)
    for k in (1, 2, 3):
        total = total + shift(pick(column, (z + k) % 4), "dp", 2 * k).astype(F32)
    return total


def lane_masks(scale):
    lane = lax.broadcasted_iota(jnp.int32, (1, 2 * HD), 1)
    first = jnp.where(lane < HD, 1.0, 0.0)
    return [(first * scale).astype(BF16), ((1.0 - first) * scale).astype(BF16)]


def rows_of(ref):
    a, b, w = ref.shape
    return ref[...].reshape(a * b, w)


def pair_lanes(halves):
    lane = lax.broadcasted_iota(jnp.int32, halves[0].shape, 1)
    return jnp.where(lane < HD, halves[0], halves[1])


def halves_joined(low, high):
    lane = lax.broadcasted_iota(jnp.int32, low.shape, 1)
    return jnp.where(lane < HD, low, pltpu.roll(high, HD, 1))


def highs_joined(low, high):
    lane = lax.broadcasted_iota(jnp.int32, low.shape, 1)
    return jnp.where(lane < HD, pltpu.roll(low, HD, 1), high)


def head_tiles(row_own, row_other):
    return (
        row_own[:, :128],
        row_other[:, :128],
        halves_joined(row_own[:, 128:256], row_other[:, 128:256]),
    )


def project(x, wa_ref, count):
    width = x.shape[1]
    tiles = []
    for p in range(2):
        w = wa_ref[p].reshape(width, wa_ref.shape[-1])
        out = mm(x, w[:, count[0] : count[1]])
        tiles.append([out[:, 128 * i : 128 * (i + 1)] for i in range(out.shape[1] // 128)])
    return tiles


def forward_own(b, x_ref, wa_ref, bias, q_ref, k_ref, v_ref):
    rows = x_ref.shape[2] * x_ref.shape[3] * 2
    x = x_ref[:, b].reshape(rows, x_ref.shape[-1])
    one, two = project(x, wa_ref, (0, 640))
    b_query, b_value = bias
    parts = (
        (q_ref, (one[0], two[0], halves_joined(one[3], two[3])), b_query),
        (k_ref, (one[1], two[1], highs_joined(one[3], two[3])), None),
        (v_ref, (one[2], two[2], halves_joined(one[4], two[4])), b_value),
    )
    for ref, tiles, added in parts:
        for t in range(3):
            tile = tiles[t] if added is None else tiles[t] + added[t]
            ref[:, b, :, 128 * t : 128 * (t + 1)] = tile.astype(BF16).reshape(2, rows // 2, 128)


def forward_attend(b, xp_ref, wa_ref, bias, swapped, q_ref, k_ref, v_ref, ku_ref, vu_ref, o_ref):
    rows = xp_ref.shape[2] * xp_ref.shape[3] * 2
    x = xp_ref[:, b].reshape(rows, xp_ref.shape[-1])
    one, two = project(x, wa_ref, (128, 640))
    far_keys = (one[0], two[0], highs_joined(one[2], two[2]))
    far_values = (one[1], two[1], halves_joined(one[3], two[3]))
    masks = lane_masks(SCALE)
    for t in range(3):
        lanes = slice(128 * t, 128 * (t + 1))

        def load(ref):
            return ref[:, b, :, lanes].reshape(rows, 128)

        take_far = swapped[t] > 0.5
        k = jnp.where(take_far, far_keys[t], load(k_ref).astype(F32)).astype(BF16)
        v = jnp.where(
            take_far, far_values[t] + bias[1][t], load(v_ref).astype(F32)
        ).astype(BF16)
        ku_ref[:, b, :, lanes] = k.reshape(2, rows // 2, 128)
        vu_ref[:, b, :, lanes] = v.reshape(2, rows // 2, 128)
        q = load(q_ref)
        outs = []
        for mask in masks:
            s = mm_t(q * mask, k)
            raised = jnp.exp(s - jnp.max(s, axis=-1, keepdims=True))
            total = jnp.sum(raised, axis=-1, keepdims=True)
            outs.append(mm(raised.astype(BF16), v) / total)
        o_ref[:, b, :, lanes] = pair_lanes(outs).astype(BF16).reshape(2, rows // 2, 128)


def forward_listed(b, member, row_ref, col_ref, q_ref, picks_ref, select_ref, qc_ref):
    slots = row_ref.shape[-1]
    quarter = q_ref.shape[2] // 2
    cap = slots // 4
    row, col = row_ref[b], col_ref[b]
    bits = quarter.bit_length() - 1
    run_row = lax.shift_right_arithmetic(row, bits)
    run_col = lax.shift_right_arithmetic(col, bits)
    before = lax.broadcasted_iota(jnp.int32, (slots, slots), 0) < lax.broadcasted_iota(
        jnp.int32, (slots, slots), 1
    )
    same = jnp.where(run_col == run_row, jnp.where(before, 1.0, 0.0), 0.0)
    rank = jnp.sum(same, axis=0, keepdims=True)
    line = lax.broadcasted_iota(jnp.int32, (slots, 1), 0)
    place = line // cap
    wanted_run = jnp.where(
        place == 0, member, jnp.where(place == 1, member + 2, jnp.where(place == 2, 1 - member, 3 - member))
    )
    wanted_rank = (line % cap).astype(F32)
    picks = jnp.where(run_row == wanted_run, jnp.where(rank == wanted_rank, 1.0, 0.0), 0.0).astype(BF16)
    lane = lax.broadcasted_iota(jnp.int32, (slots, quarter), 1)
    places = jnp.where(jnp.bitwise_and(col, quarter - 1) == lane, 1.0, 0.0).astype(BF16)
    select = mm(picks, places).astype(BF16)
    picks_ref[b] = picks
    select_ref[b] = select
    for s in range(2):
        for e in range(2):
            at = (2 * s + e) * cap
            rows = q_ref[s, b, quarter * e : quarter * (e + 1), :]
            qc_ref[s, b, cap * e : cap * (e + 1), :] = mm(select[at : at + cap], rows).astype(BF16)


def forward_kernel(comm, *refs):
    if comm:
        (
            a_ref, b_ref, t_ref, small_ref, row_ref, col_ref,
            wa_ref, wb_ref, x_ref, xt_ref, o_ref, k_ref, v_ref, ku_ref, vu_ref, qc_ref, picks_ref, select_ref, far_ref,
            xp_ref, q_ref, local_sem, send_sem, recv_sem,
        ) = refs
    else:
        (
            wa_ref, x_ref, xp_ref, small_ref, far_ref, row_ref, col_ref,
            xt_ref, o_ref, k_ref, v_ref, ku_ref, vu_ref, qc_ref, picks_ref, select_ref,
            q_ref,
        ) = refs
    blocks = x_ref.shape[1]
    head = lax.axis_index("head")
    member, pair = lax.rem(head, 2), lax.div(head, 2)

    def listed(b, carry):
        forward_listed(b, member, row_ref, col_ref, q_ref, picks_ref, select_ref, qc_ref)
        return carry

    def turned(i, carry):
        s, rest = lax.div(i, 2 * blocks), lax.rem(i, 2 * blocks)
        part = x_ref[s, lax.div(rest, 2), lax.rem(rest, 2)]
        quarter = part.shape[0]
        xt_ref[:, pl.ds(pl.multiple_of(i * quarter, quarter), quarter)] = part.T
        return carry

    def bias_of():
        own, other = small_ref[...], far_ref[...]
        rows = [head_tiles(own[i : i + 1], other[i : i + 1]) for i in range(3)]
        return (rows[0], rows[1]), rows[2]

    if not comm:
        bias, swapped = bias_of()
        lax.fori_loop(0, 4 * blocks, turned, 0)

        def own_block(b, carry):
            forward_own(b, x_ref, wa_ref, bias, q_ref, k_ref, v_ref)
            return carry

    if comm:
        index = lax.axis_index("dp")
        z, x = lax.div(index, 2), lax.rem(index, 2)
        x_peer = {"dp": 2 * z + 1 - x}
        y_peer = {"head": lax.rem(head + 2, 4)}
        sibling_peer = {"head": 2 * pair + 1 - member}
        z_peers = [{"dp": lax.rem(index + 2 * k, 8)} for k in (1, 2, 3)]
        barrier = pltpu.get_barrier_semaphore()
        for peer in [x_peer, y_peer, sibling_peer] + z_peers:
            pl.semaphore_signal(barrier, inc=1, device_id=peer, device_id_type=MESH)
        counter = [0]

        def local(src, dst, i):
            copy = pltpu.make_async_copy(src, dst, local_sem.at[i])
            copy.start()
            return copy

        def send(src, dst, peer):
            i = counter[0]
            counter[0] += 1
            copy = pltpu.make_async_remote_copy(
                src_ref=src,
                dst_ref=dst,
                send_sem=send_sem.at[i],
                recv_sem=recv_sem.at[i],
                device_id=peer,
                device_id_type=MESH,
            )
            copy.start()
            sent.append(copy)
            return copy

        def far_copy(b):
            return pltpu.make_async_remote_copy(
                src_ref=x_ref.at[0, b],
                dst_ref=xp_ref.at[0, b],
                send_sem=send_sem.at[15 + b],
                recv_sem=recv_sem.at[15 + b],
                device_id=z_peers[1],
                device_id_type=MESH,
            )

        def near_copy(b):
            return pltpu.make_async_remote_copy(
                src_ref=xp_ref.at[0, b],
                dst_ref=xp_ref.at[1, b],
                send_sem=send_sem.at[15 + blocks + b],
                recv_sem=recv_sem.at[15 + blocks + b],
                device_id=sibling_peer,
                device_id_type=MESH,
            )

        sent = []
        quarters = (member, member + 2, 1 - member, 3 - member)
        fills = [
            local(t_ref.at[pl.ds(blocks * pair, blocks), quarters[2 * s + e]], x_ref.at[s, :, e], 2 * s + e)
            for s in range(2)
            for e in range(2)
        ]
        fill_a = local(a_ref, wa_ref.at[0, z, x], 4)
        fill_b = local(b_ref, wb_ref.at[0, :, z, x], 5)
        pl.semaphore_wait(barrier, 6)
        a_z = [send(a_ref, wa_ref.at[0, z, x], peer) for peer in z_peers]
        far = send(small_ref, far_ref, y_peer)
        b_z = [send(b_ref, wb_ref.at[0, :, z, x], peer) for peer in z_peers]
        for fill in fills:
            fill.wait()
        for b in range(blocks):
            far_copy(b).start()
        lax.fori_loop(0, 4 * blocks, turned, 0)
        half = a_ref.shape[0] // 2
        up, low = pl.ds(0, half), pl.ds(half, half)
        fill_a.wait()
        for copy in a_z:
            copy.wait_recv()
        a_x = send(wa_ref.at[0, :, x, up], wa_ref.at[0, :, x, up], x_peer)
        a_y = send(wa_ref.at[0, :, x, low], wa_ref.at[1, :, x, low], y_peer)
        a_x.wait_recv()
        a_xy = send(wa_ref.at[0, :, :, up], wa_ref.at[1, :, :, up], y_peer)
        a_y.wait_recv()
        a_yx = send(wa_ref.at[:, :, x, low], wa_ref.at[:, :, x, low], x_peer)
        fill_b.wait()
        for copy in b_z:
            copy.wait_recv()
        b_x = send(wb_ref.at[0, 0, :, x], wb_ref.at[0, 0, :, x], x_peer)
        b_y = send(wb_ref.at[0, 1, :, x], wb_ref.at[1, 1, :, x], y_peer)
        far.wait_recv()
        a_xy.wait_recv()
        a_yx.wait_recv()
        bias, swapped = bias_of()

        def own_block(b, carry):
            forward_own(b, x_ref, wa_ref, bias, q_ref, k_ref, v_ref)
            return carry

    lax.fori_loop(0, blocks, own_block, 0)
    lax.fori_loop(0, blocks, listed, 0)
    if comm:
        b_x.wait_recv()
        b_xy = send(wb_ref.at[0, 0], wb_ref.at[1, 0], y_peer)
        b_y.wait_recv()
        b_yx = send(wb_ref.at[:, 1, :, x], wb_ref.at[:, 1, :, x], x_peer)
        def attend_block(b, carry):
            far_copy(b).wait_recv()
            near = near_copy(b)
            near.start()
            near.wait_recv()
            forward_attend(b, xp_ref, wa_ref, bias, swapped, q_ref, k_ref, v_ref, ku_ref, vu_ref, o_ref)
            return carry

        lax.fori_loop(0, blocks, attend_block, 0)
        b_xy.wait_recv()
        b_yx.wait_recv()
        for copy in sent:
            copy.wait_send()
        for b in range(blocks):
            far_copy(b).wait_send()
            near_copy(b).wait_send()
    else:

        def attend_block(b, carry):
            forward_attend(b, xp_ref, wa_ref, bias, swapped, q_ref, k_ref, v_ref, ku_ref, vu_ref, o_ref)
            return carry

        lax.fori_loop(0, blocks, attend_block, 0)


def vmem_spec():
    return pl.BlockSpec(memory_space=pltpu.VMEM)


def any_spec():
    return pl.BlockSpec(memory_space=pl.ANY)


def forward(tokens, piece_a, piece_b, small, listed, member, pair):
    n = lax.axis_size("dp")
    block_count, block_rows, width = tokens.shape
    blocks, quarter = block_count // 2, block_rows // 4
    slots = listed.shape[1]
    cap = slots // 4
    lanes = 6 * HD
    tokens = tokens.reshape(block_count, 4, quarter, width)
    row, col = listed[:, None, :], listed[:, :, None]
    rows_shape = (2, blocks, 2, quarter, width)

    def out(*shape, dtype=BF16):
        return jax.ShapeDtypeStruct(shape, dtype)

    dense = (2, blocks, 2 * quarter, lanes)
    tail = [out(width, 2 * blocks * 2 * quarter)] + [out(*dense)] * 5 + [
        out(2, blocks, 2 * cap, lanes),
        out(blocks, slots, slots),
        out(blocks, slots, quarter),
    ]
    params = dict(vmem_limit_bytes=60 * 2**20, has_side_effects=True)
    if n == 8:
        shapes = [
            out(2, 4, 2, *piece_a.shape),
            out(2, 2, 4, 2, *piece_b.shape[1:]),
            out(*rows_shape),
            *tail,
            out(*small.shape, dtype=F32),
        ]
        specs = [vmem_spec()] * len(shapes)
        specs[1] = any_spec()
        results = pl.pallas_call(
            functools.partial(forward_kernel, True),
            out_shape=shapes,
            in_specs=[vmem_spec(), vmem_spec(), any_spec()] + [vmem_spec()] * 3,
            out_specs=specs,
            scratch_shapes=[
                pltpu.VMEM(rows_shape, BF16),
                pltpu.VMEM(dense, BF16),
                pltpu.SemaphoreType.DMA((6,)),
                pltpu.SemaphoreType.DMA((15 + 2 * blocks,)),
                pltpu.SemaphoreType.DMA((15 + 2 * blocks,)),
            ],
            compiler_params=pltpu.CompilerParams(collective_id=1, **params),
        )(piece_a, piece_b, tokens, small, row, col)
        w_attn, w_feed, rows, *rest, far = results
    else:
        mine = pick(tokens.reshape(2, blocks, 2, 2, quarter, width), pair)
        rows = jnp.stack((pick(mine, member, 2), pick(mine, 1 - member, 2)))
        w_attn = gather(piece_a, True)
        w_feed = jnp.stack([gather(piece_b[i], True) for i in range(2)], axis=1)
        far = across(small)
        shapes = tail
        rest = pl.pallas_call(
            functools.partial(forward_kernel, False),
            out_shape=shapes,
            in_specs=[vmem_spec()] * 7,
            out_specs=[vmem_spec()] * len(shapes),
            scratch_shapes=[pltpu.VMEM(dense, BF16)],
            compiler_params=pltpu.CompilerParams(vmem_limit_bytes=60 * 2**20),
        )(w_attn.reshape(2, width, -1), rows, partner(rows), small, far, row, col)
    w_attn = w_attn.reshape(2, width, -1)
    w_feed = w_feed.reshape(2, 2, width, -1)
    return (w_attn, w_feed, rows, *rest, far)


def back_queries(b, qc_ref, g_ref, ku_ref, vu_ref, select_ref, o_ref, dt_ref, oc_ref, total_ref):
    rows = ku_ref.shape[2] * 2
    slots = qc_ref.shape[2] * 2
    cap = slots // 4
    quarter = rows // 4
    select = select_ref[b]
    tiles = []
    for t in range(3):
        lanes = slice(128 * t, 128 * (t + 1))
        q = qc_ref[:, b, :, lanes].reshape(slots, 128)
        g = g_ref[:, b, :, lanes].reshape(slots, 128)
        k = ku_ref[:, b, :, lanes].reshape(rows, 128)
        v = vu_ref[:, b, :, lanes].reshape(rows, 128)
        outs = []
        for mask, one in zip(lane_masks(SCALE), lane_masks(1.0)):
            s = mm_t(q * mask, k)
            raised = jnp.exp(s - jnp.max(s, axis=-1, keepdims=True))
            probs = raised / jnp.sum(raised, axis=-1, keepdims=True)
            d_probs = mm_t(g * one, v)
            inner = jnp.sum(d_probs * probs, axis=-1, keepdims=True)
            d_scores = (probs * (d_probs - inner)).astype(BF16)
            outs.append(mm(d_scores, k) * SCALE)
        tile = pair_lanes(outs).astype(BF16)
        total_ref[0:1, lanes] += jnp.sum(tile.astype(F32), axis=0, keepdims=True)
        tiles.append(tile)
    for s in range(2):
        for e in range(2):
            at = (2 * s + e) * cap
            chosen = select[at : at + cap]
            own = slice(quarter * e, quarter * (e + 1))
            dense = [t_mm(chosen, tile[at : at + cap]) for tile in tiles]
            dt_ref[0, s, b, own, 0:128] = dense[0].astype(BF16)
            dt_ref[1, s, b, own, 0:128] = dense[1].astype(BF16)
            lane = lax.broadcasted_iota(jnp.int32, dense[2].shape, 1)
            for p in range(2):
                last = dense[2] if p == 0 else pltpu.roll(dense[2], HD, 1)
                dt_ref[p, s, b, own, 384:512] = jnp.where(lane < HD, last, 0.0).astype(BF16)
            rows_o = mm(chosen, o_ref[s, b, own, :])
            at_o = slice(cap * e, cap * (e + 1))
            lane = lax.broadcasted_iota(jnp.int32, (cap, 128), 1)
            for p in range(2):
                oc_ref[p, s, b, at_o, 128:256] = rows_o[:, 128 * p : 128 * (p + 1)].astype(BF16)
                last = rows_o[:, 256:384] if p == 1 else pltpu.roll(rows_o[:, 256:384], HD, 1)
                oc_ref[p, s, b, at_o, 0:128] = jnp.where(lane < HD, 0.0, last).astype(BF16)


def back_keys(b, swapped, qc_ref, g_ref, qf_ref, gf_ref, k_ref, v_ref, dt_ref, total_ref):
    rows = k_ref.shape[2] * 2
    slots = qc_ref.shape[2] * 2
    for t in range(3):
        lanes = slice(128 * t, 128 * (t + 1))
        take_far = swapped[t] > 0.5

        def chosen(near, far):
            near = near[:, b, :, lanes].reshape(slots, 128).astype(F32)
            far = far[:, b, :, lanes].reshape(slots, 128).astype(F32)
            return jnp.where(take_far, far, near).astype(BF16)

        q, g = chosen(qc_ref, qf_ref), chosen(g_ref, gf_ref)
        k = k_ref[:, b, :, lanes].reshape(rows, 128)
        v = v_ref[:, b, :, lanes].reshape(rows, 128)
        d_keys, d_values = [], []
        for mask, one in zip(lane_masks(SCALE), lane_masks(1.0)):
            s = mm_t(k, q * mask)
            raised = jnp.exp(s - jnp.max(s, axis=0, keepdims=True))
            probs = raised / jnp.sum(raised, axis=0, keepdims=True)
            d_probs = mm_t(v, g * one)
            inner = jnp.sum(d_probs * probs, axis=0, keepdims=True)
            d_scores = (probs * (d_probs - inner)).astype(BF16)
            d_keys.append(mm(d_scores, q) * SCALE)
            d_values.append(mm(probs.astype(BF16), g))
        dk, dv = pair_lanes(d_keys), pair_lanes(d_values)
        total_ref[1:2, lanes] += jnp.sum(dv.astype(BF16).astype(F32), axis=0, keepdims=True)
        half = (2, rows // 2, 128)
        if t < 2:
            dt_ref[t, :, b, :, 128:256] = dk.astype(BF16).reshape(half)
            dt_ref[t, :, b, :, 256:384] = dv.astype(BF16).reshape(half)
        else:
            lane = lax.broadcasted_iota(jnp.int32, dk.shape, 1)
            for p in range(2):
                last = pltpu.roll(dk, HD, 1) if p == 0 else dk
                before = dt_ref[p, :, b, :, 384:512].reshape(rows, 128).astype(F32)
                dt_ref[p, :, b, :, 384:512] = (
                    jnp.where(lane < HD, before, last).astype(BF16).reshape(half)
                )
                last = dv if p == 0 else pltpu.roll(dv, HD, 1)
                dt_ref[p, :, b, :, 512:640] = (
                    jnp.where(lane < HD, last, 0.0).astype(BF16).reshape(half)
                )


def back_weights(p, xt_ref, dt_ref, db_ref, oc_ref, ga_ref):
    width = xt_ref.shape[0]
    shape = ga_ref.shape[1:-1] + (128,)
    listed = db_ref.shape[0] * db_ref.shape[1] * db_ref.shape[2]
    d_branch = db_ref[...].reshape(listed, width)
    outs = mm(xt_ref[...], dt_ref[p].reshape(xt_ref.shape[1], 640))
    extra = t_mm(d_branch, oc_ref[p].reshape(listed, 256))
    for i in range(6):
        if i < 4:
            tile = outs[:, 128 * i : 128 * (i + 1)]
        elif i == 4:
            tile = outs[:, 512:640] + extra[:, 0:128]
        else:
            tile = extra[:, 128:256]
        ga_ref[p, ..., 128 * i : 128 * (i + 1)] = tile.astype(BF16).reshape(shape)


def back_rows(s, b, wa_ref, dt_ref):
    rows, width = dt_ref.shape[3], wa_ref.shape[-1]
    out = 0.0
    for p in range(2):
        w = wa_ref[p].reshape(-1, wa_ref.shape[-1])
        out = out + mm_t(dt_ref[p, s, b], w[:, 0:640])
    return out


def bias_totals(member, pair, total_ref):
    lane = lax.broadcasted_iota(jnp.int32, (1, 128), 1)
    line = lax.broadcasted_iota(jnp.int32, (8, 128), 0)
    first = jnp.zeros((8, 128), F32)
    second = jnp.zeros((8, 128), F32)
    for i in range(2):
        last = total_ref[i : i + 1, 256:384]
        for p in range(2):
            place = 4 * i + 2 * (pair if p == 0 else 1 - pair) + member
            tile = total_ref[i : i + 1, 128 * p : 128 * (p + 1)]
            third = last if p == 0 else pltpu.roll(last, HD, 1)
            first = first + jnp.where(line == place, tile, 0.0)
            second = second + jnp.where(line == place, jnp.where(lane < HD, third, 0.0), 0.0)
    return first, second


def back_kernel(comm, *refs):
    if comm:
        (
            gb_ref, qc_ref, g_ref, k_ref, v_ref, ku_ref, vu_ref, o_ref, xt_ref, wa_ref,
            select_ref, small_ref, far_ref, db_ref, df_ref, vec_ref,
            gx_ref, sa_ref, sb_ref, sum_ref,
            dt_ref, oc_ref, ga_ref, total_ref, qf_ref, gf_ref, term_ref, near_ref, rows_ref,
            b1_up, b1_low, b2, b3, a1_up, a1_low, a2, a3, vec1, vec4,
            local_sem, send_sem, recv_sem,
        ) = refs
    else:
        (
            qf_ref, gf_ref, qc_ref, g_ref, k_ref, v_ref, ku_ref, vu_ref, o_ref, xt_ref, wa_ref,
            select_ref, small_ref, far_ref, db_ref,
            ga_ref, term_ref, both_ref,
            dt_ref, oc_ref, total_ref,
        ) = refs
    blocks = k_ref.shape[1]
    head = lax.axis_index("head")
    member, pair = lax.rem(head, 2), lax.div(head, 2)
    swapped = head_tiles(small_ref[2:3], far_ref[2:3])
    total_ref[...] = jnp.zeros_like(total_ref)

    def queries(b, carry):
        back_queries(b, qc_ref, g_ref, ku_ref, vu_ref, select_ref, o_ref, dt_ref, oc_ref, total_ref)
        return carry

    def keys(b, carry):
        back_keys(b, swapped, qc_ref, g_ref, qf_ref, gf_ref, k_ref, v_ref, dt_ref, total_ref)
        return carry

    def weights(p, carry):
        back_weights(p, xt_ref, dt_ref, db_ref, oc_ref, ga_ref)
        return carry

    if not comm:
        lax.fori_loop(0, blocks, queries, 0)
        lax.fori_loop(0, blocks, keys, 0)
        lax.fori_loop(0, 2, weights, 0)

        def rows(i, carry):
            s, b = lax.div(i, blocks), lax.rem(i, blocks)
            term_ref[s, b] = back_rows(s, b, wa_ref, dt_ref)
            return carry

        lax.fori_loop(0, 2 * blocks, rows, 0)
        both_ref[0:8], both_ref[8:16] = bias_totals(member, pair, total_ref)
        return

    index = lax.axis_index("dp")
    z, x = lax.div(index, 2), lax.rem(index, 2)
    x_peer = {"dp": 2 * z + 1 - x}
    y_peer = {"head": lax.rem(head + 2, 4)}
    sibling_peer = {"head": 2 * pair + 1 - member}
    z_peers = [{"dp": lax.rem(index + 2 * k, 8)} for k in (1, 2, 3)]
    z_to = [lax.rem(z + k, 4) for k in (1, 2, 3)]
    barrier = pltpu.get_barrier_semaphore()
    for peer in [x_peer, y_peer, sibling_peer] + z_peers:
        pl.semaphore_signal(barrier, inc=1, device_id=peer, device_id_type=MESH)
    pl.semaphore_wait(barrier, 6)
    sent = []

    def send(src, dst, peer):
        i = len(sent)
        copy = pltpu.make_async_remote_copy(
            src_ref=src,
            dst_ref=dst,
            send_sem=send_sem.at[i],
            recv_sem=recv_sem.at[i],
            device_id=peer,
            device_id_type=MESH,
        )
        copy.start()
        sent.append(copy)
        return copy

    def plus(a, b):
        return (a.astype(F32) + b.astype(F32)).astype(BF16)

    def first_phase(up_other, low_other, up_buffer, low_buffer):
        return send(up_other, up_buffer, y_peer), send(low_other, low_buffer, x_peer)

    far_g = send(g_ref, gf_ref, z_peers[1])
    far_q = send(qc_ref, qf_ref, z_peers[1])
    b_up = send(gb_ref.at[1, 0], b1_up, y_peer)
    b_low = send(gb_ref.at[:, 1, :, 1 - x], b1_low, x_peer)
    lax.fori_loop(0, blocks, queries, 0)
    far_g.wait_recv()
    far_q.wait_recv()
    lax.fori_loop(0, blocks, keys, 0)

    vec_rows = vec_ref.shape[0]
    vec1[0, 0:vec_rows] = vec_ref[...]
    vec1[0, vec_rows : vec_rows + 8], vec1[0, vec_rows + 8 : vec_rows + 16] = bias_totals(
        member, pair, total_ref
    )
    v_sib = send(vec1.at[0], vec1.at[1], sibling_peer)

    halves = gb_ref.shape[2]

    def add_up(i, carry):
        b1_up[i] = plus(b1_up[i], gb_ref[0, 0, i])
        return carry

    def add_low(i, carry):
        for p in range(2):
            b1_low[p, i] = plus(b1_low[p, i], gb_ref[p, 1, i, x])
        return carry

    b_up.wait_recv()
    lax.fori_loop(0, halves, add_up, 0)
    b_up = send(b1_up.at[:, 1 - x], b2.at[0], x_peer)
    b_low.wait_recv()
    lax.fori_loop(0, halves, add_low, 0)
    b_low = send(b1_low.at[1], b2.at[1], y_peer)
    v_sib.wait_recv()
    vec1[2] = vec1[0] + vec1[1]
    v_y = send(vec1.at[2], vec1.at[3], y_peer)

    lax.fori_loop(0, 2, weights, 0)
    half = ga_ref.shape[3] // 2
    up, low = slice(0, half), slice(half, 2 * half)
    a_up = send(ga_ref.at[1, :, :, pl.ds(0, half)], a1_up, y_peer)
    a_low = send(ga_ref.at[:, :, 1 - x, pl.ds(half, half)], a1_low, x_peer)

    def rows_other(b, carry):
        term_ref[b] = back_rows(1, b, wa_ref, dt_ref).astype(BF16)
        return carry

    lax.fori_loop(0, blocks, rows_other, 0)
    term = send(term_ref, near_ref, sibling_peer)

    b_up.wait_recv()
    b_low.wait_recv()

    def add_second(i, carry):
        b2[0, i] = plus(b2[0, i], b1_up[i, x])
        b2[1, i] = plus(b2[1, i], b1_low[0, i])
        return carry

    lax.fori_loop(0, halves, add_second, 0)
    b_z = [send(b2.at[:, to], b3.at[k], peer) for k, (to, peer) in enumerate(zip(z_to, z_peers))]
    v_y.wait_recv()
    vec1[4] = vec1[2] + vec1[3]
    v_x = send(vec1.at[4], vec1.at[5], x_peer)

    a_up.wait_recv()

    def a_add_up(i, carry):
        a1_up[i] = plus(a1_up[i], ga_ref[0, i, :, up])
        return carry

    lax.fori_loop(0, halves, a_add_up, 0)
    a_up = send(a1_up.at[:, 1 - x], a2.at[0], x_peer)
    a_low.wait_recv()

    def a_add_low(i, carry):
        for p in range(2):
            a1_low[p, i] = plus(a1_low[p, i], ga_ref[p, i, x, low])
        return carry

    lax.fori_loop(0, halves, a_add_low, 0)
    a_low = send(a1_low.at[1], a2.at[1], y_peer)

    cap = df_ref.shape[1] // 2
    quarter = rows_ref.shape[2]
    term.wait_recv()

    def rows_own(b, carry):
        own = back_rows(0, b, wa_ref, dt_ref) + near_ref[b].astype(F32)
        for e in range(2):
            first = df_ref[b, cap * e : cap * (e + 1), :]
            high = first.astype(BF16)
            rest = (first - high.astype(F32)).astype(BF16)
            chosen = select_ref[b, cap * e : cap * (e + 1), :]
            spread = t_mm(chosen, high) + t_mm(chosen, rest)
            rows_ref[e, b] = (own[quarter * e : quarter * (e + 1)] + spread).astype(BF16)
        return carry

    lax.fori_loop(0, blocks, rows_own, 0)
    moved = send(rows_ref.at[1 - pair], gx_ref.at[pair], y_peer)
    kept = pltpu.make_async_copy(rows_ref.at[pair], gx_ref.at[pair], local_sem.at[0])
    kept.start()
    v_x.wait_recv()
    vec1[6] = vec1[4] + vec1[5]
    own_vec = pltpu.make_async_copy(vec1.at[6], vec4.at[z], local_sem.at[1])
    own_vec.start()
    v_z = [send(vec1.at[6], vec4.at[z], peer) for peer in z_peers]

    a_up.wait_recv()
    a_low.wait_recv()

    def a_add_second(i, carry):
        a2[0, i] = plus(a2[0, i], a1_up[i, x])
        a2[1, i] = plus(a2[1, i], a1_low[0, i])
        return carry

    lax.fori_loop(0, halves, a_add_second, 0)
    a_z = [send(a2.at[:, to], a3.at[k], peer) for k, (to, peer) in enumerate(zip(z_to, z_peers))]

    for copy in b_z:
        copy.wait_recv()
    for t in range(2):
        total = b2[t, z].astype(F32)
        for k in range(3):
            total = total + b3[k, t].astype(F32)
        sb_ref[t] = total
    own_vec.wait()
    for copy in v_z:
        copy.wait_recv()
    sum_ref[...] = (vec4[0] + vec4[1]) + (vec4[2] + vec4[3])
    for copy in a_z:
        copy.wait_recv()
    for t, part in enumerate((up, low)):
        total = a2[t, z].astype(F32)
        for k in range(3):
            total = total + a3[k, t].astype(F32)
        sa_ref[part] = total
    kept.wait()
    moved.wait_recv()
    for copy in sent:
        copy.wait_send()


def backward(gb, q_compact, d_attention, keys, values, keys_used, values_used, attention, rows_t, w_attn, select, small, far, d_branch, d_first, vectors):
    n = lax.axis_size("dp")
    _, blocks, block_half, lanes = keys.shape
    width = rows_t.shape[0]
    quarter = block_half // 2
    piece = width // n
    slots = select.shape[1]
    vec_rows = vectors.shape[0] + 16

    def out(*shape, dtype=BF16):
        return jax.ShapeDtypeStruct(shape, dtype)

    compact = (2, blocks, slots // 2, lanes)
    scratch = [
        pltpu.VMEM((2, 2, blocks, block_half, 640), BF16),
        pltpu.VMEM((2, 2, blocks, slots // 2, 256), BF16),
    ]
    shared = (q_compact, d_attention, keys, values, keys_used, values_used, attention, rows_t, w_attn, select, small, far, d_branch)
    if n == 8:
        half = piece // 2
        return pl.pallas_call(
            functools.partial(back_kernel, True),
            out_shape=[
                out(2, blocks, quarter, width),
                out(piece, width, dtype=F32),
                out(2, piece, width, dtype=F32),
                out(vec_rows, 128, dtype=F32),
            ],
            in_specs=[vmem_spec()] * 16,
            out_specs=[vmem_spec()] * 4,
            scratch_shapes=scratch
            + [
                pltpu.VMEM((2, 4, 2, piece, width), BF16),
                pltpu.VMEM((8, lanes), F32),
                pltpu.VMEM(compact, BF16),
                pltpu.VMEM(compact, BF16),
                pltpu.VMEM((blocks, block_half, width), BF16),
                pltpu.VMEM((blocks, block_half, width), BF16),
                pltpu.VMEM((2, blocks, quarter, width), BF16),
                pltpu.VMEM((4, 2, piece, width), BF16),
                pltpu.VMEM((2, 4, piece, width), BF16),
                pltpu.VMEM((2, 4, piece, width), BF16),
                pltpu.VMEM((3, 2, piece, width), BF16),
                pltpu.VMEM((4, 2, half, width), BF16),
                pltpu.VMEM((2, 4, half, width), BF16),
                pltpu.VMEM((2, 4, half, width), BF16),
                pltpu.VMEM((3, 2, half, width), BF16),
                pltpu.VMEM((7, vec_rows, 128), F32),
                pltpu.VMEM((4, vec_rows, 128), F32),
                pltpu.SemaphoreType.DMA((2,)),
                pltpu.SemaphoreType.DMA((24,)),
                pltpu.SemaphoreType.DMA((24,)),
            ],
            compiler_params=pltpu.CompilerParams(
                collective_id=2, vmem_limit_bytes=62 * 2**20, has_side_effects=True
            ),
        )(gb.reshape(2, 2, 4, 2, piece, width), *shared, d_first, vectors)
    ga, term, both = pl.pallas_call(
        functools.partial(back_kernel, False),
        out_shape=[
            out(2, 1, 1, width, width),
            out(2, blocks, block_half, width, dtype=F32),
            out(16, 128, dtype=F32),
        ],
        in_specs=[vmem_spec()] * 15,
        out_specs=[vmem_spec()] * 3,
        scratch_shapes=scratch + [pltpu.VMEM((8, lanes), F32)],
        compiler_params=pltpu.CompilerParams(vmem_limit_bytes=62 * 2**20),
    )(partner(q_compact), partner(d_attention), *shared)
    pair = lax.axis_index("head") // 2
    cap = slots // 4
    chosen = select[:, : 2 * cap].reshape(blocks, 2, cap, quarter).astype(F32)
    spread = jnp.einsum(
        "bekr,bekw->berw",
        chosen,
        d_first.reshape(blocks, 2, cap, width),
        precision=lax.Precision.HIGHEST,
    )
    own = term[0].reshape(spread.shape) + sibling(term[1].astype(BF16)).astype(F32).reshape(spread.shape)
    own = (own + spread).astype(BF16)
    grad_x = ordered(pair, pick(own, pair, 1), across(pick(own, 1 - pair, 1)))
    pieces = (2, n, piece, width)
    s_attn = reduce_scatter(ga.reshape(pieces), True)
    s_feed = jnp.stack([reduce_scatter(gb[:, i].reshape(pieces), True) for i in range(2)])
    return grad_x, s_attn, s_feed, lax.psum(jnp.concatenate((vectors, both)), ("dp", "head"))


def per_device(
    tokens,
    query_weight,
    query_bias,
    key_weight,
    value_weight,
    value_bias,
    out_weight,
    out_bias,
    first_gain,
    first_shift,
    up_weight,
    up_bias,
    down_weight,
    down_bias,
    second_gain,
    second_shift,
    block_order,
    masked_rows,
    out_grad,
):
    block_count, block_rows, width = tokens.shape
    quarter = block_rows // 4
    slots = masked_rows.shape[1]
    cap = slots // 4
    blocks = block_count // 2
    piece_rows = query_weight.shape[0]
    local = query_weight.shape[1]
    columns = 2 * local
    hidden_piece = up_weight.shape[1]
    head = lax.axis_index("head")
    c, p = head % 2, head // 2

    out_t = out_weight.T
    first, last = slice(0, 2 * HD), slice(2 * HD, 3 * HD)
    piece = jnp.concatenate(
        (
            query_weight[:, first],
            key_weight[:, first],
            value_weight[:, first],
            query_weight[:, last],
            key_weight[:, last],
            value_weight[:, last],
            out_t[:, last],
            out_t[:, first],
        ),
        axis=1,
    )
    half = piece_rows // 2

    def line(vector, size):
        return jnp.pad(vector, (0, size - vector.shape[0]))

    small = jnp.stack(
        [
            line(row, hidden_piece)
            for row in (
                query_bias,
                value_bias,
                jnp.repeat(block_order.astype(F32), HD),
                up_bias,
            )
        ]
        + [jnp.zeros((hidden_piece,), F32)] * 4
    )
    listed = pick(masked_rows.reshape(2, blocks, slots), p)
    (
        w_attn, w_feed, x_rows, rows_t, attention, keys, values, keys_used, values_used, q_compact, picks_b, select_b, small_far,
    ) = forward(tokens, piece, jnp.stack((up_weight, down_weight.T)), small, listed, c, p)

    def tiles(i, second, j):
        second = HD * second

        return jnp.concatenate(
            (
                w_attn[0][:, 128 * i : 128 * i + 128],
                w_attn[1][:, 128 * i : 128 * i + 128],
                w_attn[0][:, 128 * j + second : 128 * j + second + HD],
                w_attn[1][:, 128 * j + second : 128 * j + second + HD],
            ),
            axis=1,
        )

    w_out_t = tiles(5, 1, 4)
    w_out_other = sibling(w_out_t)
    w_up, w_down = w_feed[:, 0], w_feed[:, 1]
    b_up = jnp.stack((up_bias, small_far[3]))
    x_flat = x_rows.reshape(-1, width)
    own_count = x_flat.shape[0] // 2
    attn_shape = (2, blocks, 2 * quarter, columns)
    compact_shape = (2, blocks, 2 * cap, columns)
    picks = jnp.transpose(picks_b.reshape(blocks, 2, 2, cap, slots), (1, 0, 2, 3, 4))
    select = jnp.transpose(
        select_b.reshape(blocks, 2, 2, cap, quarter), (1, 0, 2, 3, 4)
    ).reshape(-1, cap, quarter)
    runs_own = 2 * blocks

    def compact(rows, which=slice(None), **kw):
        source = select[which]
        out = jnp.einsum(
            "ukr,urw->ukw",
            source.astype(rows.dtype),
            rows.reshape(source.shape[0], quarter, -1),
            preferred_element_type=F32,
            **kw,
        )
        return out.reshape(-1, rows.shape[-1])

    def spread(rows, which=slice(None), **kw):
        source = select[which]
        out = jnp.einsum(
            "ukr,ukw->urw",
            source.astype(rows.dtype),
            rows.reshape(source.shape[0], cap, -1),
            preferred_element_type=F32,
            **kw,
        )
        return out.reshape(-1, rows.shape[-1])

    own_runs, other_runs = slice(0, runs_own), slice(runs_own, None)
    exact = {"precision": lax.Precision.HIGHEST}
    grads_in = pick(out_grad.reshape(2, blocks, slots, width), p)
    grad_y = jnp.einsum(
        "beki,biw->bekw", picks[0], grads_in, preferred_element_type=F32
    ).reshape(-1, width)

    attn_other = sibling(attention[1]).reshape(own_count, columns)
    branch = mm_t(attention[0].reshape(own_count, columns), w_out_t) + mm_t(
        attn_other, w_out_other
    )
    sum_one = x_flat[:own_count].astype(F32) + branch + out_bias
    hidden = norm_parts(sum_one)[0] * first_gain + first_shift
    hidden_low = hidden.astype(BF16)
    hidden_other = sibling(hidden_low)
    hidden_all = jnp.concatenate((hidden_low, hidden_other))

    def feed(i):
        pre = mm(hidden_all, w_up[i]) + b_up[i]
        activated = jax.nn.gelu(pre, approximate=False).astype(BF16)
        return mm_t(activated, w_down[i])

    feed_term = feed(0) + feed(1)
    feed_out = (
        feed_term[:own_count]
        + sibling(feed_term[own_count:].astype(BF16)).astype(F32)
        + down_bias
    )
    sum_two = hidden + feed_out
    out_rows = (norm_parts(sum_two)[0] * second_gain + second_shift).astype(BF16)

    def to_output(rows):
        rows = rows.reshape(blocks, 2, quarter, width)
        kept = pick(rows, p, 1)
        moved = across(pick(rows, 1 - p, 1))
        return ordered(p, kept, moved).reshape(block_count, quarter, width)

    out_y = to_output(out_rows)

    one_c = compact(sum_one, own_runs, **exact)
    two_c = compact(sum_two, own_runs, **exact)
    normed_two, inverse_two = norm_parts(two_c)
    normed_one, inverse_one = norm_parts(one_c)
    hidden_c = (normed_one * first_gain + first_shift).astype(BF16)
    d_second = norm_back(grad_y, normed_two, inverse_two, second_gain)
    g_second_gain = jnp.sum(grad_y * normed_two, axis=0)
    g_second_shift = jnp.sum(grad_y, axis=0)
    d_feed = d_second.astype(BF16)
    g_down_bias = jnp.sum(d_feed.astype(F32), axis=0)
    d_feed_all = jnp.concatenate((d_feed, sibling(d_feed)))
    hidden_c_all = jnp.concatenate(
        (hidden_c, compact(hidden_other, other_runs).astype(BF16))
    )
    g_up, g_down, g_up_bias, d_hidden_term = [], [], [], 0.0
    for i in range(2):
        pre = mm(hidden_c_all, w_up[i]) + b_up[i]
        cdf = 0.5 * (1.0 + lax.erf(pre * (0.5**0.5)))
        density = jnp.exp(-0.5 * pre * pre) * (0.5 / jnp.pi) ** 0.5
        activated = (pre * cdf).astype(BF16)
        d_pre = (mm(d_feed_all, w_down[i]) * (cdf + pre * density)).astype(BF16)
        g_up_bias.append(jnp.sum(d_pre.astype(F32), axis=0))
        g_up.append(t_mm(hidden_c_all, d_pre).astype(BF16))
        g_down.append(t_mm(d_feed_all, activated).astype(BF16))
        d_hidden_term = d_hidden_term + mm_t(d_pre, w_up[i])
    compact_own = d_feed.shape[0]
    d_hidden = (
        d_second
        + d_hidden_term[:compact_own]
        + sibling(d_hidden_term[compact_own:].astype(BF16)).astype(F32)
    )
    gb = jnp.stack((jnp.stack(g_up), jnp.stack(g_down)), axis=1)
    g_first_gain = jnp.sum(d_hidden * normed_one, axis=0)
    g_first_shift = jnp.sum(d_hidden, axis=0)
    d_first = norm_back(d_hidden, normed_one, inverse_one, first_gain)
    d_branch = d_first.astype(BF16)
    g_out_bias = jnp.sum(d_branch.astype(F32), axis=0)
    d_branch_all = jnp.concatenate((d_branch, sibling(d_branch)))
    d_attention = mm(d_branch_all, w_out_t).astype(BF16).reshape(compact_shape)

    def widen(own_first):
        by_p = ordered(p, own_first[0], own_first[1])
        zero = jnp.zeros_like(by_p)
        return jnp.where(
            c == 0,
            jnp.stack((by_p, zero), axis=1),
            jnp.stack((zero, by_p), axis=1),
        ).reshape(-1)

    vectors = [
        g_out_bias,
        g_first_gain,
        g_first_shift,
        g_down_bias,
        g_second_gain,
        g_second_shift,
        widen(jnp.stack(g_up_bias)),
    ]
    flat = jnp.concatenate(vectors)
    flat = jnp.pad(flat, (0, -flat.shape[0] % 1024)).reshape(-1, 128)
    grad_x, s_attn, s_feed, summed = backward(
        gb, q_compact, d_attention, keys, values, keys_used, values_used, attention, rows_t, w_attn, select_b,
        small, small_far, d_branch_all.reshape(2, blocks, 2 * cap, width), d_first.reshape(blocks, 2 * cap, width), flat,
    )
    grad_x = grad_x.reshape(block_count, quarter, width)
    whole = summed[: flat.shape[0]].reshape(-1)
    ends, start = [], 0
    for vector in vectors:
        ends.append(whole[start : start + vector.shape[0]])
        start += vector.shape[0]
    v_out_bias, v_first_gain, v_first_shift, v_down_bias, v_second_gain, v_second_shift, v_up_bias = ends
    last = summed[flat.shape[0] :].reshape(2, 2, 4, 128)
    v_query_bias, v_value_bias = (
        jnp.concatenate((last[0, i], last[1, i, :, :HD]), axis=-1).reshape(-1)
        for i in range(2)
    )

    def columns_of(i, j, second):
        at = 128 * j + HD * second
        return jnp.concatenate((s_attn[:, 128 * i : 128 * (i + 1)], s_attn[:, at : at + HD]), axis=1)

    return (
        out_y,
        grad_x,
        columns_of(0, 3, 0),
        v_query_bias,
        columns_of(1, 3, 1),
        columns_of(2, 4, 0),
        v_value_bias,
        columns_of(5, 4, 1).T,
        v_out_bias,
        v_first_gain,
        v_first_shift,
        s_feed[0],
        v_up_bias,
        s_feed[1].T,
        v_down_bias,
        v_second_gain,
        v_second_shift,
    )


def solution(mesh):
    in_specs = (
        P("dp", None, None),
        P("dp", "head"),
        P("head"),
        P("dp", "head"),
        P("dp", "head"),
        P("head"),
        P("head", "dp"),
        P(),
        P(),
        P(),
        P("dp", "head"),
        P("head"),
        P("head", "dp"),
        P(),
        P(),
        P(),
        P("head"),
        P("dp", None),
        P("dp", None, None),
    )
    out_specs = (
        P("dp", "head", None),
        P("dp", "head", None),
        P("dp", "head"),
        P(),
        P("dp", "head"),
        P("dp", "head"),
        P(),
        P("head", "dp"),
        P(),
        P(),
        P(),
        P("dp", "head"),
        P(),
        P("head", "dp"),
        P(),
        P(),
        P(),
    )
    return jax.shard_map(
        per_device, mesh=mesh, in_specs=in_specs, out_specs=out_specs, check_vma=False
    )
```

```python
import functools

import jax
import jax.numpy as jnp
from jax import lax
from jax.experimental import pallas as pl
from jax.experimental.pallas import tpu as pltpu
from jax.sharding import PartitionSpec as P

HEADS = 12
HD = 64
FF = 3072
EPSILON = 1e-12
F32 = jnp.float32
BF16 = jnp.bfloat16
SCALE = HD ** (-0.5)
MESH = pl.DeviceIdType.MESH


def flip(block, axis, bit):
    n = lax.axis_size(axis)
    return lax.ppermute(block, axis, [(i, i ^ bit) for i in range(n)])


def shift(block, axis, distance):
    n = lax.axis_size(axis)
    return lax.ppermute(block, axis, [(i, (i + distance) % n) for i in range(n)])


def sibling(block):
    return flip(block, "head", 1)


def across(block):
    return flip(block, "head", 2)


def partner(block):
    return shift(block, "dp", lax.axis_size("dp") // 2)


def pick(array, index, axis=0):
    return lax.dynamic_index_in_dim(array, index, axis, keepdims=False)


def ordered(low, own, other, axis=0):
    return jnp.stack(
        (jnp.where(low == 0, own, other), jnp.where(low == 0, other, own)), axis=axis
    )


def mm(a, b):
    return jnp.dot(a, b, preferred_element_type=F32)


def mm_t(a, b):
    return lax.dot_general(a, b, (((1,), (1,)), ((), ())), preferred_element_type=F32)


def t_mm(a, b):
    return lax.dot_general(a, b, (((0,), (0,)), ((), ())), preferred_element_type=F32)


def norm_parts(rows):
    centered = rows - jnp.mean(rows, axis=-1, keepdims=True)
    inverse = lax.rsqrt(jnp.mean(centered * centered, axis=-1, keepdims=True) + EPSILON)
    return centered * inverse, inverse


def norm_back(incoming, normed, inverse, gain):
    scaled = incoming * gain
    return inverse * (
        scaled
        - jnp.mean(scaled, axis=-1, keepdims=True)
        - normed * jnp.mean(scaled * normed, axis=-1, keepdims=True)
    )


def gaussian_parts(t):
    k = 1.0 / (1.0 + (0.3275911 * 0.5**0.5) * jnp.abs(t))
    bell = jnp.exp(-0.5 * t * t)
    series = 0.5 * 1.061405429
    for a in (-1.453152027, 1.421413741, -0.284496736, 0.254829592):
        series = series * k + 0.5 * a
    tail = series * k * bell
    return jnp.where(t < 0.0, tail, 1.0 - tail), bell


def gather(piece, x_first):
    n = lax.axis_size("dp")
    if n != 8:
        mine = lax.all_gather(piece, "dp", axis=0, tiled=False)
        return jnp.stack((mine, across(mine)))
    index = lax.axis_index("dp")
    z, x = index // 2, index % 2
    column = jnp.zeros((4,) + piece.shape, piece.dtype)
    column = lax.dynamic_update_index_in_dim(column, piece, z, 0)
    for k in (1, 2, 3):
        column = lax.dynamic_update_index_in_dim(
            column, shift(piece, "dp", 2 * k), (z - k) % 4, 0
        )
    if x_first:
        plane = ordered(x, column, flip(column, "dp", 1), axis=1)
        both = jnp.stack((plane, across(plane)))
    else:
        both = jnp.stack((column, across(column)))
        both = ordered(x, both, flip(both, "dp", 1), axis=2)
    return both.reshape((2, 8) + piece.shape)


def reduce_scatter(terms, x_last):
    n = lax.axis_size("dp")
    if n != 8:
        total = terms[0].astype(F32) + across(terms[1].astype(BF16)).astype(F32)
        return lax.psum_scatter(total, "dp", scatter_dimension=0, tiled=False)
    index = lax.axis_index("dp")
    z, x = index // 2, index % 2
    terms = terms.reshape((2, 4, 2) + terms.shape[2:])
    if x_last:
        arrived = across(terms[1])
        plane = (terms[0].astype(F32) + arrived.astype(F32)).astype(BF16)
        arrived = flip(pick(plane, 1 - x, 1), "dp", 1)
        column = pick(plane, x, 1).astype(F32) + arrived.astype(F32)
    else:
        arrived = flip(pick(terms, 1 - x, 2), "dp", 1)
        both = (pick(terms, x, 2).astype(F32) + arrived.astype(F32)).astype(BF16)
        column = both[0].astype(F32) + across(both[1]).astype(F32)
    column = column.astype(BF16)
    total = pick(column, z).astype(F32)
    for k in (1, 2, 3):
        total = total + shift(pick(column, (z + k) % 4), "dp", 2 * k).astype(F32)
    return total


def lane_masks(scale):
    lane = lax.broadcasted_iota(jnp.int32, (1, 2 * HD), 1)
    first = jnp.where(lane < HD, 1.0, 0.0)
    return [(first * scale).astype(BF16), ((1.0 - first) * scale).astype(BF16)]


def rows_of(ref):
    a, b, w = ref.shape
    return ref[...].reshape(a * b, w)


def pair_lanes(halves):
    lane = lax.broadcasted_iota(jnp.int32, halves[0].shape, 1)
    return jnp.where(lane < HD, halves[0], halves[1])


def halves_joined(low, high):
    lane = lax.broadcasted_iota(jnp.int32, low.shape, 1)
    return jnp.where(lane < HD, low, pltpu.roll(high, HD, 1))


def highs_joined(low, high):
    lane = lax.broadcasted_iota(jnp.int32, low.shape, 1)
    return jnp.where(lane < HD, pltpu.roll(low, HD, 1), high)


def head_tiles(row_own, row_other):
    return (
        row_own[:, :128],
        row_other[:, :128],
        halves_joined(row_own[:, 128:256], row_other[:, 128:256]),
    )


def project(x, wa_ref, count):
    width = x.shape[1]
    tiles = []
    for p in range(2):
        w = wa_ref[p].reshape(width, wa_ref.shape[-1])
        out = mm(x, w[:, count[0] : count[1]])
        tiles.append([out[:, 128 * i : 128 * (i + 1)] for i in range(out.shape[1] // 128)])
    return tiles


def forward_own(b, x_ref, wa_ref, bias, q_ref, k_ref, v_ref):
    rows = x_ref.shape[2] * x_ref.shape[3] * 2
    x = x_ref[:, b].reshape(rows, x_ref.shape[-1])
    one, two = project(x, wa_ref, (0, 640))
    b_query, b_value = bias
    parts = (
        (q_ref, (one[0], two[0], halves_joined(one[3], two[3])), b_query),
        (k_ref, (one[1], two[1], highs_joined(one[3], two[3])), None),
        (v_ref, (one[2], two[2], halves_joined(one[4], two[4])), b_value),
    )
    for ref, tiles, added in parts:
        for t in range(3):
            tile = tiles[t] if added is None else tiles[t] + added[t]
            ref[:, b, :, 128 * t : 128 * (t + 1)] = tile.astype(BF16).reshape(2, rows // 2, 128)


def forward_attend(b, xp_ref, wa_ref, bias, swapped, q_ref, k_ref, v_ref, ku_ref, vu_ref, o_ref):
    rows = xp_ref.shape[2] * xp_ref.shape[3] * 2
    x = xp_ref[:, b].reshape(rows, xp_ref.shape[-1])
    one, two = project(x, wa_ref, (128, 640))
    far_keys = (one[0], two[0], highs_joined(one[2], two[2]))
    far_values = (one[1], two[1], halves_joined(one[3], two[3]))
    masks = lane_masks(SCALE)
    for t in range(3):
        lanes = slice(128 * t, 128 * (t + 1))

        def load(ref):
            return ref[:, b, :, lanes].reshape(rows, 128)

        take_far = swapped[t] > 0.5
        k = jnp.where(take_far, far_keys[t], load(k_ref).astype(F32)).astype(BF16)
        v = jnp.where(
            take_far, far_values[t] + bias[1][t], load(v_ref).astype(F32)
        ).astype(BF16)
        ku_ref[:, b, :, lanes] = k.reshape(2, rows // 2, 128)
        vu_ref[:, b, :, lanes] = v.reshape(2, rows // 2, 128)
        q = load(q_ref)
        outs = []
        for mask in masks:
            s = mm_t(q * mask, k)
            raised = jnp.exp(s - jnp.max(s, axis=-1, keepdims=True))
            total = jnp.sum(raised, axis=-1, keepdims=True)
            outs.append(mm(raised.astype(BF16), v) / total)
        o_ref[:, b, :, lanes] = pair_lanes(outs).astype(BF16).reshape(2, rows // 2, 128)


def forward_listed(b, member, row_ref, col_ref, q_ref, picks_ref, select_ref, qc_ref):
    slots = row_ref.shape[-1]
    quarter = q_ref.shape[2] // 2
    cap = slots // 4
    row, col = row_ref[b], col_ref[b]
    bits = quarter.bit_length() - 1
    run_row = lax.shift_right_arithmetic(row, bits)
    run_col = lax.shift_right_arithmetic(col, bits)
    before = lax.broadcasted_iota(jnp.int32, (slots, slots), 0) < lax.broadcasted_iota(
        jnp.int32, (slots, slots), 1
    )
    same = jnp.where(run_col == run_row, jnp.where(before, 1.0, 0.0), 0.0)
    rank = jnp.sum(same, axis=0, keepdims=True)
    line = lax.broadcasted_iota(jnp.int32, (slots, 1), 0)
    place = line // cap
    wanted_run = jnp.where(
        place == 0, member, jnp.where(place == 1, member + 2, jnp.where(place == 2, 1 - member, 3 - member))
    )
    wanted_rank = (line % cap).astype(F32)
    picks = jnp.where(run_row == wanted_run, jnp.where(rank == wanted_rank, 1.0, 0.0), 0.0).astype(BF16)
    lane = lax.broadcasted_iota(jnp.int32, (slots, quarter), 1)
    places = jnp.where(jnp.bitwise_and(col, quarter - 1) == lane, 1.0, 0.0).astype(BF16)
    select = mm(picks, places).astype(BF16)
    picks_ref[b] = picks
    select_ref[b] = select
    for s in range(2):
        for e in range(2):
            at = (2 * s + e) * cap
            rows = q_ref[s, b, quarter * e : quarter * (e + 1), :]
            qc_ref[s, b, cap * e : cap * (e + 1), :] = mm(select[at : at + cap], rows).astype(BF16)


def forward_kernel(comm, *refs):
    if comm:
        (
            a_ref, b_ref, t_ref, small_ref, row_ref, col_ref,
            wa_ref, wb_ref, x_ref, xt_ref, o_ref, k_ref, v_ref, ku_ref, vu_ref, qc_ref, picks_ref, select_ref, far_ref,
            xp_ref, q_ref, local_sem, send_sem, recv_sem,
        ) = refs
    else:
        (
            wa_ref, x_ref, xp_ref, small_ref, far_ref, row_ref, col_ref,
            xt_ref, o_ref, k_ref, v_ref, ku_ref, vu_ref, qc_ref, picks_ref, select_ref,
            q_ref,
        ) = refs
    blocks = x_ref.shape[1]
    head = lax.axis_index("head")
    member, pair = lax.rem(head, 2), lax.div(head, 2)

    def listed(b, carry):
        forward_listed(b, member, row_ref, col_ref, q_ref, picks_ref, select_ref, qc_ref)
        return carry

    def turned(i, carry):
        s, rest = lax.div(i, 2 * blocks), lax.rem(i, 2 * blocks)
        part = x_ref[s, lax.div(rest, 2), lax.rem(rest, 2)]
        quarter = part.shape[0]
        xt_ref[:, pl.ds(pl.multiple_of(i * quarter, quarter), quarter)] = part.T
        return carry

    def bias_of():
        own, other = small_ref[...], far_ref[...]
        rows = [head_tiles(own[i : i + 1], other[i : i + 1]) for i in range(3)]
        return (rows[0], rows[1]), rows[2]

    if not comm:
        bias, swapped = bias_of()
        lax.fori_loop(0, 4 * blocks, turned, 0)

        def own_block(b, carry):
            forward_own(b, x_ref, wa_ref, bias, q_ref, k_ref, v_ref)
            return carry

    if comm:
        index = lax.axis_index("dp")
        z, x = lax.div(index, 2), lax.rem(index, 2)
        x_peer = {"dp": 2 * z + 1 - x}
        y_peer = {"head": lax.rem(head + 2, 4)}
        sibling_peer = {"head": 2 * pair + 1 - member}
        z_peers = [{"dp": lax.rem(index + 2 * k, 8)} for k in (1, 2, 3)]
        barrier = pltpu.get_barrier_semaphore()
        for peer in [x_peer, y_peer, sibling_peer] + z_peers:
            pl.semaphore_signal(barrier, inc=1, device_id=peer, device_id_type=MESH)
        counter = [0]

        def local(src, dst, i):
            copy = pltpu.make_async_copy(src, dst, local_sem.at[i])
            copy.start()
            return copy

        def send(src, dst, peer):
            i = counter[0]
            counter[0] += 1
            copy = pltpu.make_async_remote_copy(
                src_ref=src,
                dst_ref=dst,
                send_sem=send_sem.at[i],
                recv_sem=recv_sem.at[i],
                device_id=peer,
                device_id_type=MESH,
            )
            copy.start()
            sent.append(copy)
            return copy

        def far_copy(b):
            return pltpu.make_async_remote_copy(
                src_ref=x_ref.at[0, b],
                dst_ref=xp_ref.at[0, b],
                send_sem=send_sem.at[15 + b],
                recv_sem=recv_sem.at[15 + b],
                device_id=z_peers[1],
                device_id_type=MESH,
            )

        def near_copy(b):
            return pltpu.make_async_remote_copy(
                src_ref=xp_ref.at[0, b],
                dst_ref=xp_ref.at[1, b],
                send_sem=send_sem.at[15 + blocks + b],
                recv_sem=recv_sem.at[15 + blocks + b],
                device_id=sibling_peer,
                device_id_type=MESH,
            )

        sent = []
        quarters = (member, member + 2, 1 - member, 3 - member)
        fills = [
            local(t_ref.at[pl.ds(blocks * pair, blocks), quarters[2 * s + e]], x_ref.at[s, :, e], 2 * s + e)
            for s in range(2)
            for e in range(2)
        ]
        fill_a = local(a_ref, wa_ref.at[0, z, x], 4)
        fill_b = local(b_ref, wb_ref.at[0, :, z, x], 5)
        pl.semaphore_wait(barrier, 6)
        a_z = [send(a_ref, wa_ref.at[0, z, x], peer) for peer in z_peers]
        far = send(small_ref, far_ref, y_peer)
        b_z = [send(b_ref, wb_ref.at[0, :, z, x], peer) for peer in z_peers]
        for fill in fills:
            fill.wait()
        for b in range(blocks):
            far_copy(b).start()
        lax.fori_loop(0, 4 * blocks, turned, 0)
        half = a_ref.shape[0] // 2
        up, low = pl.ds(0, half), pl.ds(half, half)
        fill_a.wait()
        for copy in a_z:
            copy.wait_recv()
        a_x = send(wa_ref.at[0, :, x, up], wa_ref.at[0, :, x, up], x_peer)
        a_y = send(wa_ref.at[0, :, x, low], wa_ref.at[1, :, x, low], y_peer)
        a_x.wait_recv()
        a_xy = send(wa_ref.at[0, :, :, up], wa_ref.at[1, :, :, up], y_peer)
        a_y.wait_recv()
        a_yx = send(wa_ref.at[:, :, x, low], wa_ref.at[:, :, x, low], x_peer)
        fill_b.wait()
        for copy in b_z:
            copy.wait_recv()
        b_x = send(wb_ref.at[0, 0, :, x], wb_ref.at[0, 0, :, x], x_peer)
        b_y = send(wb_ref.at[0, 1, :, x], wb_ref.at[1, 1, :, x], y_peer)
        far.wait_recv()
        a_xy.wait_recv()
        a_yx.wait_recv()
        bias, swapped = bias_of()

        def own_block(b, carry):
            forward_own(b, x_ref, wa_ref, bias, q_ref, k_ref, v_ref)
            return carry

    lax.fori_loop(0, blocks, own_block, 0)
    lax.fori_loop(0, blocks, listed, 0)
    if comm:
        b_x.wait_recv()
        b_xy = send(wb_ref.at[0, 0], wb_ref.at[1, 0], y_peer)
        b_y.wait_recv()
        b_yx = send(wb_ref.at[:, 1, :, x], wb_ref.at[:, 1, :, x], x_peer)
        def attend_block(b, carry):
            far_copy(b).wait_recv()
            near = near_copy(b)
            near.start()
            near.wait_recv()
            forward_attend(b, xp_ref, wa_ref, bias, swapped, q_ref, k_ref, v_ref, ku_ref, vu_ref, o_ref)
            return carry

        lax.fori_loop(0, blocks, attend_block, 0)
        b_xy.wait_recv()
        b_yx.wait_recv()
        for copy in sent:
            copy.wait_send()
        for b in range(blocks):
            far_copy(b).wait_send()
            near_copy(b).wait_send()
    else:

        def attend_block(b, carry):
            forward_attend(b, xp_ref, wa_ref, bias, swapped, q_ref, k_ref, v_ref, ku_ref, vu_ref, o_ref)
            return carry

        lax.fori_loop(0, blocks, attend_block, 0)


def vmem_spec():
    return pl.BlockSpec(memory_space=pltpu.VMEM)


def any_spec():
    return pl.BlockSpec(memory_space=pl.ANY)


def forward(tokens, piece_a, piece_b, small, listed, member, pair):
    n = lax.axis_size("dp")
    block_count, block_rows, width = tokens.shape
    blocks, quarter = block_count // 2, block_rows // 4
    slots = listed.shape[1]
    cap = slots // 4
    lanes = 6 * HD
    tokens = tokens.reshape(block_count, 4, quarter, width)
    row, col = listed[:, None, :], listed[:, :, None]
    rows_shape = (2, blocks, 2, quarter, width)

    def out(*shape, dtype=BF16):
        return jax.ShapeDtypeStruct(shape, dtype)

    dense = (2, blocks, 2 * quarter, lanes)
    tail = [out(width, 2 * blocks * 2 * quarter)] + [out(*dense)] * 5 + [
        out(2, blocks, 2 * cap, lanes),
        out(blocks, slots, slots),
        out(blocks, slots, quarter),
    ]
    params = dict(vmem_limit_bytes=60 * 2**20, has_side_effects=True)
    if n == 8:
        shapes = [
            out(2, 4, 2, *piece_a.shape),
            out(2, 2, 4, 2, *piece_b.shape[1:]),
            out(*rows_shape),
            *tail,
            out(*small.shape, dtype=F32),
        ]
        specs = [vmem_spec()] * len(shapes)
        specs[1] = any_spec()
        results = pl.pallas_call(
            functools.partial(forward_kernel, True),
            out_shape=shapes,
            in_specs=[vmem_spec(), vmem_spec(), any_spec()] + [vmem_spec()] * 3,
            out_specs=specs,
            scratch_shapes=[
                pltpu.VMEM(rows_shape, BF16),
                pltpu.VMEM(dense, BF16),
                pltpu.SemaphoreType.DMA((6,)),
                pltpu.SemaphoreType.DMA((15 + 2 * blocks,)),
                pltpu.SemaphoreType.DMA((15 + 2 * blocks,)),
            ],
            compiler_params=pltpu.CompilerParams(collective_id=1, **params),
        )(piece_a, piece_b, tokens, small, row, col)
        w_attn, w_feed, rows, *rest, far = results
    else:
        mine = pick(tokens.reshape(2, blocks, 2, 2, quarter, width), pair)
        rows = jnp.stack((pick(mine, member, 2), pick(mine, 1 - member, 2)))
        w_attn = gather(piece_a, True)
        w_feed = jnp.stack([gather(piece_b[i], True) for i in range(2)], axis=1)
        far = across(small)
        shapes = tail
        rest = pl.pallas_call(
            functools.partial(forward_kernel, False),
            out_shape=shapes,
            in_specs=[vmem_spec()] * 7,
            out_specs=[vmem_spec()] * len(shapes),
            scratch_shapes=[pltpu.VMEM(dense, BF16)],
            compiler_params=pltpu.CompilerParams(vmem_limit_bytes=60 * 2**20),
        )(w_attn.reshape(2, width, -1), rows, partner(rows), small, far, row, col)
    w_attn = w_attn.reshape(2, width, -1)
    w_feed = w_feed.reshape(2, 2, width, -1)
    return (w_attn, w_feed, rows, *rest, far)


def back_queries(b, qc_ref, g_ref, ku_ref, vu_ref, select_ref, o_ref, dt_ref, oc_ref, total_ref):
    rows = ku_ref.shape[2] * 2
    slots = qc_ref.shape[2] * 2
    cap = slots // 4
    quarter = rows // 4
    select = select_ref[b]
    tiles = []
    for t in range(3):
        lanes = slice(128 * t, 128 * (t + 1))
        q = qc_ref[:, b, :, lanes].reshape(slots, 128)
        g = g_ref[:, b, :, lanes].reshape(slots, 128)
        k = ku_ref[:, b, :, lanes].reshape(rows, 128)
        v = vu_ref[:, b, :, lanes].reshape(rows, 128)
        outs = []
        for mask, one in zip(lane_masks(SCALE), lane_masks(1.0)):
            s = mm_t(q * mask, k)
            raised = jnp.exp(s - jnp.max(s, axis=-1, keepdims=True))
            probs = raised / jnp.sum(raised, axis=-1, keepdims=True)
            d_probs = mm_t(g * one, v)
            inner = jnp.sum(d_probs * probs, axis=-1, keepdims=True)
            d_scores = (probs * (d_probs - inner)).astype(BF16)
            outs.append(mm(d_scores, k) * SCALE)
        tile = pair_lanes(outs).astype(BF16)
        total_ref[0:1, lanes] += jnp.sum(tile.astype(F32), axis=0, keepdims=True)
        tiles.append(tile)
    for s in range(2):
        for e in range(2):
            at = (2 * s + e) * cap
            chosen = select[at : at + cap]
            own = slice(quarter * e, quarter * (e + 1))
            dense = [t_mm(chosen, tile[at : at + cap]) for tile in tiles]
            dt_ref[0, s, b, own, 0:128] = dense[0].astype(BF16)
            dt_ref[1, s, b, own, 0:128] = dense[1].astype(BF16)
            lane = lax.broadcasted_iota(jnp.int32, dense[2].shape, 1)
            for p in range(2):
                last = dense[2] if p == 0 else pltpu.roll(dense[2], HD, 1)
                dt_ref[p, s, b, own, 384:512] = jnp.where(lane < HD, last, 0.0).astype(BF16)
            rows_o = mm(chosen, o_ref[s, b, own, :])
            at_o = slice(cap * e, cap * (e + 1))
            lane = lax.broadcasted_iota(jnp.int32, (cap, 128), 1)
            for p in range(2):
                oc_ref[p, s, b, at_o, 128:256] = rows_o[:, 128 * p : 128 * (p + 1)].astype(BF16)
                last = rows_o[:, 256:384] if p == 1 else pltpu.roll(rows_o[:, 256:384], HD, 1)
                oc_ref[p, s, b, at_o, 0:128] = jnp.where(lane < HD, 0.0, last).astype(BF16)


def back_keys(b, swapped, qc_ref, g_ref, qf_ref, gf_ref, k_ref, v_ref, dt_ref, total_ref):
    rows = k_ref.shape[2] * 2
    slots = qc_ref.shape[2] * 2
    for t in range(3):
        lanes = slice(128 * t, 128 * (t + 1))
        take_far = swapped[t] > 0.5

        def chosen(near, far):
            near = near[:, b, :, lanes].reshape(slots, 128).astype(F32)
            far = far[:, b, :, lanes].reshape(slots, 128).astype(F32)
            return jnp.where(take_far, far, near).astype(BF16)

        q, g = chosen(qc_ref, qf_ref), chosen(g_ref, gf_ref)
        k = k_ref[:, b, :, lanes].reshape(rows, 128)
        v = v_ref[:, b, :, lanes].reshape(rows, 128)
        d_keys, d_values = [], []
        for mask, one in zip(lane_masks(SCALE), lane_masks(1.0)):
            s = mm_t(k, q * mask)
            raised = jnp.exp(s - jnp.max(s, axis=0, keepdims=True))
            probs = raised / jnp.sum(raised, axis=0, keepdims=True)
            d_probs = mm_t(v, g * one)
            inner = jnp.sum(d_probs * probs, axis=0, keepdims=True)
            d_scores = (probs * (d_probs - inner)).astype(BF16)
            d_keys.append(mm(d_scores, q) * SCALE)
            d_values.append(mm(probs.astype(BF16), g))
        dk, dv = pair_lanes(d_keys), pair_lanes(d_values)
        total_ref[1:2, lanes] += jnp.sum(dv.astype(BF16).astype(F32), axis=0, keepdims=True)
        half = (2, rows // 2, 128)
        if t < 2:
            dt_ref[t, :, b, :, 128:256] = dk.astype(BF16).reshape(half)
            dt_ref[t, :, b, :, 256:384] = dv.astype(BF16).reshape(half)
        else:
            lane = lax.broadcasted_iota(jnp.int32, dk.shape, 1)
            for p in range(2):
                last = pltpu.roll(dk, HD, 1) if p == 0 else dk
                before = dt_ref[p, :, b, :, 384:512].reshape(rows, 128).astype(F32)
                dt_ref[p, :, b, :, 384:512] = (
                    jnp.where(lane < HD, before, last).astype(BF16).reshape(half)
                )
                last = dv if p == 0 else pltpu.roll(dv, HD, 1)
                dt_ref[p, :, b, :, 512:640] = (
                    jnp.where(lane < HD, last, 0.0).astype(BF16).reshape(half)
                )


def back_weights(p, xt_ref, dt_ref, db_ref, oc_ref, ga_ref):
    width = xt_ref.shape[0]
    shape = ga_ref.shape[1:-1] + (128,)
    listed = db_ref.shape[0] * db_ref.shape[1] * db_ref.shape[2]
    d_branch = db_ref[...].reshape(listed, width)
    outs = mm(xt_ref[...], dt_ref[p].reshape(xt_ref.shape[1], 640))
    extra = t_mm(d_branch, oc_ref[p].reshape(listed, 256))
    for i in range(6):
        if i < 4:
            tile = outs[:, 128 * i : 128 * (i + 1)]
        elif i == 4:
            tile = outs[:, 512:640] + extra[:, 0:128]
        else:
            tile = extra[:, 128:256]
        ga_ref[p, ..., 128 * i : 128 * (i + 1)] = tile.astype(BF16).reshape(shape)


def back_rows(s, b, wa_ref, dt_ref):
    rows, width = dt_ref.shape[3], wa_ref.shape[-1]
    out = 0.0
    for p in range(2):
        w = wa_ref[p].reshape(-1, wa_ref.shape[-1])
        out = out + mm_t(dt_ref[p, s, b], w[:, 0:640])
    return out


def bias_totals(member, pair, total_ref):
    lane = lax.broadcasted_iota(jnp.int32, (1, 128), 1)
    line = lax.broadcasted_iota(jnp.int32, (8, 128), 0)
    first = jnp.zeros((8, 128), F32)
    second = jnp.zeros((8, 128), F32)
    for i in range(2):
        last = total_ref[i : i + 1, 256:384]
        for p in range(2):
            place = 4 * i + 2 * (pair if p == 0 else 1 - pair) + member
            tile = total_ref[i : i + 1, 128 * p : 128 * (p + 1)]
            third = last if p == 0 else pltpu.roll(last, HD, 1)
            first = first + jnp.where(line == place, tile, 0.0)
            second = second + jnp.where(line == place, jnp.where(lane < HD, third, 0.0), 0.0)
    return first, second


def back_kernel(comm, *refs):
    if comm:
        (
            gb_ref, qc_ref, g_ref, k_ref, v_ref, ku_ref, vu_ref, o_ref, xt_ref, wa_ref,
            select_ref, small_ref, far_ref, db_ref, df_ref, vec_ref,
            gx_ref, sa_ref, sb_ref, sum_ref,
            dt_ref, oc_ref, ga_ref, total_ref, qf_ref, gf_ref, term_ref, near_ref, rows_ref,
            b1_up, b1_low, b2, b3, a1_up, a1_low, a2, a3, vec1, vec4,
            local_sem, send_sem, recv_sem,
        ) = refs
    else:
        (
            qf_ref, gf_ref, qc_ref, g_ref, k_ref, v_ref, ku_ref, vu_ref, o_ref, xt_ref, wa_ref,
            select_ref, small_ref, far_ref, db_ref,
            ga_ref, term_ref, both_ref,
            dt_ref, oc_ref, total_ref,
        ) = refs
    blocks = k_ref.shape[1]
    head = lax.axis_index("head")
    member, pair = lax.rem(head, 2), lax.div(head, 2)
    swapped = head_tiles(small_ref[2:3], far_ref[2:3])
    total_ref[...] = jnp.zeros_like(total_ref)

    def queries(b, carry):
        back_queries(b, qc_ref, g_ref, ku_ref, vu_ref, select_ref, o_ref, dt_ref, oc_ref, total_ref)
        return carry

    def keys(b, carry):
        back_keys(b, swapped, qc_ref, g_ref, qf_ref, gf_ref, k_ref, v_ref, dt_ref, total_ref)
        return carry

    def weights(p, carry):
        back_weights(p, xt_ref, dt_ref, db_ref, oc_ref, ga_ref)
        return carry

    if not comm:
        lax.fori_loop(0, blocks, queries, 0)
        lax.fori_loop(0, blocks, keys, 0)
        lax.fori_loop(0, 2, weights, 0)

        def rows(i, carry):
            s, b = lax.div(i, blocks), lax.rem(i, blocks)
            term_ref[s, b] = back_rows(s, b, wa_ref, dt_ref)
            return carry

        lax.fori_loop(0, 2 * blocks, rows, 0)
        both_ref[0:8], both_ref[8:16] = bias_totals(member, pair, total_ref)
        return

    index = lax.axis_index("dp")
    z, x = lax.div(index, 2), lax.rem(index, 2)
    x_peer = {"dp": 2 * z + 1 - x}
    y_peer = {"head": lax.rem(head + 2, 4)}
    sibling_peer = {"head": 2 * pair + 1 - member}
    z_peers = [{"dp": lax.rem(index + 2 * k, 8)} for k in (1, 2, 3)]
    z_to = [lax.rem(z + k, 4) for k in (1, 2, 3)]
    barrier = pltpu.get_barrier_semaphore()
    for peer in [x_peer, y_peer, sibling_peer] + z_peers:
        pl.semaphore_signal(barrier, inc=1, device_id=peer, device_id_type=MESH)
    pl.semaphore_wait(barrier, 6)
    sent = []

    def send(src, dst, peer):
        i = len(sent)
        copy = pltpu.make_async_remote_copy(
            src_ref=src,
            dst_ref=dst,
            send_sem=send_sem.at[i],
            recv_sem=recv_sem.at[i],
            device_id=peer,
            device_id_type=MESH,
        )
        copy.start()
        sent.append(copy)
        return copy

    def plus(a, b):
        return (a.astype(F32) + b.astype(F32)).astype(BF16)

    def first_phase(up_other, low_other, up_buffer, low_buffer):
        return send(up_other, up_buffer, y_peer), send(low_other, low_buffer, x_peer)

    far_g = send(g_ref, gf_ref, z_peers[1])
    far_q = send(qc_ref, qf_ref, z_peers[1])
    b_up = send(gb_ref.at[1, 0], b1_up, y_peer)
    b_low = send(gb_ref.at[:, 1, :, 1 - x], b1_low, x_peer)
    lax.fori_loop(0, blocks, queries, 0)
    far_g.wait_recv()
    far_q.wait_recv()
    lax.fori_loop(0, blocks, keys, 0)

    vec_rows = vec_ref.shape[0]
    vec1[0, 0:vec_rows] = vec_ref[...]
    vec1[0, vec_rows : vec_rows + 8], vec1[0, vec_rows + 8 : vec_rows + 16] = bias_totals(
        member, pair, total_ref
    )
    v_sib = send(vec1.at[0], vec1.at[1], sibling_peer)

    halves = gb_ref.shape[2]

    def add_up(i, carry):
        b1_up[i] = plus(b1_up[i], gb_ref[0, 0, i])
        return carry

    def add_low(i, carry):
        for p in range(2):
            b1_low[p, i] = plus(b1_low[p, i], gb_ref[p, 1, i, x])
        return carry

    b_up.wait_recv()
    lax.fori_loop(0, halves, add_up, 0)
    b_up = send(b1_up.at[:, 1 - x], b2.at[0], x_peer)
    b_low.wait_recv()
    lax.fori_loop(0, halves, add_low, 0)
    b_low = send(b1_low.at[1], b2.at[1], y_peer)
    v_sib.wait_recv()
    vec1[2] = vec1[0] + vec1[1]
    v_y = send(vec1.at[2], vec1.at[3], y_peer)

    lax.fori_loop(0, 2, weights, 0)
    half = ga_ref.shape[3] // 2
    up, low = slice(0, half), slice(half, 2 * half)
    a_up = send(ga_ref.at[1, :, :, pl.ds(0, half)], a1_up, y_peer)
    a_low = send(ga_ref.at[:, :, 1 - x, pl.ds(half, half)], a1_low, x_peer)

    def rows_other(b, carry):
        term_ref[b] = back_rows(1, b, wa_ref, dt_ref).astype(BF16)
        return carry

    lax.fori_loop(0, blocks, rows_other, 0)
    term = send(term_ref, near_ref, sibling_peer)

    b_up.wait_recv()
    b_low.wait_recv()

    def add_second(i, carry):
        b2[0, i] = plus(b2[0, i], b1_up[i, x])
        b2[1, i] = plus(b2[1, i], b1_low[0, i])
        return carry

    lax.fori_loop(0, halves, add_second, 0)
    b_z = [send(b2.at[:, to], b3.at[k], peer) for k, (to, peer) in enumerate(zip(z_to, z_peers))]
    v_y.wait_recv()
    vec1[4] = vec1[2] + vec1[3]
    v_x = send(vec1.at[4], vec1.at[5], x_peer)

    a_up.wait_recv()

    def a_add_up(i, carry):
        a1_up[i] = plus(a1_up[i], ga_ref[0, i, :, up])
        return carry

    lax.fori_loop(0, halves, a_add_up, 0)
    a_up = send(a1_up.at[:, 1 - x], a2.at[0], x_peer)
    a_low.wait_recv()

    def a_add_low(i, carry):
        for p in range(2):
            a1_low[p, i] = plus(a1_low[p, i], ga_ref[p, i, x, low])
        return carry

    lax.fori_loop(0, halves, a_add_low, 0)
    a_low = send(a1_low.at[1], a2.at[1], y_peer)

    cap = df_ref.shape[1] // 2
    quarter = rows_ref.shape[2]
    term.wait_recv()

    def rows_own(b, carry):
        own = back_rows(0, b, wa_ref, dt_ref) + near_ref[b].astype(F32)
        for e in range(2):
            first = df_ref[b, cap * e : cap * (e + 1), :]
            high = first.astype(BF16)
            rest = (first - high.astype(F32)).astype(BF16)
            chosen = select_ref[b, cap * e : cap * (e + 1), :]
            spread = t_mm(chosen, high) + t_mm(chosen, rest)
            rows_ref[e, b] = (own[quarter * e : quarter * (e + 1)] + spread).astype(BF16)
        return carry

    lax.fori_loop(0, blocks, rows_own, 0)
    moved = send(rows_ref.at[1 - pair], gx_ref.at[pair], y_peer)
    kept = pltpu.make_async_copy(rows_ref.at[pair], gx_ref.at[pair], local_sem.at[0])
    kept.start()
    v_x.wait_recv()
    vec1[6] = vec1[4] + vec1[5]
    own_vec = pltpu.make_async_copy(vec1.at[6], vec4.at[z], local_sem.at[1])
    own_vec.start()
    v_z = [send(vec1.at[6], vec4.at[z], peer) for peer in z_peers]

    a_up.wait_recv()
    a_low.wait_recv()

    def a_add_second(i, carry):
        a2[0, i] = plus(a2[0, i], a1_up[i, x])
        a2[1, i] = plus(a2[1, i], a1_low[0, i])
        return carry

    lax.fori_loop(0, halves, a_add_second, 0)
    a_z = [send(a2.at[:, to], a3.at[k], peer) for k, (to, peer) in enumerate(zip(z_to, z_peers))]

    for copy in b_z:
        copy.wait_recv()
    for t in range(2):
        total = b2[t, z].astype(F32)
        for k in range(3):
            total = total + b3[k, t].astype(F32)
        sb_ref[t] = total
    own_vec.wait()
    for copy in v_z:
        copy.wait_recv()
    sum_ref[...] = (vec4[0] + vec4[1]) + (vec4[2] + vec4[3])
    for copy in a_z:
        copy.wait_recv()
    for t, part in enumerate((up, low)):
        total = a2[t, z].astype(F32)
        for k in range(3):
            total = total + a3[k, t].astype(F32)
        sa_ref[part] = total
    kept.wait()
    moved.wait_recv()
    for copy in sent:
        copy.wait_send()


def backward(gb, q_compact, d_attention, keys, values, keys_used, values_used, attention, rows_t, w_attn, select, small, far, d_branch, d_first, vectors):
    n = lax.axis_size("dp")
    _, blocks, block_half, lanes = keys.shape
    width = rows_t.shape[0]
    quarter = block_half // 2
    piece = width // n
    slots = select.shape[1]
    vec_rows = vectors.shape[0] + 16

    def out(*shape, dtype=BF16):
        return jax.ShapeDtypeStruct(shape, dtype)

    compact = (2, blocks, slots // 2, lanes)
    scratch = [
        pltpu.VMEM((2, 2, blocks, block_half, 640), BF16),
        pltpu.VMEM((2, 2, blocks, slots // 2, 256), BF16),
    ]
    shared = (q_compact, d_attention, keys, values, keys_used, values_used, attention, rows_t, w_attn, select, small, far, d_branch)
    if n == 8:
        half = piece // 2
        return pl.pallas_call(
            functools.partial(back_kernel, True),
            out_shape=[
                out(2, blocks, quarter, width),
                out(piece, width, dtype=F32),
                out(2, piece, width, dtype=F32),
                out(vec_rows, 128, dtype=F32),
            ],
            in_specs=[vmem_spec()] * 16,
            out_specs=[vmem_spec()] * 4,
            scratch_shapes=scratch
            + [
                pltpu.VMEM((2, 4, 2, piece, width), BF16),
                pltpu.VMEM((8, lanes), F32),
                pltpu.VMEM(compact, BF16),
                pltpu.VMEM(compact, BF16),
                pltpu.VMEM((blocks, block_half, width), BF16),
                pltpu.VMEM((blocks, block_half, width), BF16),
                pltpu.VMEM((2, blocks, quarter, width), BF16),
                pltpu.VMEM((4, 2, piece, width), BF16),
                pltpu.VMEM((2, 4, piece, width), BF16),
                pltpu.VMEM((2, 4, piece, width), BF16),
                pltpu.VMEM((3, 2, piece, width), BF16),
                pltpu.VMEM((4, 2, half, width), BF16),
                pltpu.VMEM((2, 4, half, width), BF16),
                pltpu.VMEM((2, 4, half, width), BF16),
                pltpu.VMEM((3, 2, half, width), BF16),
                pltpu.VMEM((7, vec_rows, 128), F32),
                pltpu.VMEM((4, vec_rows, 128), F32),
                pltpu.SemaphoreType.DMA((2,)),
                pltpu.SemaphoreType.DMA((24,)),
                pltpu.SemaphoreType.DMA((24,)),
            ],
            compiler_params=pltpu.CompilerParams(
                collective_id=2, vmem_limit_bytes=62 * 2**20, has_side_effects=True
            ),
        )(gb.reshape(2, 2, 4, 2, piece, width), *shared, d_first, vectors)
    ga, term, both = pl.pallas_call(
        functools.partial(back_kernel, False),
        out_shape=[
            out(2, 1, 1, width, width),
            out(2, blocks, block_half, width, dtype=F32),
            out(16, 128, dtype=F32),
        ],
        in_specs=[vmem_spec()] * 15,
        out_specs=[vmem_spec()] * 3,
        scratch_shapes=scratch + [pltpu.VMEM((8, lanes), F32)],
        compiler_params=pltpu.CompilerParams(vmem_limit_bytes=62 * 2**20),
    )(partner(q_compact), partner(d_attention), *shared)
    pair = lax.axis_index("head") // 2
    cap = slots // 4
    chosen = select[:, : 2 * cap].reshape(blocks, 2, cap, quarter).astype(F32)
    spread = jnp.einsum(
        "bekr,bekw->berw",
        chosen,
        d_first.reshape(blocks, 2, cap, width),
        precision=lax.Precision.HIGHEST,
    )
    own = term[0].reshape(spread.shape) + sibling(term[1].astype(BF16)).astype(F32).reshape(spread.shape)
    own = (own + spread).astype(BF16)
    grad_x = ordered(pair, pick(own, pair, 1), across(pick(own, 1 - pair, 1)))
    pieces = (2, n, piece, width)
    s_attn = reduce_scatter(ga.reshape(pieces), True)
    s_feed = jnp.stack([reduce_scatter(gb[:, i].reshape(pieces), True) for i in range(2)])
    return grad_x, s_attn, s_feed, lax.psum(jnp.concatenate((vectors, both)), ("dp", "head"))


def per_device(
    tokens,
    query_weight,
    query_bias,
    key_weight,
    value_weight,
    value_bias,
    out_weight,
    out_bias,
    first_gain,
    first_shift,
    up_weight,
    up_bias,
    down_weight,
    down_bias,
    second_gain,
    second_shift,
    block_order,
    masked_rows,
    out_grad,
):
    block_count, block_rows, width = tokens.shape
    quarter = block_rows // 4
    slots = masked_rows.shape[1]
    cap = slots // 4
    blocks = block_count // 2
    piece_rows = query_weight.shape[0]
    local = query_weight.shape[1]
    columns = 2 * local
    hidden_piece = up_weight.shape[1]
    head = lax.axis_index("head")
    c, p = head % 2, head // 2

    out_t = out_weight.T
    first, last = slice(0, 2 * HD), slice(2 * HD, 3 * HD)
    piece = jnp.concatenate(
        (
            query_weight[:, first],
            key_weight[:, first],
            value_weight[:, first],
            query_weight[:, last],
            key_weight[:, last],
            value_weight[:, last],
            out_t[:, last],
            out_t[:, first],
        ),
        axis=1,
    )
    half = piece_rows // 2

    def line(vector, size):
        return jnp.pad(vector, (0, size - vector.shape[0]))

    small = jnp.stack(
        [
            line(row, hidden_piece)
            for row in (
                query_bias,
                value_bias,
                jnp.repeat(block_order.astype(F32), HD),
                up_bias,
            )
        ]
        + [jnp.zeros((hidden_piece,), F32)] * 4
    )
    listed = pick(masked_rows.reshape(2, blocks, slots), p)
    (
        w_attn, w_feed, x_rows, rows_t, attention, keys, values, keys_used, values_used, q_compact, picks_b, select_b, small_far,
    ) = forward(tokens, piece, jnp.stack((up_weight, down_weight.T)), small, listed, c, p)

    def tiles(i, second, j):
        second = HD * second

        return jnp.concatenate(
            (
                w_attn[0][:, 128 * i : 128 * i + 128],
                w_attn[1][:, 128 * i : 128 * i + 128],
                w_attn[0][:, 128 * j + second : 128 * j + second + HD],
                w_attn[1][:, 128 * j + second : 128 * j + second + HD],
            ),
            axis=1,
        )

    w_out_t = tiles(5, 1, 4)
    w_out_other = sibling(w_out_t)
    w_up, w_down = w_feed[:, 0], w_feed[:, 1]
    b_up = jnp.stack((up_bias, small_far[3]))
    x_flat = x_rows.reshape(-1, width)
    own_count = x_flat.shape[0] // 2
    attn_shape = (2, blocks, 2 * quarter, columns)
    compact_shape = (2, blocks, 2 * cap, columns)
    picks = jnp.transpose(picks_b.reshape(blocks, 2, 2, cap, slots), (1, 0, 2, 3, 4))
    select = jnp.transpose(
        select_b.reshape(blocks, 2, 2, cap, quarter), (1, 0, 2, 3, 4)
    ).reshape(-1, cap, quarter)
    runs_own = 2 * blocks

    def compact(rows, which=slice(None), **kw):
        source = select[which]
        out = jnp.einsum(
            "ukr,urw->ukw",
            source.astype(rows.dtype),
            rows.reshape(source.shape[0], quarter, -1),
            preferred_element_type=F32,
            **kw,
        )
        return out.reshape(-1, rows.shape[-1])

    def spread(rows, which=slice(None), **kw):
        source = select[which]
        out = jnp.einsum(
            "ukr,ukw->urw",
            source.astype(rows.dtype),
            rows.reshape(source.shape[0], cap, -1),
            preferred_element_type=F32,
            **kw,
        )
        return out.reshape(-1, rows.shape[-1])

    own_runs, other_runs = slice(0, runs_own), slice(runs_own, None)
    exact = {"precision": lax.Precision.HIGHEST}
    grads_in = pick(out_grad.reshape(2, blocks, slots, width), p)
    grad_y = jnp.einsum(
        "beki,biw->bekw", picks[0], grads_in, preferred_element_type=F32
    ).reshape(-1, width)

    attn_other = sibling(attention[1]).reshape(own_count, columns)
    branch = mm_t(attention[0].reshape(own_count, columns), w_out_t) + mm_t(
        attn_other, w_out_other
    )
    sum_one = x_flat[:own_count].astype(F32) + branch + out_bias
    hidden = norm_parts(sum_one)[0] * first_gain + first_shift
    hidden_low = hidden.astype(BF16)
    hidden_other = sibling(hidden_low)
    hidden_all = jnp.concatenate((hidden_low, hidden_other))

    def feed(i):
        pre = mm(hidden_all, w_up[i]) + b_up[i]
        activated = (pre * gaussian_parts(pre)[0]).astype(BF16)
        return mm_t(activated, w_down[i])

    feed_term = feed(0) + feed(1)
    feed_out = (
        feed_term[:own_count]
        + sibling(feed_term[own_count:].astype(BF16)).astype(F32)
        + down_bias
    )
    sum_two = hidden + feed_out
    out_rows = (norm_parts(sum_two)[0] * second_gain + second_shift).astype(BF16)

    def to_output(rows):
        rows = rows.reshape(blocks, 2, quarter, width)
        kept = pick(rows, p, 1)
        moved = across(pick(rows, 1 - p, 1))
        return ordered(p, kept, moved).reshape(block_count, quarter, width)

    out_y = to_output(out_rows)

    one_c = compact(sum_one, own_runs, **exact)
    two_c = compact(sum_two, own_runs, **exact)
    normed_two, inverse_two = norm_parts(two_c)
    normed_one, inverse_one = norm_parts(one_c)
    hidden_c = (normed_one * first_gain + first_shift).astype(BF16)
    d_second = norm_back(grad_y, normed_two, inverse_two, second_gain)
    g_second_gain = jnp.sum(grad_y * normed_two, axis=0)
    g_second_shift = jnp.sum(grad_y, axis=0)
    d_feed = d_second.astype(BF16)
    g_down_bias = jnp.sum(d_feed.astype(F32), axis=0)
    d_feed_all = jnp.concatenate((d_feed, sibling(d_feed)))
    hidden_c_all = jnp.concatenate(
        (hidden_c, compact(hidden_other, other_runs).astype(BF16))
    )
    g_up, g_down, g_up_bias, d_hidden_term = [], [], [], 0.0
    for i in range(2):
        pre = mm(hidden_c_all, w_up[i]) + b_up[i]
        cdf, bell = gaussian_parts(pre)
        density = bell * (0.5 / jnp.pi) ** 0.5
        activated = (pre * cdf).astype(BF16)
        d_pre = (mm(d_feed_all, w_down[i]) * (cdf + pre * density)).astype(BF16)
        g_up_bias.append(jnp.sum(d_pre.astype(F32), axis=0))
        g_up.append(t_mm(hidden_c_all, d_pre).astype(BF16))
        g_down.append(t_mm(d_feed_all, activated).astype(BF16))
        d_hidden_term = d_hidden_term + mm_t(d_pre, w_up[i])
    compact_own = d_feed.shape[0]
    d_hidden = (
        d_second
        + d_hidden_term[:compact_own]
        + sibling(d_hidden_term[compact_own:].astype(BF16)).astype(F32)
    )
    gb = jnp.stack((jnp.stack(g_up), jnp.stack(g_down)), axis=1)
    g_first_gain = jnp.sum(d_hidden * normed_one, axis=0)
    g_first_shift = jnp.sum(d_hidden, axis=0)
    d_first = norm_back(d_hidden, normed_one, inverse_one, first_gain)
    d_branch = d_first.astype(BF16)
    g_out_bias = jnp.sum(d_branch.astype(F32), axis=0)
    d_branch_all = jnp.concatenate((d_branch, sibling(d_branch)))
    d_attention = mm(d_branch_all, w_out_t).astype(BF16).reshape(compact_shape)

    def widen(own_first):
        by_p = ordered(p, own_first[0], own_first[1])
        zero = jnp.zeros_like(by_p)
        return jnp.where(
            c == 0,
            jnp.stack((by_p, zero), axis=1),
            jnp.stack((zero, by_p), axis=1),
        ).reshape(-1)

    vectors = [
        g_out_bias,
        g_first_gain,
        g_first_shift,
        g_down_bias,
        g_second_gain,
        g_second_shift,
        widen(jnp.stack(g_up_bias)),
    ]
    flat = jnp.concatenate(vectors)
    flat = jnp.pad(flat, (0, -flat.shape[0] % 1024)).reshape(-1, 128)
    grad_x, s_attn, s_feed, summed = backward(
        gb, q_compact, d_attention, keys, values, keys_used, values_used, attention, rows_t, w_attn, select_b,
        small, small_far, d_branch_all.reshape(2, blocks, 2 * cap, width), d_first.reshape(blocks, 2 * cap, width), flat,
    )
    grad_x = grad_x.reshape(block_count, quarter, width)
    whole = summed[: flat.shape[0]].reshape(-1)
    ends, start = [], 0
    for vector in vectors:
        ends.append(whole[start : start + vector.shape[0]])
        start += vector.shape[0]
    v_out_bias, v_first_gain, v_first_shift, v_down_bias, v_second_gain, v_second_shift, v_up_bias = ends
    last = summed[flat.shape[0] :].reshape(2, 2, 4, 128)
    v_query_bias, v_value_bias = (
        jnp.concatenate((last[0, i], last[1, i, :, :HD]), axis=-1).reshape(-1)
        for i in range(2)
    )

    def columns_of(i, j, second):
        at = 128 * j + HD * second
        return jnp.concatenate((s_attn[:, 128 * i : 128 * (i + 1)], s_attn[:, at : at + HD]), axis=1)

    return (
        out_y,
        grad_x,
        columns_of(0, 3, 0),
        v_query_bias,
        columns_of(1, 3, 1),
        columns_of(2, 4, 0),
        v_value_bias,
        columns_of(5, 4, 1).T,
        v_out_bias,
        v_first_gain,
        v_first_shift,
        s_feed[0],
        v_up_bias,
        s_feed[1].T,
        v_down_bias,
        v_second_gain,
        v_second_shift,
    )


def solution(mesh):
    in_specs = (
        P("dp", None, None),
        P("dp", "head"),
        P("head"),
        P("dp", "head"),
        P("dp", "head"),
        P("head"),
        P("head", "dp"),
        P(),
        P(),
        P(),
        P("dp", "head"),
        P("head"),
        P("head", "dp"),
        P(),
        P(),
        P(),
        P("head"),
        P("dp", None),
        P("dp", None, None),
    )
    out_specs = (
        P("dp", "head", None),
        P("dp", "head", None),
        P("dp", "head"),
        P(),
        P("dp", "head"),
        P("dp", "head"),
        P(),
        P("head", "dp"),
        P(),
        P(),
        P(),
        P("dp", "head"),
        P(),
        P("head", "dp"),
        P(),
        P(),
        P(),
    )
    return jax.shard_map(
        per_device, mesh=mesh, in_specs=in_specs, out_specs=out_specs, check_vma=False
    )
```

```python
import functools

import jax
import jax.numpy as jnp
from jax import lax
from jax.experimental import pallas as pl
from jax.experimental.pallas import tpu as pltpu
from jax.sharding import PartitionSpec as P

HEADS = 12
HD = 64
FF = 3072
EPSILON = 1e-12
F32 = jnp.float32
BF16 = jnp.bfloat16
SCALE = HD ** (-0.5)
MESH = pl.DeviceIdType.MESH


def flip(block, axis, bit):
    n = lax.axis_size(axis)
    return lax.ppermute(block, axis, [(i, i ^ bit) for i in range(n)])


def shift(block, axis, distance):
    n = lax.axis_size(axis)
    return lax.ppermute(block, axis, [(i, (i + distance) % n) for i in range(n)])


def sibling(block):
    return flip(block, "head", 1)


def across(block):
    return flip(block, "head", 2)


def partner(block):
    return shift(block, "dp", lax.axis_size("dp") // 2)


def pick(array, index, axis=0):
    return lax.dynamic_index_in_dim(array, index, axis, keepdims=False)


def ordered(low, own, other, axis=0):
    return jnp.stack(
        (jnp.where(low == 0, own, other), jnp.where(low == 0, other, own)), axis=axis
    )


def mm(a, b):
    return jnp.dot(a, b, preferred_element_type=F32)


def mm_t(a, b):
    return lax.dot_general(a, b, (((1,), (1,)), ((), ())), preferred_element_type=F32)


def t_mm(a, b):
    return lax.dot_general(a, b, (((0,), (0,)), ((), ())), preferred_element_type=F32)


def norm_parts(rows):
    centered = rows - jnp.mean(rows, axis=-1, keepdims=True)
    inverse = lax.rsqrt(jnp.mean(centered * centered, axis=-1, keepdims=True) + EPSILON)
    return centered * inverse, inverse


def norm_back(incoming, normed, inverse, gain):
    scaled = incoming * gain
    return inverse * (
        scaled
        - jnp.mean(scaled, axis=-1, keepdims=True)
        - normed * jnp.mean(scaled * normed, axis=-1, keepdims=True)
    )


def gaussian_parts(t):
    k = 1.0 / (1.0 + (0.3275911 * 0.5**0.5) * jnp.abs(t))
    bell = jnp.exp(-0.5 * t * t)
    series = 0.5 * 1.061405429
    for a in (-1.453152027, 1.421413741, -0.284496736, 0.254829592):
        series = series * k + 0.5 * a
    tail = series * k * bell
    return jnp.where(t < 0.0, tail, 1.0 - tail), bell


def gather(piece, x_first):
    n = lax.axis_size("dp")
    if n != 8:
        mine = lax.all_gather(piece, "dp", axis=0, tiled=False)
        return jnp.stack((mine, across(mine)))
    index = lax.axis_index("dp")
    z, x = index // 2, index % 2
    column = jnp.zeros((4,) + piece.shape, piece.dtype)
    column = lax.dynamic_update_index_in_dim(column, piece, z, 0)
    for k in (1, 2, 3):
        column = lax.dynamic_update_index_in_dim(
            column, shift(piece, "dp", 2 * k), (z - k) % 4, 0
        )
    if x_first:
        plane = ordered(x, column, flip(column, "dp", 1), axis=1)
        both = jnp.stack((plane, across(plane)))
    else:
        both = jnp.stack((column, across(column)))
        both = ordered(x, both, flip(both, "dp", 1), axis=2)
    return both.reshape((2, 8) + piece.shape)


def reduce_scatter(terms, x_last):
    n = lax.axis_size("dp")
    if n != 8:
        total = terms[0].astype(F32) + across(terms[1].astype(BF16)).astype(F32)
        return lax.psum_scatter(total, "dp", scatter_dimension=0, tiled=False)
    index = lax.axis_index("dp")
    z, x = index // 2, index % 2
    terms = terms.reshape((2, 4, 2) + terms.shape[2:])
    if x_last:
        arrived = across(terms[1])
        plane = (terms[0].astype(F32) + arrived.astype(F32)).astype(BF16)
        arrived = flip(pick(plane, 1 - x, 1), "dp", 1)
        column = pick(plane, x, 1).astype(F32) + arrived.astype(F32)
    else:
        arrived = flip(pick(terms, 1 - x, 2), "dp", 1)
        both = (pick(terms, x, 2).astype(F32) + arrived.astype(F32)).astype(BF16)
        column = both[0].astype(F32) + across(both[1]).astype(F32)
    column = column.astype(BF16)
    total = pick(column, z).astype(F32)
    for k in (1, 2, 3):
        total = total + shift(pick(column, (z + k) % 4), "dp", 2 * k).astype(F32)
    return total


def lane_masks(scale):
    lane = lax.broadcasted_iota(jnp.int32, (1, 2 * HD), 1)
    first = jnp.where(lane < HD, 1.0, 0.0)
    return [(first * scale).astype(BF16), ((1.0 - first) * scale).astype(BF16)]


def rows_of(ref):
    a, b, w = ref.shape
    return ref[...].reshape(a * b, w)


def pair_lanes(halves):
    lane = lax.broadcasted_iota(jnp.int32, halves[0].shape, 1)
    return jnp.where(lane < HD, halves[0], halves[1])


def halves_joined(low, high):
    lane = lax.broadcasted_iota(jnp.int32, low.shape, 1)
    return jnp.where(lane < HD, low, pltpu.roll(high, HD, 1))


def highs_joined(low, high):
    lane = lax.broadcasted_iota(jnp.int32, low.shape, 1)
    return jnp.where(lane < HD, pltpu.roll(low, HD, 1), high)


def head_tiles(row_own, row_other):
    return (
        row_own[:, :128],
        row_other[:, :128],
        halves_joined(row_own[:, 128:256], row_other[:, 128:256]),
    )


def project(x, wa_ref, count):
    width = x.shape[1]
    tiles = []
    for p in range(2):
        w = wa_ref[p].reshape(width, wa_ref.shape[-1])
        out = mm(x, w[:, count[0] : count[1]])
        tiles.append([out[:, 128 * i : 128 * (i + 1)] for i in range(out.shape[1] // 128)])
    return tiles


def forward_own(b, x_ref, wa_ref, bias, q_ref, k_ref, v_ref):
    rows = x_ref.shape[2] * x_ref.shape[3] * 2
    x = x_ref[:, b].reshape(rows, x_ref.shape[-1])
    one, two = project(x, wa_ref, (0, 640))
    b_query, b_value = bias
    parts = (
        (q_ref, (one[0], two[0], halves_joined(one[3], two[3])), b_query),
        (k_ref, (one[1], two[1], highs_joined(one[3], two[3])), None),
        (v_ref, (one[2], two[2], halves_joined(one[4], two[4])), b_value),
    )
    for ref, tiles, added in parts:
        for t in range(3):
            tile = tiles[t] if added is None else tiles[t] + added[t]
            ref[:, b, :, 128 * t : 128 * (t + 1)] = tile.astype(BF16).reshape(2, rows // 2, 128)


def forward_attend(b, xp_ref, wa_ref, bias, swapped, q_ref, k_ref, v_ref, ku_ref, vu_ref, o_ref):
    rows = xp_ref.shape[2] * xp_ref.shape[3] * 2
    x = xp_ref[:, b].reshape(rows, xp_ref.shape[-1])
    one, two = project(x, wa_ref, (128, 640))
    far_keys = (one[0], two[0], highs_joined(one[2], two[2]))
    far_values = (one[1], two[1], halves_joined(one[3], two[3]))
    masks = lane_masks(SCALE)
    for t in range(3):
        lanes = slice(128 * t, 128 * (t + 1))

        def load(ref):
            return ref[:, b, :, lanes].reshape(rows, 128)

        take_far = swapped[t] > 0.5
        k = jnp.where(take_far, far_keys[t], load(k_ref).astype(F32)).astype(BF16)
        v = jnp.where(
            take_far, far_values[t] + bias[1][t], load(v_ref).astype(F32)
        ).astype(BF16)
        ku_ref[:, b, :, lanes] = k.reshape(2, rows // 2, 128)
        vu_ref[:, b, :, lanes] = v.reshape(2, rows // 2, 128)
        q = load(q_ref)
        outs = []
        for mask in masks:
            s = mm_t(q * mask, k)
            raised = jnp.exp(s - jnp.max(s, axis=-1, keepdims=True))
            total = jnp.sum(raised, axis=-1, keepdims=True)
            outs.append(mm(raised.astype(BF16), v) / total)
        o_ref[:, b, :, lanes] = pair_lanes(outs).astype(BF16).reshape(2, rows // 2, 128)


def forward_listed(b, member, row_ref, col_ref, q_ref, picks_ref, select_ref, qc_ref):
    slots = row_ref.shape[-1]
    quarter = q_ref.shape[2] // 2
    cap = slots // 4
    row, col = row_ref[b], col_ref[b]
    bits = quarter.bit_length() - 1
    run_row = lax.shift_right_arithmetic(row, bits)
    run_col = lax.shift_right_arithmetic(col, bits)
    before = lax.broadcasted_iota(jnp.int32, (slots, slots), 0) < lax.broadcasted_iota(
        jnp.int32, (slots, slots), 1
    )
    same = jnp.where(run_col == run_row, jnp.where(before, 1.0, 0.0), 0.0)
    rank = jnp.sum(same, axis=0, keepdims=True)
    line = lax.broadcasted_iota(jnp.int32, (slots, 1), 0)
    place = line // cap
    wanted_run = jnp.where(
        place == 0, member, jnp.where(place == 1, member + 2, jnp.where(place == 2, 1 - member, 3 - member))
    )
    wanted_rank = (line % cap).astype(F32)
    picks = jnp.where(run_row == wanted_run, jnp.where(rank == wanted_rank, 1.0, 0.0), 0.0).astype(BF16)
    lane = lax.broadcasted_iota(jnp.int32, (slots, quarter), 1)
    places = jnp.where(jnp.bitwise_and(col, quarter - 1) == lane, 1.0, 0.0).astype(BF16)
    select = mm(picks, places).astype(BF16)
    picks_ref[b] = picks
    select_ref[b] = select
    for s in range(2):
        for e in range(2):
            at = (2 * s + e) * cap
            rows = q_ref[s, b, quarter * e : quarter * (e + 1), :]
            qc_ref[s, b, cap * e : cap * (e + 1), :] = mm(select[at : at + cap], rows).astype(BF16)


def forward_kernel(comm, *refs):
    if comm:
        (
            a_ref, b_ref, t_ref, small_ref, row_ref, col_ref,
            wa_ref, wb_ref, x_ref, xt_ref, o_ref, k_ref, v_ref, ku_ref, vu_ref, qc_ref, picks_ref, select_ref, far_ref,
            xp_ref, q_ref, local_sem, send_sem, recv_sem,
        ) = refs
    else:
        (
            wa_ref, x_ref, xp_ref, small_ref, far_ref, row_ref, col_ref,
            xt_ref, o_ref, k_ref, v_ref, ku_ref, vu_ref, qc_ref, picks_ref, select_ref,
            q_ref,
        ) = refs
    blocks = x_ref.shape[1]
    head = lax.axis_index("head")
    member, pair = lax.rem(head, 2), lax.div(head, 2)

    def listed(b, carry):
        forward_listed(b, member, row_ref, col_ref, q_ref, picks_ref, select_ref, qc_ref)
        return carry

    def turned(i, carry):
        s, rest = lax.div(i, 2 * blocks), lax.rem(i, 2 * blocks)
        part = x_ref[s, lax.div(rest, 2), lax.rem(rest, 2)]
        quarter = part.shape[0]
        xt_ref[:, pl.ds(pl.multiple_of(i * quarter, quarter), quarter)] = part.T
        return carry

    def bias_of():
        own, other = small_ref[...], far_ref[...]
        rows = [head_tiles(own[i : i + 1], other[i : i + 1]) for i in range(3)]
        return (rows[0], rows[1]), rows[2]

    if not comm:
        bias, swapped = bias_of()
        lax.fori_loop(0, 4 * blocks, turned, 0)

        def own_block(b, carry):
            forward_own(b, x_ref, wa_ref, bias, q_ref, k_ref, v_ref)
            return carry

    if comm:
        index = lax.axis_index("dp")
        z, x = lax.div(index, 2), lax.rem(index, 2)
        x_peer = {"dp": 2 * z + 1 - x}
        y_peer = {"head": lax.rem(head + 2, 4)}
        sibling_peer = {"head": 2 * pair + 1 - member}
        z_peers = [{"dp": lax.rem(index + 2 * k, 8)} for k in (1, 2, 3)]
        barrier = pltpu.get_barrier_semaphore()
        for peer in [x_peer, y_peer, sibling_peer] + z_peers:
            pl.semaphore_signal(barrier, inc=1, device_id=peer, device_id_type=MESH)
        counter = [0]

        def local(src, dst, i):
            copy = pltpu.make_async_copy(src, dst, local_sem.at[i])
            copy.start()
            return copy

        def send(src, dst, peer):
            i = counter[0]
            counter[0] += 1
            copy = pltpu.make_async_remote_copy(
                src_ref=src,
                dst_ref=dst,
                send_sem=send_sem.at[i],
                recv_sem=recv_sem.at[i],
                device_id=peer,
                device_id_type=MESH,
            )
            copy.start()
            sent.append(copy)
            return copy

        def far_copy(b):
            return pltpu.make_async_remote_copy(
                src_ref=x_ref.at[0, b],
                dst_ref=xp_ref.at[0, b],
                send_sem=send_sem.at[15 + b],
                recv_sem=recv_sem.at[15 + b],
                device_id=z_peers[1],
                device_id_type=MESH,
            )

        def near_copy(b):
            return pltpu.make_async_remote_copy(
                src_ref=xp_ref.at[0, b],
                dst_ref=xp_ref.at[1, b],
                send_sem=send_sem.at[15 + blocks + b],
                recv_sem=recv_sem.at[15 + blocks + b],
                device_id=sibling_peer,
                device_id_type=MESH,
            )

        sent = []
        quarters = (member, member + 2, 1 - member, 3 - member)
        fills = [
            local(t_ref.at[pl.ds(blocks * pair, blocks), quarters[2 * s + e]], x_ref.at[s, :, e], 2 * s + e)
            for s in range(2)
            for e in range(2)
        ]
        fill_a = local(a_ref, wa_ref.at[0, z, x], 4)
        fill_b = local(b_ref, wb_ref.at[0, :, z, x], 5)
        pl.semaphore_wait(barrier, 6)
        a_z = [send(a_ref, wa_ref.at[0, z, x], peer) for peer in z_peers]
        far = send(small_ref, far_ref, y_peer)
        b_z = [send(b_ref, wb_ref.at[0, :, z, x], peer) for peer in z_peers]
        for fill in fills:
            fill.wait()
        for b in range(blocks):
            far_copy(b).start()
        lax.fori_loop(0, 4 * blocks, turned, 0)
        half = a_ref.shape[0] // 2
        up, low = pl.ds(0, half), pl.ds(half, half)
        fill_a.wait()
        for copy in a_z:
            copy.wait_recv()
        a_x = send(wa_ref.at[0, :, x, up], wa_ref.at[0, :, x, up], x_peer)
        a_y = send(wa_ref.at[0, :, x, low], wa_ref.at[1, :, x, low], y_peer)
        a_x.wait_recv()
        a_xy = send(wa_ref.at[0, :, :, up], wa_ref.at[1, :, :, up], y_peer)
        a_y.wait_recv()
        a_yx = send(wa_ref.at[:, :, x, low], wa_ref.at[:, :, x, low], x_peer)
        fill_b.wait()
        for copy in b_z:
            copy.wait_recv()
        b_x = send(wb_ref.at[0, 0, :, x], wb_ref.at[0, 0, :, x], x_peer)
        b_y = send(wb_ref.at[0, 1, :, x], wb_ref.at[1, 1, :, x], y_peer)
        far.wait_recv()
        a_xy.wait_recv()
        a_yx.wait_recv()
        bias, swapped = bias_of()

        def own_block(b, carry):
            forward_own(b, x_ref, wa_ref, bias, q_ref, k_ref, v_ref)
            return carry

    lax.fori_loop(0, blocks, own_block, 0)
    lax.fori_loop(0, blocks, listed, 0)
    if comm:
        b_x.wait_recv()
        b_xy = send(wb_ref.at[0, 0], wb_ref.at[1, 0], y_peer)
        b_y.wait_recv()
        b_yx = send(wb_ref.at[:, 1, :, x], wb_ref.at[:, 1, :, x], x_peer)
        def attend_block(b, carry):
            far_copy(b).wait_recv()
            near = near_copy(b)
            near.start()
            near.wait_recv()
            forward_attend(b, xp_ref, wa_ref, bias, swapped, q_ref, k_ref, v_ref, ku_ref, vu_ref, o_ref)
            return carry

        lax.fori_loop(0, blocks, attend_block, 0)
        b_xy.wait_recv()
        b_yx.wait_recv()
        for copy in sent:
            copy.wait_send()
        for b in range(blocks):
            far_copy(b).wait_send()
            near_copy(b).wait_send()
    else:

        def attend_block(b, carry):
            forward_attend(b, xp_ref, wa_ref, bias, swapped, q_ref, k_ref, v_ref, ku_ref, vu_ref, o_ref)
            return carry

        lax.fori_loop(0, blocks, attend_block, 0)


def vmem_spec():
    return pl.BlockSpec(memory_space=pltpu.VMEM)


def any_spec():
    return pl.BlockSpec(memory_space=pl.ANY)


def forward(tokens, piece_a, piece_b, small, listed, member, pair):
    n = lax.axis_size("dp")
    block_count, block_rows, width = tokens.shape
    blocks, quarter = block_count // 2, block_rows // 4
    slots = listed.shape[1]
    cap = slots // 4
    lanes = 6 * HD
    tokens = tokens.reshape(block_count, 4, quarter, width)
    row, col = listed[:, None, :], listed[:, :, None]
    rows_shape = (2, blocks, 2, quarter, width)

    def out(*shape, dtype=BF16):
        return jax.ShapeDtypeStruct(shape, dtype)

    dense = (2, blocks, 2 * quarter, lanes)
    tail = [out(width, 2 * blocks * 2 * quarter)] + [out(*dense)] * 5 + [
        out(2, blocks, 2 * cap, lanes),
        out(blocks, slots, slots),
        out(blocks, slots, quarter),
    ]
    params = dict(vmem_limit_bytes=60 * 2**20, has_side_effects=True)
    if n == 8:
        shapes = [
            out(2, 4, 2, *piece_a.shape),
            out(2, 2, 4, 2, *piece_b.shape[1:]),
            out(*rows_shape),
            *tail,
            out(*small.shape, dtype=F32),
        ]
        specs = [vmem_spec()] * len(shapes)
        specs[1] = any_spec()
        results = pl.pallas_call(
            functools.partial(forward_kernel, True),
            out_shape=shapes,
            in_specs=[vmem_spec(), vmem_spec(), any_spec()] + [vmem_spec()] * 3,
            out_specs=specs,
            scratch_shapes=[
                pltpu.VMEM(rows_shape, BF16),
                pltpu.VMEM(dense, BF16),
                pltpu.SemaphoreType.DMA((6,)),
                pltpu.SemaphoreType.DMA((15 + 2 * blocks,)),
                pltpu.SemaphoreType.DMA((15 + 2 * blocks,)),
            ],
            compiler_params=pltpu.CompilerParams(collective_id=1, **params),
        )(piece_a, piece_b, tokens, small, row, col)
        w_attn, w_feed, rows, *rest, far = results
    else:
        mine = pick(tokens.reshape(2, blocks, 2, 2, quarter, width), pair)
        rows = jnp.stack((pick(mine, member, 2), pick(mine, 1 - member, 2)))
        w_attn = gather(piece_a, True)
        w_feed = jnp.stack([gather(piece_b[i], True) for i in range(2)], axis=1)
        far = across(small)
        shapes = tail
        rest = pl.pallas_call(
            functools.partial(forward_kernel, False),
            out_shape=shapes,
            in_specs=[vmem_spec()] * 7,
            out_specs=[vmem_spec()] * len(shapes),
            scratch_shapes=[pltpu.VMEM(dense, BF16)],
            compiler_params=pltpu.CompilerParams(vmem_limit_bytes=60 * 2**20),
        )(w_attn.reshape(2, width, -1), rows, partner(rows), small, far, row, col)
    w_attn = w_attn.reshape(2, width, -1)
    w_feed = w_feed.reshape(2, 2, width, -1)
    return (w_attn, w_feed, rows, *rest, far)


OUT_BIAS, FIRST_GAIN, FIRST_SHIFT, DOWN_BIAS, SECOND_GAIN, SECOND_SHIFT = range(4, 10)


def picked(chosen, rows):
    high = rows.astype(BF16)
    rest = (rows - high.astype(F32)).astype(BF16)
    return mm(chosen, high) + mm(chosen, rest)


def column_sum(rows):
    return jnp.sum(rows, axis=0, keepdims=True)


def middle_kernel(
    wa_ref, wf_in, x_in, attn_ref, select_ref, picks_ref, grads_in, small_ref, far_ref,
    y_ref, gb_ref, da_ref, db_ref, df_ref, vec_ref,
    wf, xs, gs, wo, ao, hid, hl, hc, one_c, pre, act, feeds, ft_out, ft_in, rows_ref, ds, dfd, turned_h, turned_d,
    d_act, d_pre, term, dt_out, dt_in, acc, local_sem, send_sem, recv_sem,
):
    blocks, half, width = hid.shape
    quarter = half // 2
    cap = df_ref.shape[1] // 2
    own = blocks * 2 * cap
    head = lax.axis_index("head")
    member, pair = lax.rem(head, 2), lax.div(head, 2)
    sibling_peer = {"head": 2 * pair + 1 - member}
    y_peer = {"head": lax.rem(head + 2, 4)}
    barrier = pltpu.get_barrier_semaphore()
    for peer in (sibling_peer, y_peer):
        pl.semaphore_signal(barrier, inc=1, device_id=peer, device_id_type=MESH)
    sent = []

    def remote(src, dst, peer, i):
        return pltpu.make_async_remote_copy(
            src_ref=src,
            dst_ref=dst,
            send_sem=send_sem.at[i],
            recv_sem=recv_sem.at[i],
            device_id=peer,
            device_id_type=MESH,
        )

    def send(src, dst, peer):
        copy = remote(src, dst, peer, 2 * blocks + len(sent))
        copy.start()
        sent.append(copy)
        return copy

    def local(src, dst, i):
        copy = pltpu.make_async_copy(src, dst, local_sem.at[i])
        copy.start()
        return copy

    def hidden_copy(b):
        return remote(hl.at[0, b], hl.at[1, b], sibling_peer, b)

    def feed_copy(b):
        return remote(ft_out.at[b], ft_in.at[b], sibling_peer, blocks + b)

    def vector(i):
        return small_ref[i : i + 1, :]

    up_biases = (small_ref, far_ref)

    fill_x = local(x_in.at[0], xs, 0)
    fill_w = local(wf_in, wf, 1)
    fill_g = local(grads_in.at[pl.ds(blocks * pair, blocks)], gs, 2)
    pl.semaphore_wait(barrier, 2)
    other_rows = send(attn_ref.at[1], ao, sibling_peer)
    for p in range(2):
        wo[0, :, 128 * p : 128 * (p + 1)] = wa_ref[p, :, 640:768]
    wo[0, :, 256:384] = highs_joined(
        wa_ref[0, :, 512:640].astype(F32), wa_ref[1, :, 512:640].astype(F32)
    ).astype(BF16)
    other_weights = send(wo.at[0], wo.at[1], sibling_peer)

    def branch_own(b, carry):
        feeds[b] = mm_t(attn_ref[0, b], wo[0])
        return carry

    lax.fori_loop(0, blocks, branch_own, 0)
    acc[...] = jnp.zeros_like(acc)
    fill_x.wait()
    other_rows.wait_recv()
    other_weights.wait_recv()

    def first_norm(b, carry):
        rows = xs[b].reshape(half, width).astype(F32) + feeds[b] + mm_t(ao[b], wo[1]) + vector(OUT_BIAS)
        hidden = norm_parts(rows)[0] * vector(FIRST_GAIN) + vector(FIRST_SHIFT)
        low = hidden.astype(BF16)
        hid[b] = hidden
        hl[0, b] = low
        hidden_copy(b).start()
        for e in range(2):
            at, run = slice(cap * e, cap * (e + 1)), slice(quarter * e, quarter * (e + 1))
            chosen = select_ref[b, at, :]
            one_c[b, at, :] = picked(chosen, rows[run])
            hc[0, b, at, :] = mm(chosen, low[run]).astype(BF16)
        return carry

    lax.fori_loop(0, blocks, first_norm, 0)
    other_listed = send(hc.at[0], hc.at[1], sibling_peer)
    fill_w.wait()

    def gelu_rows(i, carry):
        at = pl.ds(pl.multiple_of(16 * i, 16), 16)
        t = pre[at, :]
        act[0, at, :] = (t * gaussian_parts(t)[0]).astype(BF16)
        return carry

    def feed(s, b):
        out = 0.0
        for p in range(2):
            pre[0:half] = mm(hl[s, b], wf[p, 0]) + up_biases[p][3:4, :]
            lax.fori_loop(0, half // 16, gelu_rows, 0, unroll=2)
            out = out + mm_t(act[0, 0:half], wf[p, 1])
        return out

    def feed_other(b, carry):
        hidden_copy(b).wait_recv()
        ft_out[b] = feed(1, b).astype(BF16)
        feed_copy(b).start()
        return carry

    lax.fori_loop(0, blocks, feed_other, 0)

    def feed_own(b, carry):
        feeds[b] = feed(0, b)
        return carry

    lax.fori_loop(0, blocks, feed_own, 0)
    fill_g.wait()

    def second_norm(b, carry):
        feed_copy(b).wait_recv()
        rows = hid[b] + feeds[b] + ft_in[b].astype(F32) + vector(DOWN_BIAS)
        out = (norm_parts(rows)[0] * vector(SECOND_GAIN) + vector(SECOND_SHIFT)).astype(BF16)
        listed = []
        for e in range(2):
            at, run = slice(cap * e, cap * (e + 1)), slice(quarter * e, quarter * (e + 1))
            rows_ref[e, b] = out[run]
            listed.append(picked(select_ref[b, at, :], rows[run]))
        normed, inverse = norm_parts(jnp.concatenate(listed, axis=0))
        grad_y = mm(picks_ref[b, 0 : 2 * cap, :], gs[b])
        d_second = norm_back(grad_y, normed, inverse, vector(SECOND_GAIN))
        d_feed = d_second.astype(BF16)
        ds[b] = d_second
        dfd[0, b] = d_feed
        acc[3:4] += column_sum(d_feed.astype(F32))
        acc[4:5] += column_sum(grad_y * normed)
        acc[5:6] += column_sum(grad_y)
        return carry

    lax.fori_loop(0, blocks, second_norm, 0)
    other_d = send(dfd.at[0], dfd.at[1], sibling_peer)
    moved = send(rows_ref.at[1 - pair], y_ref.at[pair], y_peer)
    kept = local(rows_ref.at[pair], y_ref.at[pair], 3)

    other_listed.wait_recv()

    def turn(ref, out):
        flat = ref[...].reshape(2 * own, width)
        for i in range(2 * own // 128):
            out[:, 128 * i : 128 * (i + 1)] = flat[128 * i : 128 * (i + 1)].T

    turn(hc, turned_h)
    other_d.wait_recv()
    turn(dfd, turned_d)

    for p in range(2):
        pre[...] = mm(hc[...].reshape(2 * own, width), wf[p, 0]) + up_biases[p][3:4, :]
        d_act[...] = mm(dfd[...].reshape(2 * own, width), wf[p, 1])

        def back_rows_of(i, total):
            at = pl.ds(pl.multiple_of(16 * i, 16), 16)
            t = pre[at, :]
            cdf, bell = gaussian_parts(t)
            act[p, at, :] = (t * cdf).astype(BF16)
            d = (d_act[at, :] * (cdf + t * (bell * (0.5 / jnp.pi) ** 0.5))).astype(BF16)
            d_pre[p, at, :] = d
            d = d.astype(F32)
            return total + (d[0:8] + d[8:16])

        total = lax.fori_loop(0, 2 * own // 16, back_rows_of, jnp.zeros((8, width), F32))
        acc[6 + p : 7 + p] = column_sum(total)
        part = mm_t(d_pre[p], wf[p, 0])
        if p == 0:
            term[...] = part
        else:
            part = part + term[...]
            dt_out[...] = part[own:].astype(BF16)
            other_term = send(dt_out, dt_in, sibling_peer)
            term[0:own] = part[:own]

    gb_ref[0, 0] = mm(turned_h[...], d_pre[0]).astype(BF16)
    other_term.wait_recv()

    def first_back(b, carry):
        at = pl.ds(pl.multiple_of(2 * cap * b, 2 * cap), 2 * cap)
        d_hidden = ds[b] + term[at, :] + dt_in[at, :].astype(F32)
        normed, inverse = norm_parts(one_c[b])
        d_first = norm_back(d_hidden, normed, inverse, vector(FIRST_GAIN))
        d_branch = d_first.astype(BF16)
        df_ref[b] = d_first
        db_ref[0, b] = d_branch
        acc[0:1] += column_sum(d_branch.astype(F32))
        acc[1:2] += column_sum(d_hidden * normed)
        acc[2:3] += column_sum(d_hidden)
        return carry

    lax.fori_loop(0, blocks, first_back, 0)
    other_branch = send(db_ref.at[0], db_ref.at[1], sibling_peer)
    gb_ref[0, 1] = mm(turned_d[...], act[0]).astype(BF16)
    gb_ref[1, 0] = mm(turned_h[...], d_pre[1]).astype(BF16)
    gb_ref[1, 1] = mm(turned_d[...], act[1]).astype(BF16)
    tiles = width // 128
    vec_ref[...] = jnp.zeros_like(vec_ref)
    for t in range(tiles):
        lanes = slice(128 * t, 128 * (t + 1))
        for i in range(6):
            vec_ref[tiles * i + t : tiles * i + t + 1, :] = acc[i : i + 1, lanes]
        for h in range(4):
            mine = jnp.where(head == h, acc[6:7, lanes], 0.0)
            other = jnp.where(lax.rem(head + 2, 4) == h, acc[7:8, lanes], 0.0)
            at = tiles * (6 + h) + t
            vec_ref[at : at + 1, :] = mine + other
    other_branch.wait_recv()
    for s in range(2):
        da = mm(db_ref[s].reshape(own, width), wo[0])
        da_ref[s] = da.astype(BF16).reshape(da_ref.shape[1:])
    kept.wait()
    moved.wait_recv()
    for copy in sent:
        copy.wait_send()
    for b in range(blocks):
        hidden_copy(b).wait_send()
        feed_copy(b).wait_send()


def middle(w_attn, w_feed, x_rows, attention, select, picks, out_grad, small, far):
    _, blocks, block_half, lanes = attention.shape
    width = w_attn.shape[1]
    quarter = block_half // 2
    listed = select.shape[1] // 2
    own = blocks * listed

    def out(*shape, dtype=BF16):
        return jax.ShapeDtypeStruct(shape, dtype)

    def room(*shape, dtype=BF16):
        return pltpu.VMEM(shape, dtype)

    in_specs = [vmem_spec()] * 9
    for i in (1, 2, 6):
        in_specs[i] = any_spec()
    return pl.pallas_call(
        middle_kernel,
        out_shape=[
            out(2, blocks, quarter, width),
            out(*w_feed.shape),
            out(2, blocks, listed, lanes),
            out(2, blocks, listed, width),
            out(blocks, listed, width, dtype=F32),
            out(64, 128, dtype=F32),
        ],
        in_specs=in_specs,
        out_specs=[vmem_spec()] * 6,
        scratch_shapes=[
            room(*w_feed.shape),
            room(blocks, 2, quarter, width),
            room(blocks, *out_grad.shape[1:]),
            room(2, width, lanes),
            room(blocks, block_half, lanes),
            room(blocks, block_half, width, dtype=F32),
            room(2, blocks, block_half, width),
            room(2, blocks, listed, width),
            room(blocks, listed, width, dtype=F32),
            room(2 * own, width, dtype=F32),
            room(2, 2 * own, width),
            room(blocks, block_half, width, dtype=F32),
            room(blocks, block_half, width),
            room(blocks, block_half, width),
            room(2, blocks, quarter, width),
            room(blocks, listed, width, dtype=F32),
            room(2, blocks, listed, width),
            room(width, 2 * own),
            room(width, 2 * own),
            room(2 * own, width, dtype=F32),
            room(2, 2 * own, width),
            room(2 * own, width, dtype=F32),
            room(own, width),
            room(own, width),
            room(8, width, dtype=F32),
            pltpu.SemaphoreType.DMA((4,)),
            pltpu.SemaphoreType.DMA((2 * blocks + 7,)),
            pltpu.SemaphoreType.DMA((2 * blocks + 7,)),
        ],
        compiler_params=pltpu.CompilerParams(
            collective_id=3, vmem_limit_bytes=60 * 2**20, has_side_effects=True
        ),
    )(w_attn, w_feed, x_rows, attention, select, picks, out_grad, small, far)


def back_queries(b, qc_ref, g_ref, ku_ref, vu_ref, select_ref, o_ref, dt_ref, oc_ref, total_ref):
    rows = ku_ref.shape[2] * 2
    slots = qc_ref.shape[2] * 2
    cap = slots // 4
    quarter = rows // 4
    select = select_ref[b]
    tiles = []
    for t in range(3):
        lanes = slice(128 * t, 128 * (t + 1))
        q = qc_ref[:, b, :, lanes].reshape(slots, 128)
        g = g_ref[:, b, :, lanes].reshape(slots, 128)
        k = ku_ref[:, b, :, lanes].reshape(rows, 128)
        v = vu_ref[:, b, :, lanes].reshape(rows, 128)
        outs = []
        for mask, one in zip(lane_masks(SCALE), lane_masks(1.0)):
            s = mm_t(q * mask, k)
            raised = jnp.exp(s - jnp.max(s, axis=-1, keepdims=True))
            probs = raised / jnp.sum(raised, axis=-1, keepdims=True)
            d_probs = mm_t(g * one, v)
            inner = jnp.sum(d_probs * probs, axis=-1, keepdims=True)
            d_scores = (probs * (d_probs - inner)).astype(BF16)
            outs.append(mm(d_scores, k) * SCALE)
        tile = pair_lanes(outs).astype(BF16)
        total_ref[0:1, lanes] += jnp.sum(tile.astype(F32), axis=0, keepdims=True)
        tiles.append(tile)
    for s in range(2):
        for e in range(2):
            at = (2 * s + e) * cap
            chosen = select[at : at + cap]
            own = slice(quarter * e, quarter * (e + 1))
            dense = [t_mm(chosen, tile[at : at + cap]) for tile in tiles]
            dt_ref[0, s, b, own, 0:128] = dense[0].astype(BF16)
            dt_ref[1, s, b, own, 0:128] = dense[1].astype(BF16)
            lane = lax.broadcasted_iota(jnp.int32, dense[2].shape, 1)
            for p in range(2):
                last = dense[2] if p == 0 else pltpu.roll(dense[2], HD, 1)
                dt_ref[p, s, b, own, 384:512] = jnp.where(lane < HD, last, 0.0).astype(BF16)
            rows_o = mm(chosen, o_ref[s, b, own, :])
            at_o = slice(cap * e, cap * (e + 1))
            lane = lax.broadcasted_iota(jnp.int32, (cap, 128), 1)
            for p in range(2):
                oc_ref[p, s, b, at_o, 128:256] = rows_o[:, 128 * p : 128 * (p + 1)].astype(BF16)
                last = rows_o[:, 256:384] if p == 1 else pltpu.roll(rows_o[:, 256:384], HD, 1)
                oc_ref[p, s, b, at_o, 0:128] = jnp.where(lane < HD, 0.0, last).astype(BF16)


def back_keys(b, swapped, qc_ref, g_ref, qf_ref, gf_ref, k_ref, v_ref, dt_ref, total_ref):
    rows = k_ref.shape[2] * 2
    slots = qc_ref.shape[2] * 2
    for t in range(3):
        lanes = slice(128 * t, 128 * (t + 1))
        take_far = swapped[t] > 0.5

        def chosen(near, far):
            near = near[:, b, :, lanes].reshape(slots, 128).astype(F32)
            far = far[:, b, :, lanes].reshape(slots, 128).astype(F32)
            return jnp.where(take_far, far, near).astype(BF16)

        q, g = chosen(qc_ref, qf_ref), chosen(g_ref, gf_ref)
        k = k_ref[:, b, :, lanes].reshape(rows, 128)
        v = v_ref[:, b, :, lanes].reshape(rows, 128)
        d_keys, d_values = [], []
        for mask, one in zip(lane_masks(SCALE), lane_masks(1.0)):
            s = mm_t(k, q * mask)
            raised = jnp.exp(s - jnp.max(s, axis=0, keepdims=True))
            probs = raised / jnp.sum(raised, axis=0, keepdims=True)
            d_probs = mm_t(v, g * one)
            inner = jnp.sum(d_probs * probs, axis=0, keepdims=True)
            d_scores = (probs * (d_probs - inner)).astype(BF16)
            d_keys.append(mm(d_scores, q) * SCALE)
            d_values.append(mm(probs.astype(BF16), g))
        dk, dv = pair_lanes(d_keys), pair_lanes(d_values)
        total_ref[1:2, lanes] += jnp.sum(dv.astype(BF16).astype(F32), axis=0, keepdims=True)
        half = (2, rows // 2, 128)
        if t < 2:
            dt_ref[t, :, b, :, 128:256] = dk.astype(BF16).reshape(half)
            dt_ref[t, :, b, :, 256:384] = dv.astype(BF16).reshape(half)
        else:
            lane = lax.broadcasted_iota(jnp.int32, dk.shape, 1)
            for p in range(2):
                last = pltpu.roll(dk, HD, 1) if p == 0 else dk
                before = dt_ref[p, :, b, :, 384:512].reshape(rows, 128).astype(F32)
                dt_ref[p, :, b, :, 384:512] = (
                    jnp.where(lane < HD, before, last).astype(BF16).reshape(half)
                )
                last = dv if p == 0 else pltpu.roll(dv, HD, 1)
                dt_ref[p, :, b, :, 512:640] = (
                    jnp.where(lane < HD, last, 0.0).astype(BF16).reshape(half)
                )


def back_weights(p, xt_ref, dt_ref, db_ref, oc_ref, ga_ref):
    width = xt_ref.shape[0]
    shape = ga_ref.shape[1:-1] + (128,)
    listed = db_ref.shape[0] * db_ref.shape[1] * db_ref.shape[2]
    d_branch = db_ref[...].reshape(listed, width)
    outs = mm(xt_ref[...], dt_ref[p].reshape(xt_ref.shape[1], 640))
    extra = t_mm(d_branch, oc_ref[p].reshape(listed, 256))
    for i in range(6):
        if i < 4:
            tile = outs[:, 128 * i : 128 * (i + 1)]
        elif i == 4:
            tile = outs[:, 512:640] + extra[:, 0:128]
        else:
            tile = extra[:, 128:256]
        ga_ref[p, ..., 128 * i : 128 * (i + 1)] = tile.astype(BF16).reshape(shape)


def back_rows(s, b, wa_ref, dt_ref):
    rows, width = dt_ref.shape[3], wa_ref.shape[-1]
    out = 0.0
    for p in range(2):
        w = wa_ref[p].reshape(-1, wa_ref.shape[-1])
        out = out + mm_t(dt_ref[p, s, b], w[:, 0:640])
    return out


def bias_totals(member, pair, total_ref):
    lane = lax.broadcasted_iota(jnp.int32, (1, 128), 1)
    line = lax.broadcasted_iota(jnp.int32, (8, 128), 0)
    first = jnp.zeros((8, 128), F32)
    second = jnp.zeros((8, 128), F32)
    for i in range(2):
        last = total_ref[i : i + 1, 256:384]
        for p in range(2):
            place = 4 * i + 2 * (pair if p == 0 else 1 - pair) + member
            tile = total_ref[i : i + 1, 128 * p : 128 * (p + 1)]
            third = last if p == 0 else pltpu.roll(last, HD, 1)
            first = first + jnp.where(line == place, tile, 0.0)
            second = second + jnp.where(line == place, jnp.where(lane < HD, third, 0.0), 0.0)
    return first, second


def back_kernel(comm, *refs):
    if comm:
        (
            gb_ref, qc_ref, g_ref, k_ref, v_ref, ku_ref, vu_ref, o_ref, xt_ref, wa_ref,
            select_ref, small_ref, far_ref, db_ref, df_ref, vec_ref,
            gx_ref, sa_ref, sb_ref, sum_ref,
            dt_ref, oc_ref, ga_ref, total_ref, qf_ref, gf_ref, term_ref, near_ref, rows_ref,
            b1_up, b1_low, b2, b3, a1_up, a1_low, a2, a3, vec1, vec4,
            local_sem, send_sem, recv_sem,
        ) = refs
    else:
        (
            qf_ref, gf_ref, qc_ref, g_ref, k_ref, v_ref, ku_ref, vu_ref, o_ref, xt_ref, wa_ref,
            select_ref, small_ref, far_ref, db_ref,
            ga_ref, term_ref, both_ref,
            dt_ref, oc_ref, total_ref,
        ) = refs
    blocks = k_ref.shape[1]
    head = lax.axis_index("head")
    member, pair = lax.rem(head, 2), lax.div(head, 2)
    swapped = head_tiles(small_ref[2:3], far_ref[2:3])
    total_ref[...] = jnp.zeros_like(total_ref)

    def queries(b, carry):
        back_queries(b, qc_ref, g_ref, ku_ref, vu_ref, select_ref, o_ref, dt_ref, oc_ref, total_ref)
        return carry

    def keys(b, carry):
        back_keys(b, swapped, qc_ref, g_ref, qf_ref, gf_ref, k_ref, v_ref, dt_ref, total_ref)
        return carry

    def weights(p, carry):
        back_weights(p, xt_ref, dt_ref, db_ref, oc_ref, ga_ref)
        return carry

    if not comm:
        lax.fori_loop(0, blocks, queries, 0)
        lax.fori_loop(0, blocks, keys, 0)
        lax.fori_loop(0, 2, weights, 0)

        def rows(i, carry):
            s, b = lax.div(i, blocks), lax.rem(i, blocks)
            term_ref[s, b] = back_rows(s, b, wa_ref, dt_ref)
            return carry

        lax.fori_loop(0, 2 * blocks, rows, 0)
        both_ref[0:8], both_ref[8:16] = bias_totals(member, pair, total_ref)
        return

    index = lax.axis_index("dp")
    z, x = lax.div(index, 2), lax.rem(index, 2)
    x_peer = {"dp": 2 * z + 1 - x}
    y_peer = {"head": lax.rem(head + 2, 4)}
    sibling_peer = {"head": 2 * pair + 1 - member}
    z_peers = [{"dp": lax.rem(index + 2 * k, 8)} for k in (1, 2, 3)]
    z_to = [lax.rem(z + k, 4) for k in (1, 2, 3)]
    barrier = pltpu.get_barrier_semaphore()
    for peer in [x_peer, y_peer, sibling_peer] + z_peers:
        pl.semaphore_signal(barrier, inc=1, device_id=peer, device_id_type=MESH)
    pl.semaphore_wait(barrier, 6)
    sent = []

    def send(src, dst, peer):
        i = len(sent)
        copy = pltpu.make_async_remote_copy(
            src_ref=src,
            dst_ref=dst,
            send_sem=send_sem.at[i],
            recv_sem=recv_sem.at[i],
            device_id=peer,
            device_id_type=MESH,
        )
        copy.start()
        sent.append(copy)
        return copy

    def plus(a, b):
        return (a.astype(F32) + b.astype(F32)).astype(BF16)

    def first_phase(up_other, low_other, up_buffer, low_buffer):
        return send(up_other, up_buffer, y_peer), send(low_other, low_buffer, x_peer)

    far_g = send(g_ref, gf_ref, z_peers[1])
    far_q = send(qc_ref, qf_ref, z_peers[1])
    b_up = send(gb_ref.at[1, 0], b1_up, y_peer)
    b_low = send(gb_ref.at[:, 1, :, 1 - x], b1_low, x_peer)
    lax.fori_loop(0, blocks, queries, 0)
    far_g.wait_recv()
    far_q.wait_recv()
    lax.fori_loop(0, blocks, keys, 0)

    vec_rows = vec_ref.shape[0]
    vec1[0, 0:vec_rows] = vec_ref[...]
    vec1[0, vec_rows : vec_rows + 8], vec1[0, vec_rows + 8 : vec_rows + 16] = bias_totals(
        member, pair, total_ref
    )
    v_sib = send(vec1.at[0], vec1.at[1], sibling_peer)

    halves = gb_ref.shape[2]

    def add_up(i, carry):
        b1_up[i] = plus(b1_up[i], gb_ref[0, 0, i])
        return carry

    def add_low(i, carry):
        for p in range(2):
            b1_low[p, i] = plus(b1_low[p, i], gb_ref[p, 1, i, x])
        return carry

    b_up.wait_recv()
    lax.fori_loop(0, halves, add_up, 0)
    b_up = send(b1_up.at[:, 1 - x], b2.at[0], x_peer)
    b_low.wait_recv()
    lax.fori_loop(0, halves, add_low, 0)
    b_low = send(b1_low.at[1], b2.at[1], y_peer)
    v_sib.wait_recv()
    vec1[2] = vec1[0] + vec1[1]
    v_y = send(vec1.at[2], vec1.at[3], y_peer)

    lax.fori_loop(0, 2, weights, 0)
    half = ga_ref.shape[3] // 2
    up, low = slice(0, half), slice(half, 2 * half)
    a_up = send(ga_ref.at[1, :, :, pl.ds(0, half)], a1_up, y_peer)
    a_low = send(ga_ref.at[:, :, 1 - x, pl.ds(half, half)], a1_low, x_peer)

    def rows_other(b, carry):
        term_ref[b] = back_rows(1, b, wa_ref, dt_ref).astype(BF16)
        return carry

    lax.fori_loop(0, blocks, rows_other, 0)
    term = send(term_ref, near_ref, sibling_peer)

    b_up.wait_recv()
    b_low.wait_recv()

    def add_second(i, carry):
        b2[0, i] = plus(b2[0, i], b1_up[i, x])
        b2[1, i] = plus(b2[1, i], b1_low[0, i])
        return carry

    lax.fori_loop(0, halves, add_second, 0)
    b_z = [send(b2.at[:, to], b3.at[k], peer) for k, (to, peer) in enumerate(zip(z_to, z_peers))]
    v_y.wait_recv()
    vec1[4] = vec1[2] + vec1[3]
    v_x = send(vec1.at[4], vec1.at[5], x_peer)

    a_up.wait_recv()

    def a_add_up(i, carry):
        a1_up[i] = plus(a1_up[i], ga_ref[0, i, :, up])
        return carry

    lax.fori_loop(0, halves, a_add_up, 0)
    a_up = send(a1_up.at[:, 1 - x], a2.at[0], x_peer)
    a_low.wait_recv()

    def a_add_low(i, carry):
        for p in range(2):
            a1_low[p, i] = plus(a1_low[p, i], ga_ref[p, i, x, low])
        return carry

    lax.fori_loop(0, halves, a_add_low, 0)
    a_low = send(a1_low.at[1], a2.at[1], y_peer)

    cap = df_ref.shape[1] // 2
    quarter = rows_ref.shape[2]
    term.wait_recv()

    def rows_own(b, carry):
        own = back_rows(0, b, wa_ref, dt_ref) + near_ref[b].astype(F32)
        for e in range(2):
            first = df_ref[b, cap * e : cap * (e + 1), :]
            high = first.astype(BF16)
            rest = (first - high.astype(F32)).astype(BF16)
            chosen = select_ref[b, cap * e : cap * (e + 1), :]
            spread = t_mm(chosen, high) + t_mm(chosen, rest)
            rows_ref[e, b] = (own[quarter * e : quarter * (e + 1)] + spread).astype(BF16)
        return carry

    lax.fori_loop(0, blocks, rows_own, 0)
    moved = send(rows_ref.at[1 - pair], gx_ref.at[pair], y_peer)
    kept = pltpu.make_async_copy(rows_ref.at[pair], gx_ref.at[pair], local_sem.at[0])
    kept.start()
    v_x.wait_recv()
    vec1[6] = vec1[4] + vec1[5]
    own_vec = pltpu.make_async_copy(vec1.at[6], vec4.at[z], local_sem.at[1])
    own_vec.start()
    v_z = [send(vec1.at[6], vec4.at[z], peer) for peer in z_peers]

    a_up.wait_recv()
    a_low.wait_recv()

    def a_add_second(i, carry):
        a2[0, i] = plus(a2[0, i], a1_up[i, x])
        a2[1, i] = plus(a2[1, i], a1_low[0, i])
        return carry

    lax.fori_loop(0, halves, a_add_second, 0)
    a_z = [send(a2.at[:, to], a3.at[k], peer) for k, (to, peer) in enumerate(zip(z_to, z_peers))]

    for copy in b_z:
        copy.wait_recv()
    for t in range(2):
        total = b2[t, z].astype(F32)
        for k in range(3):
            total = total + b3[k, t].astype(F32)
        sb_ref[t] = total
    own_vec.wait()
    for copy in v_z:
        copy.wait_recv()
    sum_ref[...] = (vec4[0] + vec4[1]) + (vec4[2] + vec4[3])
    for copy in a_z:
        copy.wait_recv()
    for t, part in enumerate((up, low)):
        total = a2[t, z].astype(F32)
        for k in range(3):
            total = total + a3[k, t].astype(F32)
        sa_ref[part] = total
    kept.wait()
    moved.wait_recv()
    for copy in sent:
        copy.wait_send()


def backward(gb, q_compact, d_attention, keys, values, keys_used, values_used, attention, rows_t, w_attn, select, small, far, d_branch, d_first, vectors):
    n = lax.axis_size("dp")
    _, blocks, block_half, lanes = keys.shape
    width = rows_t.shape[0]
    quarter = block_half // 2
    piece = width // n
    slots = select.shape[1]
    vec_rows = vectors.shape[0] + 16

    def out(*shape, dtype=BF16):
        return jax.ShapeDtypeStruct(shape, dtype)

    compact = (2, blocks, slots // 2, lanes)
    scratch = [
        pltpu.VMEM((2, 2, blocks, block_half, 640), BF16),
        pltpu.VMEM((2, 2, blocks, slots // 2, 256), BF16),
    ]
    shared = (q_compact, d_attention, keys, values, keys_used, values_used, attention, rows_t, w_attn, select, small, far, d_branch)
    if n == 8:
        half = piece // 2
        return pl.pallas_call(
            functools.partial(back_kernel, True),
            out_shape=[
                out(2, blocks, quarter, width),
                out(piece, width, dtype=F32),
                out(2, piece, width, dtype=F32),
                out(vec_rows, 128, dtype=F32),
            ],
            in_specs=[vmem_spec()] * 16,
            out_specs=[vmem_spec()] * 4,
            scratch_shapes=scratch
            + [
                pltpu.VMEM((2, 4, 2, piece, width), BF16),
                pltpu.VMEM((8, lanes), F32),
                pltpu.VMEM(compact, BF16),
                pltpu.VMEM(compact, BF16),
                pltpu.VMEM((blocks, block_half, width), BF16),
                pltpu.VMEM((blocks, block_half, width), BF16),
                pltpu.VMEM((2, blocks, quarter, width), BF16),
                pltpu.VMEM((4, 2, piece, width), BF16),
                pltpu.VMEM((2, 4, piece, width), BF16),
                pltpu.VMEM((2, 4, piece, width), BF16),
                pltpu.VMEM((3, 2, piece, width), BF16),
                pltpu.VMEM((4, 2, half, width), BF16),
                pltpu.VMEM((2, 4, half, width), BF16),
                pltpu.VMEM((2, 4, half, width), BF16),
                pltpu.VMEM((3, 2, half, width), BF16),
                pltpu.VMEM((7, vec_rows, 128), F32),
                pltpu.VMEM((4, vec_rows, 128), F32),
                pltpu.SemaphoreType.DMA((2,)),
                pltpu.SemaphoreType.DMA((24,)),
                pltpu.SemaphoreType.DMA((24,)),
            ],
            compiler_params=pltpu.CompilerParams(
                collective_id=2, vmem_limit_bytes=62 * 2**20, has_side_effects=True
            ),
        )(gb.reshape(2, 2, 4, 2, piece, width), *shared, d_first, vectors)
    ga, term, both = pl.pallas_call(
        functools.partial(back_kernel, False),
        out_shape=[
            out(2, 1, 1, width, width),
            out(2, blocks, block_half, width, dtype=F32),
            out(16, 128, dtype=F32),
        ],
        in_specs=[vmem_spec()] * 15,
        out_specs=[vmem_spec()] * 3,
        scratch_shapes=scratch + [pltpu.VMEM((8, lanes), F32)],
        compiler_params=pltpu.CompilerParams(vmem_limit_bytes=62 * 2**20),
    )(partner(q_compact), partner(d_attention), *shared)
    pair = lax.axis_index("head") // 2
    cap = slots // 4
    chosen = select[:, : 2 * cap].reshape(blocks, 2, cap, quarter).astype(F32)
    spread = jnp.einsum(
        "bekr,bekw->berw",
        chosen,
        d_first.reshape(blocks, 2, cap, width),
        precision=lax.Precision.HIGHEST,
    )
    own = term[0].reshape(spread.shape) + sibling(term[1].astype(BF16)).astype(F32).reshape(spread.shape)
    own = (own + spread).astype(BF16)
    grad_x = ordered(pair, pick(own, pair, 1), across(pick(own, 1 - pair, 1)))
    pieces = (2, n, piece, width)
    s_attn = reduce_scatter(ga.reshape(pieces), True)
    s_feed = jnp.stack([reduce_scatter(gb[:, i].reshape(pieces), True) for i in range(2)])
    return grad_x, s_attn, s_feed, lax.psum(jnp.concatenate((vectors, both)), ("dp", "head"))


def per_device(
    tokens,
    query_weight,
    query_bias,
    key_weight,
    value_weight,
    value_bias,
    out_weight,
    out_bias,
    first_gain,
    first_shift,
    up_weight,
    up_bias,
    down_weight,
    down_bias,
    second_gain,
    second_shift,
    block_order,
    masked_rows,
    out_grad,
):
    block_count, block_rows, width = tokens.shape
    quarter = block_rows // 4
    slots = masked_rows.shape[1]
    cap = slots // 4
    blocks = block_count // 2
    piece_rows = query_weight.shape[0]
    local = query_weight.shape[1]
    columns = 2 * local
    hidden_piece = up_weight.shape[1]
    head = lax.axis_index("head")
    c, p = head % 2, head // 2

    out_t = out_weight.T
    first, last = slice(0, 2 * HD), slice(2 * HD, 3 * HD)
    piece = jnp.concatenate(
        (
            query_weight[:, first],
            key_weight[:, first],
            value_weight[:, first],
            query_weight[:, last],
            key_weight[:, last],
            value_weight[:, last],
            out_t[:, last],
            out_t[:, first],
        ),
        axis=1,
    )
    half = piece_rows // 2

    def line(vector, size):
        return jnp.pad(vector, (0, size - vector.shape[0]))

    small = jnp.stack(
        [
            line(row, hidden_piece)
            for row in (
                query_bias,
                value_bias,
                jnp.repeat(block_order.astype(F32), HD),
                up_bias,
                out_bias,
                first_gain,
                first_shift,
                down_bias,
                second_gain,
                second_shift,
            )
        ]
        + [jnp.zeros((hidden_piece,), F32)] * 6
    )
    listed = pick(masked_rows.reshape(2, blocks, slots), p)
    (
        w_attn, w_feed, x_rows, rows_t, attention, keys, values, keys_used, values_used, q_compact, picks_b, select_b, small_far,
    ) = forward(tokens, piece, jnp.stack((up_weight, down_weight.T)), small, listed, c, p)

    out_y, gb, d_attention, d_branch_all, d_first, flat = middle(
        w_attn, w_feed, x_rows, attention, select_b, picks_b, out_grad, small, small_far
    )
    out_y = out_y.reshape(block_count, quarter, width)
    grad_x, s_attn, s_feed, summed = backward(
        gb, q_compact, d_attention, keys, values, keys_used, values_used, attention, rows_t, w_attn, select_b,
        small, small_far, d_branch_all, d_first, flat,
    )
    grad_x = grad_x.reshape(block_count, quarter, width)
    whole = summed[: flat.shape[0]].reshape(-1)
    ends, start = [], 0
    for size in [width] * 6 + [4 * hidden_piece]:
        ends.append(whole[start : start + size])
        start += size
    v_out_bias, v_first_gain, v_first_shift, v_down_bias, v_second_gain, v_second_shift, v_up_bias = ends
    last = summed[flat.shape[0] :].reshape(2, 2, 4, 128)
    v_query_bias, v_value_bias = (
        jnp.concatenate((last[0, i], last[1, i, :, :HD]), axis=-1).reshape(-1)
        for i in range(2)
    )

    def columns_of(i, j, second):
        at = 128 * j + HD * second
        return jnp.concatenate((s_attn[:, 128 * i : 128 * (i + 1)], s_attn[:, at : at + HD]), axis=1)

    return (
        out_y,
        grad_x,
        columns_of(0, 3, 0),
        v_query_bias,
        columns_of(1, 3, 1),
        columns_of(2, 4, 0),
        v_value_bias,
        columns_of(5, 4, 1).T,
        v_out_bias,
        v_first_gain,
        v_first_shift,
        s_feed[0],
        v_up_bias,
        s_feed[1].T,
        v_down_bias,
        v_second_gain,
        v_second_shift,
    )


def solution(mesh):
    in_specs = (
        P("dp", None, None),
        P("dp", "head"),
        P("head"),
        P("dp", "head"),
        P("dp", "head"),
        P("head"),
        P("head", "dp"),
        P(),
        P(),
        P(),
        P("dp", "head"),
        P("head"),
        P("head", "dp"),
        P(),
        P(),
        P(),
        P("head"),
        P("dp", None),
        P("dp", None, None),
    )
    out_specs = (
        P("dp", "head", None),
        P("dp", "head", None),
        P("dp", "head"),
        P(),
        P("dp", "head"),
        P("dp", "head"),
        P(),
        P("head", "dp"),
        P(),
        P(),
        P(),
        P("dp", "head"),
        P(),
        P("head", "dp"),
        P(),
        P(),
        P(),
    )
    return jax.shard_map(
        per_device, mesh=mesh, in_specs=in_specs, out_specs=out_specs, check_vma=False
    )
```

```python
import functools

import jax
import jax.numpy as jnp
from jax import lax
from jax.experimental import pallas as pl
from jax.experimental.pallas import tpu as pltpu
from jax.sharding import PartitionSpec as P

HEADS = 12
HD = 64
FF = 3072
EPSILON = 1e-12
F32 = jnp.float32
BF16 = jnp.bfloat16
SCALE = HD ** (-0.5)
MESH = pl.DeviceIdType.MESH


def flip(block, axis, bit):
    n = lax.axis_size(axis)
    return lax.ppermute(block, axis, [(i, i ^ bit) for i in range(n)])


def shift(block, axis, distance):
    n = lax.axis_size(axis)
    return lax.ppermute(block, axis, [(i, (i + distance) % n) for i in range(n)])


def sibling(block):
    return flip(block, "head", 1)


def across(block):
    return flip(block, "head", 2)


def partner(block):
    return shift(block, "dp", lax.axis_size("dp") // 2)


def pick(array, index, axis=0):
    return lax.dynamic_index_in_dim(array, index, axis, keepdims=False)


def ordered(low, own, other, axis=0):
    return jnp.stack(
        (jnp.where(low == 0, own, other), jnp.where(low == 0, other, own)), axis=axis
    )


def mm(a, b):
    return jnp.dot(a, b, preferred_element_type=F32)


def mm_t(a, b):
    return lax.dot_general(a, b, (((1,), (1,)), ((), ())), preferred_element_type=F32)


def t_mm(a, b):
    return lax.dot_general(a, b, (((0,), (0,)), ((), ())), preferred_element_type=F32)


def norm_parts(rows):
    centered = rows - jnp.mean(rows, axis=-1, keepdims=True)
    inverse = lax.rsqrt(jnp.mean(centered * centered, axis=-1, keepdims=True) + EPSILON)
    return centered * inverse, inverse


def norm_back(incoming, normed, inverse, gain):
    scaled = incoming * gain
    return inverse * (
        scaled
        - jnp.mean(scaled, axis=-1, keepdims=True)
        - normed * jnp.mean(scaled * normed, axis=-1, keepdims=True)
    )


def gaussian_parts(t):
    k = 1.0 / (1.0 + (0.3275911 * 0.5**0.5) * jnp.abs(t))
    bell = jnp.exp(-0.5 * t * t)
    series = 0.5 * 1.061405429
    for a in (-1.453152027, 1.421413741, -0.284496736, 0.254829592):
        series = series * k + 0.5 * a
    tail = series * k * bell
    return jnp.where(t < 0.0, tail, 1.0 - tail), bell


def gather(piece, x_first):
    n = lax.axis_size("dp")
    if n != 8:
        mine = lax.all_gather(piece, "dp", axis=0, tiled=False)
        return jnp.stack((mine, across(mine)))
    index = lax.axis_index("dp")
    z, x = index // 2, index % 2
    column = jnp.zeros((4,) + piece.shape, piece.dtype)
    column = lax.dynamic_update_index_in_dim(column, piece, z, 0)
    for k in (1, 2, 3):
        column = lax.dynamic_update_index_in_dim(
            column, shift(piece, "dp", 2 * k), (z - k) % 4, 0
        )
    if x_first:
        plane = ordered(x, column, flip(column, "dp", 1), axis=1)
        both = jnp.stack((plane, across(plane)))
    else:
        both = jnp.stack((column, across(column)))
        both = ordered(x, both, flip(both, "dp", 1), axis=2)
    return both.reshape((2, 8) + piece.shape)


def reduce_scatter(terms, x_last):
    n = lax.axis_size("dp")
    if n != 8:
        total = terms[0].astype(F32) + across(terms[1].astype(BF16)).astype(F32)
        return lax.psum_scatter(total, "dp", scatter_dimension=0, tiled=False)
    index = lax.axis_index("dp")
    z, x = index // 2, index % 2
    terms = terms.reshape((2, 4, 2) + terms.shape[2:])
    if x_last:
        arrived = across(terms[1])
        plane = (terms[0].astype(F32) + arrived.astype(F32)).astype(BF16)
        arrived = flip(pick(plane, 1 - x, 1), "dp", 1)
        column = pick(plane, x, 1).astype(F32) + arrived.astype(F32)
    else:
        arrived = flip(pick(terms, 1 - x, 2), "dp", 1)
        both = (pick(terms, x, 2).astype(F32) + arrived.astype(F32)).astype(BF16)
        column = both[0].astype(F32) + across(both[1]).astype(F32)
    column = column.astype(BF16)
    total = pick(column, z).astype(F32)
    for k in (1, 2, 3):
        total = total + shift(pick(column, (z + k) % 4), "dp", 2 * k).astype(F32)
    return total


def lane_masks(scale):
    lane = lax.broadcasted_iota(jnp.int32, (1, 2 * HD), 1)
    first = jnp.where(lane < HD, 1.0, 0.0)
    return [(first * scale).astype(BF16), ((1.0 - first) * scale).astype(BF16)]


def rows_of(ref):
    a, b, w = ref.shape
    return ref[...].reshape(a * b, w)


def pair_lanes(halves):
    lane = lax.broadcasted_iota(jnp.int32, halves[0].shape, 1)
    return jnp.where(lane < HD, halves[0], halves[1])


def halves_joined(low, high):
    lane = lax.broadcasted_iota(jnp.int32, low.shape, 1)
    return jnp.where(lane < HD, low, pltpu.roll(high, HD, 1))


def highs_joined(low, high):
    lane = lax.broadcasted_iota(jnp.int32, low.shape, 1)
    return jnp.where(lane < HD, pltpu.roll(low, HD, 1), high)


def head_tiles(row_own, row_other):
    return (
        row_own[:, :128],
        row_other[:, :128],
        halves_joined(row_own[:, 128:256], row_other[:, 128:256]),
    )


def heads_repeated(row):
    head = lax.div(lax.broadcasted_iota(jnp.int32, (1, 256), 1), HD)
    return sum(jnp.where(head == h, row[:, h : h + 1], 0.0) for h in range(3))


def project(x, wa_ref, count):
    width = x.shape[1]
    tiles = []
    for p in range(2):
        w = wa_ref[p].reshape(width, wa_ref.shape[-1])
        out = mm(x, w[:, count[0] : count[1]])
        tiles.append([out[:, 128 * i : 128 * (i + 1)] for i in range(out.shape[1] // 128)])
    return tiles


def forward_own(b, x_ref, wa_ref, bias, q_ref, k_ref, v_ref):
    rows = x_ref.shape[2] * x_ref.shape[3] * 2
    x = x_ref[:, b].reshape(rows, x_ref.shape[-1])
    one, two = project(x, wa_ref, (0, 640))
    b_query, b_value = bias
    parts = (
        (q_ref, (one[0], two[0], halves_joined(one[3], two[3])), b_query),
        (k_ref, (one[1], two[1], highs_joined(one[3], two[3])), None),
        (v_ref, (one[2], two[2], halves_joined(one[4], two[4])), b_value),
    )
    for ref, tiles, added in parts:
        for t in range(3):
            tile = tiles[t] if added is None else tiles[t] + added[t]
            ref[:, b, :, 128 * t : 128 * (t + 1)] = tile.astype(BF16).reshape(2, rows // 2, 128)


def forward_attend(b, xp_ref, wa_ref, bias, swapped, q_ref, k_ref, v_ref, ku_ref, vu_ref, o_ref):
    rows = xp_ref.shape[2] * xp_ref.shape[3] * 2
    x = xp_ref[:, b].reshape(rows, xp_ref.shape[-1])
    one, two = project(x, wa_ref, (128, 640))
    far_keys = (one[0], two[0], highs_joined(one[2], two[2]))
    far_values = (one[1], two[1], halves_joined(one[3], two[3]))
    masks = lane_masks(SCALE)
    for t in range(3):
        lanes = slice(128 * t, 128 * (t + 1))

        def load(ref):
            return ref[:, b, :, lanes].reshape(rows, 128)

        take_far = swapped[t] > 0.5
        k = jnp.where(take_far, far_keys[t], load(k_ref).astype(F32)).astype(BF16)
        v = jnp.where(
            take_far, far_values[t] + bias[1][t], load(v_ref).astype(F32)
        ).astype(BF16)
        ku_ref[:, b, :, lanes] = k.reshape(2, rows // 2, 128)
        vu_ref[:, b, :, lanes] = v.reshape(2, rows // 2, 128)
        q = load(q_ref)
        outs = []
        for mask in masks:
            s = mm_t(q * mask, k)
            raised = jnp.exp(s - jnp.max(s, axis=-1, keepdims=True))
            total = jnp.sum(raised, axis=-1, keepdims=True)
            outs.append(mm(raised.astype(BF16), v) / total)
        o_ref[:, b, :, lanes] = pair_lanes(outs).astype(BF16).reshape(2, rows // 2, 128)


def forward_listed(b, member, pair, listed_ref, q_ref, picks_ref, select_ref, qc_ref):
    slots = listed_ref.shape[-1]
    quarter = q_ref.shape[2] // 2
    cap = slots // 4
    row = listed_ref[pl.ds(q_ref.shape[1] * pair + b, 1), :]
    col = jnp.broadcast_to(row.astype(F32), (slots, slots)).T[:, 0:1].astype(jnp.int32)
    bits = quarter.bit_length() - 1
    run_row = lax.shift_right_arithmetic(row, bits)
    run_col = lax.shift_right_arithmetic(col, bits)
    before = lax.broadcasted_iota(jnp.int32, (slots, slots), 0) < lax.broadcasted_iota(
        jnp.int32, (slots, slots), 1
    )
    same = jnp.where(run_col == run_row, jnp.where(before, 1.0, 0.0), 0.0)
    rank = jnp.sum(same, axis=0, keepdims=True)
    line = lax.broadcasted_iota(jnp.int32, (slots, 1), 0)
    place = line // cap
    wanted_run = jnp.where(
        place == 0, member, jnp.where(place == 1, member + 2, jnp.where(place == 2, 1 - member, 3 - member))
    )
    wanted_rank = (line % cap).astype(F32)
    picks = jnp.where(run_row == wanted_run, jnp.where(rank == wanted_rank, 1.0, 0.0), 0.0).astype(BF16)
    lane = lax.broadcasted_iota(jnp.int32, (slots, quarter), 1)
    places = jnp.where(jnp.bitwise_and(col, quarter - 1) == lane, 1.0, 0.0).astype(BF16)
    select = mm(picks, places).astype(BF16)
    picks_ref[b] = picks
    select_ref[b] = select
    for s in range(2):
        for e in range(2):
            at = (2 * s + e) * cap
            rows = q_ref[s, b, quarter * e : quarter * (e + 1), :]
            qc_ref[s, b, cap * e : cap * (e + 1), :] = mm(select[at : at + cap], rows).astype(BF16)


def pack_piece(query_ref, key_ref, value_ref, out_ref, a_ref):
    out = out_ref[...].T
    query, key, value = query_ref[...], key_ref[...], value_ref[...]
    for i, tile in enumerate((query, key, value)):
        a_ref[:, 128 * i : 128 * (i + 1)] = tile[:, 0:128]
    a_ref[:, 384:512] = jnp.concatenate((query[:, 128:192], key[:, 128:192]), axis=1)
    a_ref[:, 512:640] = jnp.concatenate((value[:, 128:192], out[:, 128:192]), axis=1)
    a_ref[:, 640:768] = out[:, 0:128]


def forward_kernel(comm, *refs):
    if comm:
        (
            query_ref, key_ref, value_ref, out_ref, up_ref, down_ref, t_ref, small_ref, listed_ref,
            wa_ref, wb_ref, x_ref, xt_ref, o_ref, k_ref, v_ref, ku_ref, vu_ref, qc_ref, picks_ref, select_ref, far_ref,
            a_ref, b_ref, xp_ref, q_ref, local_sem, send_sem, recv_sem,
        ) = refs
    else:
        (
            wa_ref, x_ref, xp_ref, small_ref, far_ref, listed_ref,
            xt_ref, o_ref, k_ref, v_ref, ku_ref, vu_ref, qc_ref, picks_ref, select_ref,
            q_ref,
        ) = refs
    blocks = x_ref.shape[1]
    head = lax.axis_index("head")
    member, pair = lax.rem(head, 2), lax.div(head, 2)

    def listed(b, carry):
        forward_listed(b, member, pair, listed_ref, q_ref, picks_ref, select_ref, qc_ref)
        return carry

    def turned(i, carry):
        s, rest = lax.div(i, 2 * blocks), lax.rem(i, 2 * blocks)
        part = x_ref[s, lax.div(rest, 2), lax.rem(rest, 2)]
        quarter = part.shape[0]
        xt_ref[:, pl.ds(pl.multiple_of(i * quarter, quarter), quarter)] = part.T
        return carry

    def bias_of():
        own, other = small_ref[...], far_ref[...]
        rows = [head_tiles(own[i : i + 1], other[i : i + 1]) for i in range(2)]
        order = head_tiles(heads_repeated(own[2:3]), heads_repeated(other[2:3]))
        return (rows[0], rows[1]), order

    if not comm:
        bias, swapped = bias_of()
        lax.fori_loop(0, 4 * blocks, turned, 0)

        def own_block(b, carry):
            forward_own(b, x_ref, wa_ref, bias, q_ref, k_ref, v_ref)
            return carry

    if comm:
        index = lax.axis_index("dp")
        z, x = lax.div(index, 2), lax.rem(index, 2)
        x_peer = {"dp": 2 * z + 1 - x}
        y_peer = {"head": lax.rem(head + 2, 4)}
        sibling_peer = {"head": 2 * pair + 1 - member}
        z_next = z + 1 - 2 * lax.rem(z, 2)
        z_far = lax.rem(z + 2, 4)
        next_peer, far_peer = {"dp": 2 * z_next + x}, {"dp": 2 * z_far + x}
        barrier = pltpu.get_barrier_semaphore()
        for peer in (x_peer, y_peer, sibling_peer, next_peer, far_peer):
            pl.semaphore_signal(barrier, inc=1, device_id=peer, device_id_type=MESH)
        counter = [0]

        def local(src, dst, i):
            copy = pltpu.make_async_copy(src, dst, local_sem.at[i])
            copy.start()
            return copy

        def send(src, dst, peer):
            i = counter[0]
            counter[0] += 1
            copy = pltpu.make_async_remote_copy(
                src_ref=src,
                dst_ref=dst,
                send_sem=send_sem.at[i],
                recv_sem=recv_sem.at[i],
                device_id=peer,
                device_id_type=MESH,
            )
            copy.start()
            sent.append(copy)
            return copy

        def far_copy(b):
            return pltpu.make_async_remote_copy(
                src_ref=x_ref.at[0, b],
                dst_ref=xp_ref.at[0, b],
                send_sem=send_sem.at[15 + b],
                recv_sem=recv_sem.at[15 + b],
                device_id=far_peer,
                device_id_type=MESH,
            )

        def near_copy(b):
            return pltpu.make_async_remote_copy(
                src_ref=xp_ref.at[0, b],
                dst_ref=xp_ref.at[1, b],
                send_sem=send_sem.at[15 + blocks + b],
                recv_sem=recv_sem.at[15 + blocks + b],
                device_id=sibling_peer,
                device_id_type=MESH,
            )

        sent = []
        quarters = (member, member + 2, 1 - member, 3 - member)
        fills = [
            local(t_ref.at[pl.ds(blocks * pair, blocks), quarters[2 * s + e]], x_ref.at[s, :, e], 2 * s + e)
            for s in range(2)
            for e in range(2)
        ]
        pack_piece(query_ref, key_ref, value_ref, out_ref, a_ref)
        fill_a = local(a_ref, wa_ref.at[0, z, x], 4)
        pl.semaphore_wait(barrier, 5)
        a_next = send(a_ref, wa_ref.at[0, z, x], next_peer)
        a_far = send(a_ref, wa_ref.at[0, z, x], far_peer)
        far = send(small_ref, far_ref, y_peer)
        b_ref[0] = up_ref[...]
        b_ref[1] = down_ref[...]
        fill_b = local(b_ref, wb_ref.at[0, :, z, x], 5)
        b_far = send(b_ref, wb_ref.at[0, :, z, x], far_peer)
        for fill in fills:
            fill.wait()
        lax.fori_loop(0, 4 * blocks, turned, 0)
        a_far.wait_recv()
        a_pass = send(wa_ref.at[0, z_far, x], wa_ref.at[0, z_far, x], next_peer)
        b_next = send(b_ref, wb_ref.at[0, :, z, x], next_peer)
        far_copy(0).start()
        half = a_ref.shape[0] // 2
        up, low = pl.ds(0, half), pl.ds(half, half)
        fill_a.wait()
        a_next.wait_recv()
        a_pass.wait_recv()
        a_x = send(wa_ref.at[0, :, x, up], wa_ref.at[0, :, x, up], x_peer)
        a_y = send(wa_ref.at[0, :, x, low], wa_ref.at[1, :, x, low], y_peer)
        b_far.wait_recv()
        b_pass = send(wb_ref.at[0, :, z_far, x], wb_ref.at[0, :, z_far, x], next_peer)
        for b in range(1, blocks):
            far_copy(b).start()
        a_x.wait_recv()
        a_xy = send(wa_ref.at[0, :, :, up], wa_ref.at[1, :, :, up], y_peer)
        a_y.wait_recv()
        a_yx = send(wa_ref.at[:, :, x, low], wa_ref.at[:, :, x, low], x_peer)
        fill_b.wait()
        b_next.wait_recv()
        b_pass.wait_recv()
        b_x = send(wb_ref.at[0, 0, :, x], wb_ref.at[0, 0, :, x], x_peer)
        b_y = send(wb_ref.at[0, 1, :, x], wb_ref.at[1, 1, :, x], y_peer)
        far.wait_recv()
        a_xy.wait_recv()
        a_yx.wait_recv()
        bias, swapped = bias_of()

        def own_block(b, carry):
            forward_own(b, x_ref, wa_ref, bias, q_ref, k_ref, v_ref)
            return carry

    lax.fori_loop(0, blocks, own_block, 0)
    lax.fori_loop(0, blocks, listed, 0)
    if comm:

        def attend_block(b, carry):
            far_copy(b).wait_recv()
            near = near_copy(b)
            near.start()
            near.wait_recv()
            forward_attend(b, xp_ref, wa_ref, bias, swapped, q_ref, k_ref, v_ref, ku_ref, vu_ref, o_ref)
            return carry

        lax.fori_loop(0, 1, attend_block, 0)
        b_x.wait_recv()
        b_xy = send(wb_ref.at[0, 0], wb_ref.at[1, 0], y_peer)
        b_y.wait_recv()
        b_yx = send(wb_ref.at[:, 1, :, x], wb_ref.at[:, 1, :, x], x_peer)
        lax.fori_loop(1, blocks, attend_block, 0)
        b_xy.wait_recv()
        b_yx.wait_recv()
        for copy in sent:
            copy.wait_send()
        for b in range(blocks):
            far_copy(b).wait_send()
            near_copy(b).wait_send()
    else:

        def attend_block(b, carry):
            forward_attend(b, xp_ref, wa_ref, bias, swapped, q_ref, k_ref, v_ref, ku_ref, vu_ref, o_ref)
            return carry

        lax.fori_loop(0, blocks, attend_block, 0)


def vmem_spec():
    return pl.BlockSpec(memory_space=pltpu.VMEM)


def any_spec():
    return pl.BlockSpec(memory_space=pl.ANY)


def forward(tokens, weights, small, listed, member, pair):
    n = lax.axis_size("dp")
    block_count, block_rows, width = tokens.shape
    blocks, quarter = block_count // 2, block_rows // 4
    slots = listed.shape[1]
    cap = slots // 4
    lanes = 6 * HD
    tokens = tokens.reshape(block_count, 4, quarter, width)
    query, key, value, out_weight, up_weight, down_weight = weights
    piece_rows, hidden = up_weight.shape
    rows_shape = (2, blocks, 2, quarter, width)

    def out(*shape, dtype=BF16):
        return jax.ShapeDtypeStruct(shape, dtype)

    dense = (2, blocks, 2 * quarter, lanes)
    tail = [out(width, 2 * blocks * 2 * quarter)] + [out(*dense)] * 5 + [
        out(2, blocks, 2 * cap, lanes),
        out(blocks, slots, slots),
        out(blocks, slots, quarter),
    ]
    params = dict(vmem_limit_bytes=60 * 2**20, has_side_effects=True)
    if n == 8:
        shapes = [
            out(2, 4, 2, piece_rows, 12 * HD),
            out(2, 2, 4, 2, piece_rows, hidden),
            out(*rows_shape),
            *tail,
            out(*small.shape, dtype=F32),
        ]
        specs = [vmem_spec()] * len(shapes)
        specs[1] = any_spec()
        results = pl.pallas_call(
            functools.partial(forward_kernel, True),
            out_shape=shapes,
            in_specs=[vmem_spec()] * 6 + [any_spec()] + [vmem_spec()] * 2,
            out_specs=specs,
            scratch_shapes=[
                pltpu.VMEM((piece_rows, 12 * HD), BF16),
                pltpu.VMEM((2, piece_rows, hidden), BF16),
                pltpu.VMEM(rows_shape, BF16),
                pltpu.VMEM(dense, BF16),
                pltpu.SemaphoreType.DMA((6,)),
                pltpu.SemaphoreType.DMA((15 + 2 * blocks,)),
                pltpu.SemaphoreType.DMA((15 + 2 * blocks,)),
            ],
            compiler_params=pltpu.CompilerParams(collective_id=1, **params),
        )(*weights, tokens, small, listed)
        w_attn, w_feed, rows, *rest, far = results
    else:
        mine = pick(tokens.reshape(2, blocks, 2, 2, quarter, width), pair)
        rows = jnp.stack((pick(mine, member, 2), pick(mine, 1 - member, 2)))
        out_t = out_weight.T
        first, last = slice(0, 2 * HD), slice(2 * HD, 3 * HD)
        piece_a = jnp.concatenate(
            [part[:, first] for part in (query, key, value)]
            + [part[:, last] for part in (query, key, value, out_t)]
            + [out_t[:, first]],
            axis=1,
        )
        w_attn = gather(piece_a, True)
        w_feed = jnp.stack([gather(piece, True) for piece in (up_weight, down_weight)], axis=1)
        far = across(small)
        shapes = tail
        rest = pl.pallas_call(
            functools.partial(forward_kernel, False),
            out_shape=shapes,
            in_specs=[vmem_spec()] * 6,
            out_specs=[vmem_spec()] * len(shapes),
            scratch_shapes=[pltpu.VMEM(dense, BF16)],
            compiler_params=pltpu.CompilerParams(vmem_limit_bytes=60 * 2**20),
        )(w_attn.reshape(2, width, -1), rows, partner(rows), small, far, listed)
    w_attn = w_attn.reshape(2, width, -1)
    w_feed = w_feed.reshape(2, 2, width, -1)
    return (w_attn, w_feed, rows, *rest, far)


OUT_BIAS, FIRST_GAIN, FIRST_SHIFT, DOWN_BIAS, SECOND_GAIN, SECOND_SHIFT = range(4, 10)


def picked(chosen, rows):
    high = rows.astype(BF16)
    rest = (rows - high.astype(F32)).astype(BF16)
    return mm(chosen, high) + mm(chosen, rest)


def column_sum(rows):
    return jnp.sum(rows, axis=0, keepdims=True)


def middle_kernel(
    wa_ref, wf_in, x_in, attn_ref, select_ref, picks_ref, grads_in, small_ref, far_ref, qc_ref,
    y_ref, gb_ref, da_ref, db_ref, df_ref, vec_ref, qf_ref,
    wf, xs, gs, wo, ao, hid, hl, hc, one_c, pre, act, feeds, ft_out, ft_in, rows_ref, ds, dfd, turned_h, turned_d,
    d_act, d_pre, term, dt_out, dt_in, acc, local_sem, send_sem, recv_sem,
):
    blocks, half, width = hid.shape
    quarter = half // 2
    cap = df_ref.shape[1] // 2
    own = blocks * 2 * cap
    head = lax.axis_index("head")
    member, pair = lax.rem(head, 2), lax.div(head, 2)
    sibling_peer = {"head": 2 * pair + 1 - member}
    y_peer = {"head": lax.rem(head + 2, 4)}
    devices = lax.axis_size("dp")
    partner_peer = {"dp": lax.rem(lax.axis_index("dp") + devices // 2, devices)}
    barrier = pltpu.get_barrier_semaphore()
    for peer in (sibling_peer, y_peer, partner_peer):
        pl.semaphore_signal(barrier, inc=1, device_id=peer, device_id_type=MESH)
    sent = []

    def remote(src, dst, peer, i):
        return pltpu.make_async_remote_copy(
            src_ref=src,
            dst_ref=dst,
            send_sem=send_sem.at[i],
            recv_sem=recv_sem.at[i],
            device_id=peer,
            device_id_type=MESH,
        )

    def send(src, dst, peer):
        copy = remote(src, dst, peer, 2 * blocks + len(sent))
        copy.start()
        sent.append(copy)
        return copy

    def local(src, dst, i):
        copy = pltpu.make_async_copy(src, dst, local_sem.at[i])
        copy.start()
        return copy

    def hidden_copy(b):
        return remote(hl.at[0, b], hl.at[1, b], sibling_peer, b)

    def feed_copy(b):
        return remote(ft_out.at[b], ft_in.at[b], sibling_peer, blocks + b)

    def vector(i):
        return small_ref[i : i + 1, :]

    up_biases = (small_ref, far_ref)

    fill_x = local(x_in.at[0], xs, 0)
    fill_w = local(wf_in, wf, 1)
    fill_g = local(grads_in.at[pl.ds(blocks * pair, blocks)], gs, 2)
    pl.semaphore_wait(barrier, 3)
    far_queries = send(qc_ref, qf_ref, partner_peer)
    other_rows = send(attn_ref.at[1], ao, sibling_peer)
    for p in range(2):
        wo[0, :, 128 * p : 128 * (p + 1)] = wa_ref[p, :, 640:768]
    wo[0, :, 256:384] = highs_joined(
        wa_ref[0, :, 512:640].astype(F32), wa_ref[1, :, 512:640].astype(F32)
    ).astype(BF16)
    other_weights = send(wo.at[0], wo.at[1], sibling_peer)

    def branch_own(b, carry):
        feeds[b] = mm_t(attn_ref[0, b], wo[0])
        return carry

    lax.fori_loop(0, blocks, branch_own, 0)
    acc[...] = jnp.zeros_like(acc)
    fill_x.wait()
    other_rows.wait_recv()
    other_weights.wait_recv()

    def first_norm(b, carry):
        rows = xs[b].reshape(half, width).astype(F32) + feeds[b] + mm_t(ao[b], wo[1]) + vector(OUT_BIAS)
        hidden = norm_parts(rows)[0] * vector(FIRST_GAIN) + vector(FIRST_SHIFT)
        low = hidden.astype(BF16)
        hid[b] = hidden
        hl[0, b] = low
        hidden_copy(b).start()
        for e in range(2):
            at, run = slice(cap * e, cap * (e + 1)), slice(quarter * e, quarter * (e + 1))
            chosen = select_ref[b, at, :]
            one_c[b, at, :] = picked(chosen, rows[run])
            hc[0, b, at, :] = mm(chosen, low[run]).astype(BF16)
        return carry

    lax.fori_loop(0, blocks, first_norm, 0)
    other_listed = send(hc.at[0], hc.at[1], sibling_peer)
    fill_w.wait()

    def gelu_rows(i, carry):
        at = pl.ds(pl.multiple_of(16 * i, 16), 16)
        t = pre[at, :]
        act[0, at, :] = (t * gaussian_parts(t)[0]).astype(BF16)
        return carry

    def feed(s, b):
        out = 0.0
        for p in range(2):
            pre[0:half] = mm(hl[s, b], wf[p, 0]) + up_biases[p][3:4, :]
            lax.fori_loop(0, half // 16, gelu_rows, 0, unroll=2)
            out = out + mm_t(act[0, 0:half], wf[p, 1])
        return out

    def feed_other(b, carry):
        hidden_copy(b).wait_recv()
        ft_out[b] = feed(1, b).astype(BF16)
        feed_copy(b).start()
        return carry

    lax.fori_loop(0, blocks, feed_other, 0)

    def feed_own(b, carry):
        feeds[b] = feed(0, b)
        return carry

    lax.fori_loop(0, blocks, feed_own, 0)
    fill_g.wait()

    def second_norm(b, carry):
        feed_copy(b).wait_recv()
        rows = hid[b] + feeds[b] + ft_in[b].astype(F32) + vector(DOWN_BIAS)
        out = (norm_parts(rows)[0] * vector(SECOND_GAIN) + vector(SECOND_SHIFT)).astype(BF16)
        listed = []
        for e in range(2):
            at, run = slice(cap * e, cap * (e + 1)), slice(quarter * e, quarter * (e + 1))
            rows_ref[e, b] = out[run]
            listed.append(picked(select_ref[b, at, :], rows[run]))
        normed, inverse = norm_parts(jnp.concatenate(listed, axis=0))
        grad_y = mm(picks_ref[b, 0 : 2 * cap, :], gs[b])
        d_second = norm_back(grad_y, normed, inverse, vector(SECOND_GAIN))
        d_feed = d_second.astype(BF16)
        ds[b] = d_second
        dfd[0, b] = d_feed
        acc[3:4] += column_sum(d_feed.astype(F32))
        acc[4:5] += column_sum(grad_y * normed)
        acc[5:6] += column_sum(grad_y)
        return carry

    lax.fori_loop(0, blocks, second_norm, 0)
    other_d = send(dfd.at[0], dfd.at[1], sibling_peer)
    moved = send(rows_ref.at[1 - pair], y_ref.at[pair], y_peer)
    kept = local(rows_ref.at[pair], y_ref.at[pair], 3)

    other_listed.wait_recv()

    def turn(ref, out):
        flat = ref[...].reshape(2 * own, width)
        for i in range(2 * own // 128):
            out[:, 128 * i : 128 * (i + 1)] = flat[128 * i : 128 * (i + 1)].T

    turn(hc, turned_h)
    other_d.wait_recv()
    turn(dfd, turned_d)

    for p in range(2):
        pre[...] = mm(hc[...].reshape(2 * own, width), wf[p, 0]) + up_biases[p][3:4, :]
        d_act[...] = mm(dfd[...].reshape(2 * own, width), wf[p, 1])

        def back_rows_of(i, total):
            at = pl.ds(pl.multiple_of(16 * i, 16), 16)
            t = pre[at, :]
            cdf, bell = gaussian_parts(t)
            act[p, at, :] = (t * cdf).astype(BF16)
            d = (d_act[at, :] * (cdf + t * (bell * (0.5 / jnp.pi) ** 0.5))).astype(BF16)
            d_pre[p, at, :] = d
            d = d.astype(F32)
            return total + (d[0:8] + d[8:16])

        total = lax.fori_loop(0, 2 * own // 16, back_rows_of, jnp.zeros((8, width), F32))
        acc[6 + p : 7 + p] = column_sum(total)
        part = mm_t(d_pre[p], wf[p, 0])
        if p == 0:
            term[...] = part
        else:
            part = part + term[...]
            dt_out[...] = part[own:].astype(BF16)
            other_term = send(dt_out, dt_in, sibling_peer)
            term[0:own] = part[:own]

    gb_ref[0, 0] = mm(turned_h[...], d_pre[0]).astype(BF16)
    other_term.wait_recv()

    def first_back(b, carry):
        at = pl.ds(pl.multiple_of(2 * cap * b, 2 * cap), 2 * cap)
        d_hidden = ds[b] + term[at, :] + dt_in[at, :].astype(F32)
        normed, inverse = norm_parts(one_c[b])
        d_first = norm_back(d_hidden, normed, inverse, vector(FIRST_GAIN))
        d_branch = d_first.astype(BF16)
        df_ref[b] = d_first
        db_ref[0, b] = d_branch
        acc[0:1] += column_sum(d_branch.astype(F32))
        acc[1:2] += column_sum(d_hidden * normed)
        acc[2:3] += column_sum(d_hidden)
        return carry

    lax.fori_loop(0, blocks, first_back, 0)
    other_branch = send(db_ref.at[0], db_ref.at[1], sibling_peer)
    gb_ref[0, 1] = mm(turned_d[...], act[0]).astype(BF16)
    gb_ref[1, 0] = mm(turned_h[...], d_pre[1]).astype(BF16)
    gb_ref[1, 1] = mm(turned_d[...], act[1]).astype(BF16)
    tiles = width // 128
    vec_ref[...] = jnp.zeros_like(vec_ref)
    for t in range(tiles):
        lanes = slice(128 * t, 128 * (t + 1))
        for i in range(6):
            vec_ref[tiles * i + t : tiles * i + t + 1, :] = acc[i : i + 1, lanes]
        for h in range(4):
            mine = jnp.where(head == h, acc[6:7, lanes], 0.0)
            other = jnp.where(lax.rem(head + 2, 4) == h, acc[7:8, lanes], 0.0)
            at = tiles * (6 + h) + t
            vec_ref[at : at + 1, :] = mine + other
    other_branch.wait_recv()
    for s in range(2):
        da = mm(db_ref[s].reshape(own, width), wo[0])
        da_ref[s] = da.astype(BF16).reshape(da_ref.shape[1:])
    kept.wait()
    moved.wait_recv()
    far_queries.wait_recv()
    for copy in sent:
        copy.wait_send()
    for b in range(blocks):
        hidden_copy(b).wait_send()
        feed_copy(b).wait_send()


def middle(w_attn, w_feed, x_rows, attention, select, picks, out_grad, small, far, q_compact):
    _, blocks, block_half, lanes = attention.shape
    width = w_attn.shape[1]
    quarter = block_half // 2
    listed = select.shape[1] // 2
    own = blocks * listed

    def out(*shape, dtype=BF16):
        return jax.ShapeDtypeStruct(shape, dtype)

    def room(*shape, dtype=BF16):
        return pltpu.VMEM(shape, dtype)

    in_specs = [vmem_spec()] * 10
    for i in (1, 2, 6):
        in_specs[i] = any_spec()
    return pl.pallas_call(
        middle_kernel,
        out_shape=[
            out(2, blocks, quarter, width),
            out(*w_feed.shape),
            out(2, blocks, listed, lanes),
            out(2, blocks, listed, width),
            out(blocks, listed, width, dtype=F32),
            out(64, 128, dtype=F32),
            out(*q_compact.shape),
        ],
        in_specs=in_specs,
        out_specs=[vmem_spec()] * 7,
        scratch_shapes=[
            room(*w_feed.shape),
            room(blocks, 2, quarter, width),
            room(blocks, *out_grad.shape[1:]),
            room(2, width, lanes),
            room(blocks, block_half, lanes),
            room(blocks, block_half, width, dtype=F32),
            room(2, blocks, block_half, width),
            room(2, blocks, listed, width),
            room(blocks, listed, width, dtype=F32),
            room(2 * own, width, dtype=F32),
            room(2, 2 * own, width),
            room(blocks, block_half, width, dtype=F32),
            room(blocks, block_half, width),
            room(blocks, block_half, width),
            room(2, blocks, quarter, width),
            room(blocks, listed, width, dtype=F32),
            room(2, blocks, listed, width),
            room(width, 2 * own),
            room(width, 2 * own),
            room(2 * own, width, dtype=F32),
            room(2, 2 * own, width),
            room(2 * own, width, dtype=F32),
            room(own, width),
            room(own, width),
            room(8, width, dtype=F32),
            pltpu.SemaphoreType.DMA((4,)),
            pltpu.SemaphoreType.DMA((2 * blocks + 8,)),
            pltpu.SemaphoreType.DMA((2 * blocks + 8,)),
        ],
        compiler_params=pltpu.CompilerParams(
            collective_id=3, vmem_limit_bytes=60 * 2**20, has_side_effects=True
        ),
    )(w_attn, w_feed, x_rows, attention, select, picks, out_grad, small, far, q_compact)


def back_queries(b, qc_ref, g_ref, ku_ref, vu_ref, select_ref, o_ref, dt_ref, oc_ref, total_ref):
    rows = ku_ref.shape[2] * 2
    slots = qc_ref.shape[2] * 2
    cap = slots // 4
    quarter = rows // 4
    select = select_ref[b]
    tiles = []
    for t in range(3):
        lanes = slice(128 * t, 128 * (t + 1))
        q = qc_ref[:, b, :, lanes].reshape(slots, 128)
        g = g_ref[:, b, :, lanes].reshape(slots, 128)
        k = ku_ref[:, b, :, lanes].reshape(rows, 128)
        v = vu_ref[:, b, :, lanes].reshape(rows, 128)
        outs = []
        for mask, one in zip(lane_masks(SCALE), lane_masks(1.0)):
            s = mm_t(q * mask, k)
            raised = jnp.exp(s - jnp.max(s, axis=-1, keepdims=True))
            probs = raised / jnp.sum(raised, axis=-1, keepdims=True)
            d_probs = mm_t(g * one, v)
            inner = jnp.sum(d_probs * probs, axis=-1, keepdims=True)
            d_scores = (probs * (d_probs - inner)).astype(BF16)
            outs.append(mm(d_scores, k) * SCALE)
        tile = pair_lanes(outs).astype(BF16)
        total_ref[0:1, lanes] += jnp.sum(tile.astype(F32), axis=0, keepdims=True)
        tiles.append(tile)
    for s in range(2):
        for e in range(2):
            at = (2 * s + e) * cap
            chosen = select[at : at + cap]
            own = slice(quarter * e, quarter * (e + 1))
            dense = [t_mm(chosen, tile[at : at + cap]) for tile in tiles]
            dt_ref[0, s, b, own, 0:128] = dense[0].astype(BF16)
            dt_ref[1, s, b, own, 0:128] = dense[1].astype(BF16)
            lane = lax.broadcasted_iota(jnp.int32, dense[2].shape, 1)
            for p in range(2):
                last = dense[2] if p == 0 else pltpu.roll(dense[2], HD, 1)
                dt_ref[p, s, b, own, 384:512] = jnp.where(lane < HD, last, 0.0).astype(BF16)
            rows_o = mm(chosen, o_ref[s, b, own, :])
            at_o = slice(cap * e, cap * (e + 1))
            lane = lax.broadcasted_iota(jnp.int32, (cap, 128), 1)
            for p in range(2):
                oc_ref[p, s, b, at_o, 128:256] = rows_o[:, 128 * p : 128 * (p + 1)].astype(BF16)
                last = rows_o[:, 256:384] if p == 1 else pltpu.roll(rows_o[:, 256:384], HD, 1)
                oc_ref[p, s, b, at_o, 0:128] = jnp.where(lane < HD, 0.0, last).astype(BF16)


def back_keys(b, swapped, qc_ref, g_ref, qf_ref, gf_ref, k_ref, v_ref, dt_ref, total_ref):
    rows = k_ref.shape[2] * 2
    slots = qc_ref.shape[2] * 2
    for t in range(3):
        lanes = slice(128 * t, 128 * (t + 1))
        take_far = swapped[t] > 0.5

        def chosen(near, far):
            near = near[:, b, :, lanes].reshape(slots, 128).astype(F32)
            far = far[:, b, :, lanes].reshape(slots, 128).astype(F32)
            return jnp.where(take_far, far, near).astype(BF16)

        q, g = chosen(qc_ref, qf_ref), chosen(g_ref, gf_ref)
        k = k_ref[:, b, :, lanes].reshape(rows, 128)
        v = v_ref[:, b, :, lanes].reshape(rows, 128)
        d_keys, d_values = [], []
        for mask, one in zip(lane_masks(SCALE), lane_masks(1.0)):
            s = mm_t(k, q * mask)
            raised = jnp.exp(s - jnp.max(s, axis=0, keepdims=True))
            probs = raised / jnp.sum(raised, axis=0, keepdims=True)
            d_probs = mm_t(v, g * one)
            inner = jnp.sum(d_probs * probs, axis=0, keepdims=True)
            d_scores = (probs * (d_probs - inner)).astype(BF16)
            d_keys.append(mm(d_scores, q) * SCALE)
            d_values.append(mm(probs.astype(BF16), g))
        dk, dv = pair_lanes(d_keys), pair_lanes(d_values)
        total_ref[1:2, lanes] += jnp.sum(dv.astype(BF16).astype(F32), axis=0, keepdims=True)
        half = (2, rows // 2, 128)
        if t < 2:
            dt_ref[t, :, b, :, 128:256] = dk.astype(BF16).reshape(half)
            dt_ref[t, :, b, :, 256:384] = dv.astype(BF16).reshape(half)
        else:
            lane = lax.broadcasted_iota(jnp.int32, dk.shape, 1)
            for p in range(2):
                last = pltpu.roll(dk, HD, 1) if p == 0 else dk
                before = dt_ref[p, :, b, :, 384:512].reshape(rows, 128).astype(F32)
                dt_ref[p, :, b, :, 384:512] = (
                    jnp.where(lane < HD, before, last).astype(BF16).reshape(half)
                )
                last = dv if p == 0 else pltpu.roll(dv, HD, 1)
                dt_ref[p, :, b, :, 512:640] = (
                    jnp.where(lane < HD, last, 0.0).astype(BF16).reshape(half)
                )


def back_weights(p, xt_ref, dt_ref, db_ref, oc_ref, ga_ref):
    width = xt_ref.shape[0]
    shape = ga_ref.shape[1:-1] + (128,)
    listed = db_ref.shape[0] * db_ref.shape[1] * db_ref.shape[2]
    d_branch = db_ref[...].reshape(listed, width)
    outs = mm(xt_ref[...], dt_ref[p].reshape(xt_ref.shape[1], 640))
    extra = t_mm(d_branch, oc_ref[p].reshape(listed, 256))
    for i in range(6):
        if i < 4:
            tile = outs[:, 128 * i : 128 * (i + 1)]
        elif i == 4:
            tile = outs[:, 512:640] + extra[:, 0:128]
        else:
            tile = extra[:, 128:256]
        ga_ref[p, ..., 128 * i : 128 * (i + 1)] = tile.astype(BF16).reshape(shape)


def back_rows(s, b, wa_ref, dt_ref):
    rows, width = dt_ref.shape[3], wa_ref.shape[-1]
    out = 0.0
    for p in range(2):
        w = wa_ref[p].reshape(-1, wa_ref.shape[-1])
        out = out + mm_t(dt_ref[p, s, b], w[:, 0:640])
    return out


def bias_totals(member, pair, total_ref):
    lane = lax.broadcasted_iota(jnp.int32, (1, 128), 1)
    line = lax.broadcasted_iota(jnp.int32, (8, 128), 0)
    first = jnp.zeros((8, 128), F32)
    second = jnp.zeros((8, 128), F32)
    for i in range(2):
        last = total_ref[i : i + 1, 256:384]
        for p in range(2):
            place = 4 * i + 2 * (pair if p == 0 else 1 - pair) + member
            tile = total_ref[i : i + 1, 128 * p : 128 * (p + 1)]
            third = last if p == 0 else pltpu.roll(last, HD, 1)
            first = first + jnp.where(line == place, tile, 0.0)
            second = second + jnp.where(line == place, jnp.where(lane < HD, third, 0.0), 0.0)
    return first, second


def store_vectors(total, refs):
    at = 0
    rows = total.shape[0] - 16
    for ref in refs[:7]:
        for t in range(ref.shape[0] // 128):
            ref[128 * t : 128 * (t + 1)] = total[at]
            at += 1
    for i, ref in enumerate(refs[7:]):
        for h in (0, 2):
            line = rows + 4 * i + h
            one, two = total[line : line + 1], total[line + 1 : line + 2]
            one_last, two_last = total[line + 8 : line + 9], total[line + 9 : line + 10]
            tiles = (one, halves_joined(one_last, two), highs_joined(two, pltpu.roll(two_last, HD, 1)))
            for t, tile in enumerate(tiles):
                at = 192 * h + 128 * t
                ref[at : at + 128] = tile[0]


def back_kernel(comm, *refs):
    if comm:
        (
            gb_ref, qf_ref, qc_ref, g_ref, k_ref, v_ref, ku_ref, vu_ref, o_ref, xt_ref, wa_ref,
            select_ref, small_ref, far_ref, db_ref, df_ref, vec_ref,
            gx_ref, gq_ref, gk_ref, gv_ref, go_ref, gu_ref, gd_ref,
            v1_ref, v2_ref, v3_ref, v4_ref, v5_ref, v6_ref, v7_ref, v8_ref, v9_ref,
            dt_ref, oc_ref, ga_ref, total_ref, gf_ref, term_ref, near_ref, rows_ref,
            b1_up, b1_low, b2, b3, a1_up, a1_low, a2, a3, vec1, vec4,
            local_sem, send_sem, recv_sem,
        ) = refs
    else:
        (
            qf_ref, gf_ref, qc_ref, g_ref, k_ref, v_ref, ku_ref, vu_ref, o_ref, xt_ref, wa_ref,
            select_ref, small_ref, far_ref, db_ref,
            ga_ref, term_ref, both_ref,
            dt_ref, oc_ref, total_ref,
        ) = refs
    blocks = k_ref.shape[1]
    head = lax.axis_index("head")
    member, pair = lax.rem(head, 2), lax.div(head, 2)
    swapped = head_tiles(heads_repeated(small_ref[2:3]), heads_repeated(far_ref[2:3]))
    total_ref[...] = jnp.zeros_like(total_ref)

    def queries(b, carry):
        back_queries(b, qc_ref, g_ref, ku_ref, vu_ref, select_ref, o_ref, dt_ref, oc_ref, total_ref)
        return carry

    def keys(b, carry):
        back_keys(b, swapped, qc_ref, g_ref, qf_ref, gf_ref, k_ref, v_ref, dt_ref, total_ref)
        return carry

    def weights(p, carry):
        back_weights(p, xt_ref, dt_ref, db_ref, oc_ref, ga_ref)
        return carry

    if not comm:
        lax.fori_loop(0, blocks, queries, 0)
        lax.fori_loop(0, blocks, keys, 0)
        lax.fori_loop(0, 2, weights, 0)

        def rows(i, carry):
            s, b = lax.div(i, blocks), lax.rem(i, blocks)
            term_ref[s, b] = back_rows(s, b, wa_ref, dt_ref)
            return carry

        lax.fori_loop(0, 2 * blocks, rows, 0)
        both_ref[0:8], both_ref[8:16] = bias_totals(member, pair, total_ref)
        return

    index = lax.axis_index("dp")
    z, x = lax.div(index, 2), lax.rem(index, 2)
    x_peer = {"dp": 2 * z + 1 - x}
    y_peer = {"head": lax.rem(head + 2, 4)}
    sibling_peer = {"head": 2 * pair + 1 - member}
    z_peers = [{"dp": lax.rem(index + 2 * k, 8)} for k in (1, 2, 3)]
    z_to = [lax.rem(z + k, 4) for k in (1, 2, 3)]
    barrier = pltpu.get_barrier_semaphore()
    for peer in [x_peer, y_peer, sibling_peer] + z_peers:
        pl.semaphore_signal(barrier, inc=1, device_id=peer, device_id_type=MESH)
    pl.semaphore_wait(barrier, 6)
    sent = []

    def send(src, dst, peer):
        i = len(sent)
        copy = pltpu.make_async_remote_copy(
            src_ref=src,
            dst_ref=dst,
            send_sem=send_sem.at[i],
            recv_sem=recv_sem.at[i],
            device_id=peer,
            device_id_type=MESH,
        )
        copy.start()
        sent.append(copy)
        return copy

    def plus(a, b):
        return (a.astype(F32) + b.astype(F32)).astype(BF16)

    def first_phase(up_other, low_other, up_buffer, low_buffer):
        return send(up_other, up_buffer, y_peer), send(low_other, low_buffer, x_peer)

    far_g = send(g_ref, gf_ref, z_peers[1])
    b_up = send(gb_ref.at[1, 0], b1_up, y_peer)
    b_low = send(gb_ref.at[:, 1, :, 1 - x], b1_low, x_peer)
    lax.fori_loop(0, blocks, queries, 0)
    far_g.wait_recv()
    lax.fori_loop(0, blocks, keys, 0)

    vec_rows = vec_ref.shape[0]
    vec1[0, 0:vec_rows] = vec_ref[...]
    vec1[0, vec_rows : vec_rows + 8], vec1[0, vec_rows + 8 : vec_rows + 16] = bias_totals(
        member, pair, total_ref
    )
    v_sib = send(vec1.at[0], vec1.at[1], sibling_peer)

    halves = gb_ref.shape[2]

    def add_up(i, carry):
        b1_up[i] = plus(b1_up[i], gb_ref[0, 0, i])
        return carry

    def add_low(i, carry):
        for p in range(2):
            b1_low[p, i] = plus(b1_low[p, i], gb_ref[p, 1, i, x])
        return carry

    b_up.wait_recv()
    lax.fori_loop(0, halves, add_up, 0)
    b_up = send(b1_up.at[:, 1 - x], b2.at[0], x_peer)
    b_low.wait_recv()
    lax.fori_loop(0, halves, add_low, 0)
    b_low = send(b1_low.at[1], b2.at[1], y_peer)
    v_sib.wait_recv()
    vec1[2] = vec1[0] + vec1[1]
    v_y = send(vec1.at[2], vec1.at[3], y_peer)

    lax.fori_loop(0, 2, weights, 0)
    half = ga_ref.shape[3] // 2
    up, low = slice(0, half), slice(half, 2 * half)
    a_up = send(ga_ref.at[1, :, :, pl.ds(0, half)], a1_up, y_peer)
    a_low = send(ga_ref.at[:, :, 1 - x, pl.ds(half, half)], a1_low, x_peer)

    def rows_other(b, carry):
        term_ref[b] = back_rows(1, b, wa_ref, dt_ref).astype(BF16)
        return carry

    lax.fori_loop(0, blocks, rows_other, 0)
    term = send(term_ref, near_ref, sibling_peer)

    b_up.wait_recv()
    b_low.wait_recv()

    def add_second(i, carry):
        b2[0, i] = plus(b2[0, i], b1_up[i, x])
        b2[1, i] = plus(b2[1, i], b1_low[0, i])
        return carry

    lax.fori_loop(0, halves, add_second, 0)
    b_z = [send(b2.at[:, to], b3.at[k], peer) for k, (to, peer) in enumerate(zip(z_to, z_peers))]
    v_y.wait_recv()
    vec1[4] = vec1[2] + vec1[3]
    v_x = send(vec1.at[4], vec1.at[5], x_peer)

    a_up.wait_recv()

    def a_add_up(i, carry):
        a1_up[i] = plus(a1_up[i], ga_ref[0, i, :, up])
        return carry

    lax.fori_loop(0, halves, a_add_up, 0)
    a_up = send(a1_up.at[:, 1 - x], a2.at[0], x_peer)
    a_low.wait_recv()

    def a_add_low(i, carry):
        for p in range(2):
            a1_low[p, i] = plus(a1_low[p, i], ga_ref[p, i, x, low])
        return carry

    lax.fori_loop(0, halves, a_add_low, 0)
    a_low = send(a1_low.at[1], a2.at[1], y_peer)

    cap = df_ref.shape[1] // 2
    quarter = rows_ref.shape[2]
    term.wait_recv()

    def rows_own(b, carry):
        own = back_rows(0, b, wa_ref, dt_ref) + near_ref[b].astype(F32)
        for e in range(2):
            first = df_ref[b, cap * e : cap * (e + 1), :]
            high = first.astype(BF16)
            rest = (first - high.astype(F32)).astype(BF16)
            chosen = select_ref[b, cap * e : cap * (e + 1), :]
            spread = t_mm(chosen, high) + t_mm(chosen, rest)
            rows_ref[e, b] = (own[quarter * e : quarter * (e + 1)] + spread).astype(BF16)
        return carry

    lax.fori_loop(0, blocks, rows_own, 0)
    moved = send(rows_ref.at[1 - pair], gx_ref.at[pair], y_peer)
    kept = pltpu.make_async_copy(rows_ref.at[pair], gx_ref.at[pair], local_sem.at[0])
    kept.start()
    v_x.wait_recv()
    vec1[6] = vec1[4] + vec1[5]
    own_vec = pltpu.make_async_copy(vec1.at[6], vec4.at[z], local_sem.at[1])
    own_vec.start()
    v_z = [send(vec1.at[6], vec4.at[z], peer) for peer in z_peers]

    a_up.wait_recv()
    a_low.wait_recv()

    def a_add_second(i, carry):
        a2[0, i] = plus(a2[0, i], a1_up[i, x])
        a2[1, i] = plus(a2[1, i], a1_low[0, i])
        return carry

    lax.fori_loop(0, halves, a_add_second, 0)
    a_z = [send(a2.at[:, to], a3.at[k], peer) for k, (to, peer) in enumerate(zip(z_to, z_peers))]

    for copy in b_z:
        copy.wait_recv()
    for t in range(2):
        total = b2[t, z].astype(F32)
        for k in range(3):
            total = total + b3[k, t].astype(F32)
        if t == 0:
            gu_ref[...] = total
        else:
            gd_ref[...] = total
    own_vec.wait()
    for copy in v_z:
        copy.wait_recv()
    store_vectors(
        (vec4[0] + vec4[1]) + (vec4[2] + vec4[3]),
        (v1_ref, v2_ref, v3_ref, v4_ref, v5_ref, v6_ref, v7_ref, v8_ref, v9_ref),
    )
    for copy in a_z:
        copy.wait_recv()
    halves_of_a = []
    for t in range(2):
        total = a2[t, z].astype(F32)
        for k in range(3):
            total = total + a3[k, t].astype(F32)
        halves_of_a.append(total)
    total = jnp.concatenate(halves_of_a, axis=0)
    last = total[:, 384:512], total[:, 512:640]
    seconds = [pltpu.roll(tile, HD, 1) for tile in last]
    for ref, i, tile in ((gq_ref, 0, last[0]), (gk_ref, 1, seconds[0]), (gv_ref, 2, last[1])):
        ref[:, 0:128] = total[:, 128 * i : 128 * (i + 1)]
        ref[:, 128:192] = tile[:, 0:HD]
    go_ref[0:128, :] = total[:, 640:768].T
    go_ref[128:192, :] = seconds[1].T[0:HD, :]
    kept.wait()
    moved.wait_recv()
    for copy in sent:
        copy.wait_send()


def backward(gb, q_far, q_compact, d_attention, keys, values, keys_used, values_used, attention, rows_t, w_attn, select, small, far, d_branch, d_first, vectors):
    n = lax.axis_size("dp")
    _, blocks, block_half, lanes = keys.shape
    width = rows_t.shape[0]
    quarter = block_half // 2
    piece = width // n
    slots = select.shape[1]
    vec_rows = vectors.shape[0] + 16
    sizes = [width] * 6 + [4 * width] + [width] * 2

    def out(*shape, dtype=BF16):
        return jax.ShapeDtypeStruct(shape, dtype)

    compact = (2, blocks, slots // 2, lanes)
    scratch = [
        pltpu.VMEM((2, 2, blocks, block_half, 640), BF16),
        pltpu.VMEM((2, 2, blocks, slots // 2, 256), BF16),
    ]
    shared = (q_compact, d_attention, keys, values, keys_used, values_used, attention, rows_t, w_attn, select, small, far, d_branch)
    if n == 8:
        half = piece // 2
        return pl.pallas_call(
            functools.partial(back_kernel, True),
            out_shape=[
                out(2, blocks, quarter, width),
                out(piece, width // 4, dtype=F32),
                out(piece, width // 4, dtype=F32),
                out(piece, width // 4, dtype=F32),
                out(width // 4, piece, dtype=F32),
                out(piece, width, dtype=F32),
                out(piece, width, dtype=F32),
            ]
            + [out(size, dtype=F32) for size in sizes],
            in_specs=[vmem_spec()] * 17,
            out_specs=[vmem_spec()] * (7 + len(sizes)),
            scratch_shapes=scratch
            + [
                pltpu.VMEM((2, 4, 2, piece, width), BF16),
                pltpu.VMEM((8, lanes), F32),
                pltpu.VMEM(compact, BF16),
                pltpu.VMEM((blocks, block_half, width), BF16),
                pltpu.VMEM((blocks, block_half, width), BF16),
                pltpu.VMEM((2, blocks, quarter, width), BF16),
                pltpu.VMEM((4, 2, piece, width), BF16),
                pltpu.VMEM((2, 4, piece, width), BF16),
                pltpu.VMEM((2, 4, piece, width), BF16),
                pltpu.VMEM((3, 2, piece, width), BF16),
                pltpu.VMEM((4, 2, half, width), BF16),
                pltpu.VMEM((2, 4, half, width), BF16),
                pltpu.VMEM((2, 4, half, width), BF16),
                pltpu.VMEM((3, 2, half, width), BF16),
                pltpu.VMEM((7, vec_rows, 128), F32),
                pltpu.VMEM((4, vec_rows, 128), F32),
                pltpu.SemaphoreType.DMA((2,)),
                pltpu.SemaphoreType.DMA((24,)),
                pltpu.SemaphoreType.DMA((24,)),
            ],
            compiler_params=pltpu.CompilerParams(
                collective_id=2, vmem_limit_bytes=62 * 2**20, has_side_effects=True
            ),
        )(gb.reshape(2, 2, 4, 2, piece, width), q_far, *shared, d_first, vectors)
    ga, term, both = pl.pallas_call(
        functools.partial(back_kernel, False),
        out_shape=[
            out(2, 1, 1, width, width),
            out(2, blocks, block_half, width, dtype=F32),
            out(16, 128, dtype=F32),
        ],
        in_specs=[vmem_spec()] * 15,
        out_specs=[vmem_spec()] * 3,
        scratch_shapes=scratch + [pltpu.VMEM((8, lanes), F32)],
        compiler_params=pltpu.CompilerParams(vmem_limit_bytes=62 * 2**20),
    )(q_far, partner(d_attention), *shared)
    pair = lax.axis_index("head") // 2
    cap = slots // 4
    chosen = select[:, : 2 * cap].reshape(blocks, 2, cap, quarter).astype(F32)
    spread = jnp.einsum(
        "bekr,bekw->berw",
        chosen,
        d_first.reshape(blocks, 2, cap, width),
        precision=lax.Precision.HIGHEST,
    )
    own = term[0].reshape(spread.shape) + sibling(term[1].astype(BF16)).astype(F32).reshape(spread.shape)
    own = (own + spread).astype(BF16)
    grad_x = ordered(pair, pick(own, pair, 1), across(pick(own, 1 - pair, 1)))
    pieces = (2, n, piece, width)
    s_attn = reduce_scatter(ga.reshape(pieces), True)
    s_feed = jnp.stack([reduce_scatter(gb[:, i].reshape(pieces), True) for i in range(2)])
    summed = lax.psum(jnp.concatenate((vectors, both)), ("dp", "head"))
    whole, ends, start = summed.reshape(-1), [], 0
    for size in sizes[:7]:
        ends.append(whole[start : start + size])
        start += size
    last = summed[vectors.shape[0] :].reshape(2, 2, 4, 128)
    ends += [
        jnp.concatenate((last[0, i], last[1, i, :, :HD]), axis=-1).reshape(-1) for i in range(2)
    ]

    def columns_of(i, j, second):
        at = 128 * j + HD * second
        return jnp.concatenate((s_attn[:, 128 * i : 128 * (i + 1)], s_attn[:, at : at + HD]), axis=1)

    return (
        grad_x,
        columns_of(0, 3, 0),
        columns_of(1, 3, 1),
        columns_of(2, 4, 0),
        columns_of(5, 4, 1).T,
        s_feed[0],
        s_feed[1],
        *ends,
    )


def deliver_kernel(*refs):
    count = (len(refs) - 1) // 2
    copies = [
        pltpu.make_async_copy(refs[i], refs[count + i], refs[-1].at[i]) for i in range(count)
    ]
    for copy in copies:
        copy.start()
    for copy in copies:
        copy.wait()


def deliver(arrays):
    return pl.pallas_call(
        deliver_kernel,
        out_shape=[jax.ShapeDtypeStruct(array.shape, array.dtype) for array in arrays],
        in_specs=[vmem_spec()] * len(arrays),
        out_specs=[any_spec()] * len(arrays),
        scratch_shapes=[pltpu.SemaphoreType.DMA((len(arrays),))],
    )(*arrays)


def per_device(
    tokens,
    query_weight,
    query_bias,
    key_weight,
    value_weight,
    value_bias,
    out_weight,
    out_bias,
    first_gain,
    first_shift,
    up_weight,
    up_bias,
    down_weight,
    down_bias,
    second_gain,
    second_shift,
    block_order,
    masked_rows,
    out_grad,
):
    block_count, block_rows, width = tokens.shape
    quarter = block_rows // 4
    hidden_piece = up_weight.shape[1]
    head = lax.axis_index("head")
    c, p = head % 2, head // 2

    lines = (
        query_bias,
        value_bias,
        block_order.astype(F32),
        up_bias,
        out_bias,
        first_gain,
        first_shift,
        down_bias,
        second_gain,
        second_shift,
    )
    flat = []
    for vector in lines:
        flat += [vector, jnp.zeros((hidden_piece - vector.shape[0],), F32)]
    flat.append(jnp.zeros((6 * hidden_piece,), F32))
    small = jnp.concatenate(flat).reshape(16, hidden_piece)
    (
        w_attn, w_feed, x_rows, rows_t, attention, keys, values, keys_used, values_used, q_compact, picks_b, select_b, small_far,
    ) = forward(
        tokens,
        (query_weight, key_weight, value_weight, out_weight, up_weight, down_weight.T),
        small,
        masked_rows,
        c,
        p,
    )

    out_y, gb, d_attention, d_branch_all, d_first, flat, q_far = middle(
        w_attn, w_feed, x_rows, attention, select_b, picks_b, out_grad, small, small_far, q_compact
    )
    grad_x, g_query, g_key, g_value, g_out, g_up, g_down, *ends = backward(
        gb, q_far, q_compact, d_attention, keys, values, keys_used, values_used, attention, rows_t, w_attn, select_b,
        small, small_far, d_branch_all, d_first, flat,
    )
    (
        v_out_bias, v_first_gain, v_first_shift, v_down_bias, v_second_gain, v_second_shift, v_up_bias, v_query_bias, v_value_bias,
        out_y, grad_x, g_query, g_key, g_value, g_out, g_up, g_down,
    ) = deliver((*ends, out_y, grad_x, g_query, g_key, g_value, g_out, g_up, g_down))

    out_y = out_y.reshape(block_count, quarter, width)
    grad_x = grad_x.reshape(block_count, quarter, width)

    return (
        out_y,
        grad_x,
        g_query,
        v_query_bias,
        g_key,
        g_value,
        v_value_bias,
        g_out,
        v_out_bias,
        v_first_gain,
        v_first_shift,
        g_up,
        v_up_bias,
        g_down.T,
        v_down_bias,
        v_second_gain,
        v_second_shift,
    )


def solution(mesh):
    in_specs = (
        P("dp", None, None),
        P("dp", "head"),
        P("head"),
        P("dp", "head"),
        P("dp", "head"),
        P("head"),
        P("head", "dp"),
        P(),
        P(),
        P(),
        P("dp", "head"),
        P("head"),
        P("head", "dp"),
        P(),
        P(),
        P(),
        P("head"),
        P("dp", None),
        P("dp", None, None),
    )
    out_specs = (
        P("dp", "head", None),
        P("dp", "head", None),
        P("dp", "head"),
        P(),
        P("dp", "head"),
        P("dp", "head"),
        P(),
        P("head", "dp"),
        P(),
        P(),
        P(),
        P("dp", "head"),
        P(),
        P("head", "dp"),
        P(),
        P(),
        P(),
    )
    return jax.shard_map(
        per_device, mesh=mesh, in_specs=in_specs, out_specs=out_specs, check_vma=False
    )
```

```python
import functools

import jax
import jax.numpy as jnp
from jax import lax
from jax.experimental import pallas as pl
from jax.experimental.pallas import tpu as pltpu
from jax.sharding import PartitionSpec as P

HEADS = 12
HD = 64
FF = 3072
EPSILON = 1e-12
F32 = jnp.float32
BF16 = jnp.bfloat16
SCALE = HD ** (-0.5)
MESH = pl.DeviceIdType.MESH


def flip(block, axis, bit):
    n = lax.axis_size(axis)
    return lax.ppermute(block, axis, [(i, i ^ bit) for i in range(n)])


def shift(block, axis, distance):
    n = lax.axis_size(axis)
    return lax.ppermute(block, axis, [(i, (i + distance) % n) for i in range(n)])


def sibling(block):
    return flip(block, "head", 1)


def across(block):
    return flip(block, "head", 2)


def partner(block):
    return shift(block, "dp", lax.axis_size("dp") // 2)


def pick(array, index, axis=0):
    return lax.dynamic_index_in_dim(array, index, axis, keepdims=False)


def ordered(low, own, other, axis=0):
    return jnp.stack(
        (jnp.where(low == 0, own, other), jnp.where(low == 0, other, own)), axis=axis
    )


def mm(a, b):
    return jnp.dot(a, b, preferred_element_type=F32)


def mm_t(a, b):
    return lax.dot_general(a, b, (((1,), (1,)), ((), ())), preferred_element_type=F32)


def t_mm(a, b):
    return lax.dot_general(a, b, (((0,), (0,)), ((), ())), preferred_element_type=F32)


def norm_parts(rows):
    centered = rows - jnp.mean(rows, axis=-1, keepdims=True)
    inverse = lax.rsqrt(jnp.mean(centered * centered, axis=-1, keepdims=True) + EPSILON)
    return centered * inverse, inverse


def norm_back(incoming, normed, inverse, gain):
    scaled = incoming * gain
    return inverse * (
        scaled
        - jnp.mean(scaled, axis=-1, keepdims=True)
        - normed * jnp.mean(scaled * normed, axis=-1, keepdims=True)
    )


def gaussian_parts(t):
    k = 1.0 / (1.0 + (0.3275911 * 0.5**0.5) * jnp.abs(t))
    bell = jnp.exp(-0.5 * t * t)
    series = 0.5 * 1.061405429
    for a in (-1.453152027, 1.421413741, -0.284496736, 0.254829592):
        series = series * k + 0.5 * a
    tail = series * k * bell
    return jnp.where(t < 0.0, tail, 1.0 - tail), bell


def gather(piece, x_first):
    n = lax.axis_size("dp")
    if n != 8:
        mine = lax.all_gather(piece, "dp", axis=0, tiled=False)
        return jnp.stack((mine, across(mine)))
    index = lax.axis_index("dp")
    z, x = index // 2, index % 2
    column = jnp.zeros((4,) + piece.shape, piece.dtype)
    column = lax.dynamic_update_index_in_dim(column, piece, z, 0)
    for k in (1, 2, 3):
        column = lax.dynamic_update_index_in_dim(
            column, shift(piece, "dp", 2 * k), (z - k) % 4, 0
        )
    if x_first:
        plane = ordered(x, column, flip(column, "dp", 1), axis=1)
        both = jnp.stack((plane, across(plane)))
    else:
        both = jnp.stack((column, across(column)))
        both = ordered(x, both, flip(both, "dp", 1), axis=2)
    return both.reshape((2, 8) + piece.shape)


def reduce_scatter(terms, x_last):
    n = lax.axis_size("dp")
    if n != 8:
        total = terms[0].astype(F32) + across(terms[1].astype(BF16)).astype(F32)
        return lax.psum_scatter(total, "dp", scatter_dimension=0, tiled=False)
    index = lax.axis_index("dp")
    z, x = index // 2, index % 2
    terms = terms.reshape((2, 4, 2) + terms.shape[2:])
    if x_last:
        arrived = across(terms[1])
        plane = (terms[0].astype(F32) + arrived.astype(F32)).astype(BF16)
        arrived = flip(pick(plane, 1 - x, 1), "dp", 1)
        column = pick(plane, x, 1).astype(F32) + arrived.astype(F32)
    else:
        arrived = flip(pick(terms, 1 - x, 2), "dp", 1)
        both = (pick(terms, x, 2).astype(F32) + arrived.astype(F32)).astype(BF16)
        column = both[0].astype(F32) + across(both[1]).astype(F32)
    column = column.astype(BF16)
    total = pick(column, z).astype(F32)
    for k in (1, 2, 3):
        total = total + shift(pick(column, (z + k) % 4), "dp", 2 * k).astype(F32)
    return total


def lane_masks(scale):
    lane = lax.broadcasted_iota(jnp.int32, (1, 2 * HD), 1)
    first = jnp.where(lane < HD, 1.0, 0.0)
    return [(first * scale).astype(BF16), ((1.0 - first) * scale).astype(BF16)]


def rows_of(ref):
    a, b, w = ref.shape
    return ref[...].reshape(a * b, w)


def pair_lanes(halves):
    lane = lax.broadcasted_iota(jnp.int32, halves[0].shape, 1)
    return jnp.where(lane < HD, halves[0], halves[1])


def halves_joined(low, high):
    lane = lax.broadcasted_iota(jnp.int32, low.shape, 1)
    return jnp.where(lane < HD, low, pltpu.roll(high, HD, 1))


def highs_joined(low, high):
    lane = lax.broadcasted_iota(jnp.int32, low.shape, 1)
    return jnp.where(lane < HD, pltpu.roll(low, HD, 1), high)


def head_tiles(row_own, row_other):
    return (
        row_own[:, :128],
        row_other[:, :128],
        halves_joined(row_own[:, 128:256], row_other[:, 128:256]),
    )


def heads_repeated(row):
    head = lax.div(lax.broadcasted_iota(jnp.int32, (1, 256), 1), HD)
    return sum(jnp.where(head == h, row[:, h : h + 1], 0.0) for h in range(3))


def project(x, wa_ref, count):
    width = x.shape[1]
    tiles = []
    for p in range(2):
        w = wa_ref[p].reshape(width, wa_ref.shape[-1])
        out = mm(x, w[:, count[0] : count[1]])
        tiles.append([out[:, 128 * i : 128 * (i + 1)] for i in range(out.shape[1] // 128)])
    return tiles


def forward_own(b, x_ref, wa_ref, bias, q_ref, k_ref, v_ref):
    rows = x_ref.shape[2] * x_ref.shape[3] * 2
    x = x_ref[:, b].reshape(rows, x_ref.shape[-1])
    one, two = project(x, wa_ref, (0, 640))
    b_query, b_value = bias
    parts = (
        (q_ref, (one[0], two[0], halves_joined(one[3], two[3])), b_query),
        (k_ref, (one[1], two[1], highs_joined(one[3], two[3])), None),
        (v_ref, (one[2], two[2], halves_joined(one[4], two[4])), b_value),
    )
    for ref, tiles, added in parts:
        for t in range(3):
            tile = tiles[t] if added is None else tiles[t] + added[t]
            ref[:, b, :, 128 * t : 128 * (t + 1)] = tile.astype(BF16).reshape(2, rows // 2, 128)


def forward_attend(b, xp_ref, wa_ref, bias, swapped, q_ref, k_ref, v_ref, ku_ref, vu_ref, o_ref):
    rows = xp_ref.shape[2] * xp_ref.shape[3] * 2
    x = xp_ref[:, b].reshape(rows, xp_ref.shape[-1])
    one, two = project(x, wa_ref, (128, 640))
    far_keys = (one[0], two[0], highs_joined(one[2], two[2]))
    far_values = (one[1], two[1], halves_joined(one[3], two[3]))
    masks = lane_masks(SCALE)
    for t in range(3):
        lanes = slice(128 * t, 128 * (t + 1))

        def load(ref):
            return ref[:, b, :, lanes].reshape(rows, 128)

        take_far = swapped[t] > 0.5
        k = jnp.where(take_far, far_keys[t], load(k_ref).astype(F32)).astype(BF16)
        v = jnp.where(
            take_far, far_values[t] + bias[1][t], load(v_ref).astype(F32)
        ).astype(BF16)
        ku_ref[:, b, :, lanes] = k.reshape(2, rows // 2, 128)
        vu_ref[:, b, :, lanes] = v.reshape(2, rows // 2, 128)
        q = load(q_ref)
        outs = []
        for mask in masks:
            s = mm_t(q * mask, k)
            raised = jnp.exp(s - jnp.max(s, axis=-1, keepdims=True))
            total = jnp.sum(raised, axis=-1, keepdims=True)
            outs.append(mm(raised.astype(BF16), v) / total)
        o_ref[:, b, :, lanes] = pair_lanes(outs).astype(BF16).reshape(2, rows // 2, 128)


def forward_listed(b, member, pair, listed_ref, q_ref, picks_ref, select_ref, qc_ref):
    slots = listed_ref.shape[-1]
    quarter = q_ref.shape[2] // 2
    cap = slots // 4
    row = listed_ref[pl.ds(q_ref.shape[1] * pair + b, 1), :]
    col = jnp.broadcast_to(row.astype(F32), (slots, slots)).T[:, 0:1].astype(jnp.int32)
    bits = quarter.bit_length() - 1
    run_row = lax.shift_right_arithmetic(row, bits)
    run_col = lax.shift_right_arithmetic(col, bits)
    before = lax.broadcasted_iota(jnp.int32, (slots, slots), 0) < lax.broadcasted_iota(
        jnp.int32, (slots, slots), 1
    )
    same = jnp.where(run_col == run_row, jnp.where(before, 1.0, 0.0), 0.0)
    rank = jnp.sum(same, axis=0, keepdims=True)
    line = lax.broadcasted_iota(jnp.int32, (slots, 1), 0)
    place = line // cap
    wanted_run = jnp.where(
        place == 0, member, jnp.where(place == 1, member + 2, jnp.where(place == 2, 1 - member, 3 - member))
    )
    wanted_rank = (line % cap).astype(F32)
    picks = jnp.where(run_row == wanted_run, jnp.where(rank == wanted_rank, 1.0, 0.0), 0.0).astype(BF16)
    lane = lax.broadcasted_iota(jnp.int32, (slots, quarter), 1)
    places = jnp.where(jnp.bitwise_and(col, quarter - 1) == lane, 1.0, 0.0).astype(BF16)
    select = mm(picks, places).astype(BF16)
    picks_ref[b] = picks
    select_ref[b] = select
    for s in range(2):
        for e in range(2):
            at = (2 * s + e) * cap
            rows = q_ref[s, b, quarter * e : quarter * (e + 1), :]
            qc_ref[s, b, cap * e : cap * (e + 1), :] = mm(select[at : at + cap], rows).astype(BF16)


def pack_piece(query_ref, key_ref, value_ref, out_ref, a_ref):
    out = out_ref[...].T
    query, key, value = query_ref[...], key_ref[...], value_ref[...]
    for i, tile in enumerate((query, key, value)):
        a_ref[:, 128 * i : 128 * (i + 1)] = tile[:, 0:128]
    a_ref[:, 384:512] = jnp.concatenate((query[:, 128:192], key[:, 128:192]), axis=1)
    a_ref[:, 512:640] = jnp.concatenate((value[:, 128:192], out[:, 128:192]), axis=1)
    a_ref[:, 640:768] = out[:, 0:128]


def forward_kernel(comm, *refs):
    if comm:
        (
            query_ref, key_ref, value_ref, out_ref, up_ref, down_ref, t_ref, small_ref, listed_ref,
            wa_ref, wb_ref, x_ref, xt_ref, o_ref, k_ref, v_ref, ku_ref, vu_ref, qc_ref, picks_ref, select_ref, far_ref,
            a_ref, b_ref, xp_ref, q_ref, local_sem, send_sem, recv_sem,
        ) = refs
    else:
        (
            wa_ref, x_ref, xp_ref, small_ref, far_ref, listed_ref,
            xt_ref, o_ref, k_ref, v_ref, ku_ref, vu_ref, qc_ref, picks_ref, select_ref,
            q_ref,
        ) = refs
    blocks = x_ref.shape[1]
    head = lax.axis_index("head")
    member, pair = lax.rem(head, 2), lax.div(head, 2)

    def listed(b, carry):
        forward_listed(b, member, pair, listed_ref, q_ref, picks_ref, select_ref, qc_ref)
        return carry

    def turned(i, carry):
        s, rest = lax.div(i, 2 * blocks), lax.rem(i, 2 * blocks)
        part = x_ref[s, lax.div(rest, 2), lax.rem(rest, 2)]
        quarter = part.shape[0]
        xt_ref[:, pl.ds(pl.multiple_of(i * quarter, quarter), quarter)] = part.T
        return carry

    def bias_of():
        own, other = small_ref[...], far_ref[...]
        rows = [head_tiles(own[i : i + 1], other[i : i + 1]) for i in range(2)]
        order = head_tiles(heads_repeated(own[2:3]), heads_repeated(other[2:3]))
        return (rows[0], rows[1]), order

    if not comm:
        bias, swapped = bias_of()
        lax.fori_loop(0, 4 * blocks, turned, 0)

        def own_block(b, carry):
            forward_own(b, x_ref, wa_ref, bias, q_ref, k_ref, v_ref)
            return carry

    if comm:
        index = lax.axis_index("dp")
        z, x = lax.div(index, 2), lax.rem(index, 2)
        x_peer = {"dp": 2 * z + 1 - x}
        y_peer = {"head": lax.rem(head + 2, 4)}
        sibling_peer = {"head": 2 * pair + 1 - member}
        z_next = z + 1 - 2 * lax.rem(z, 2)
        z_far = lax.rem(z + 2, 4)
        next_peer, far_peer = {"dp": 2 * z_next + x}, {"dp": 2 * z_far + x}
        barrier = pltpu.get_barrier_semaphore()
        for peer in (x_peer, y_peer, sibling_peer, next_peer, far_peer):
            pl.semaphore_signal(barrier, inc=1, device_id=peer, device_id_type=MESH)
        counter = [0]

        def local(src, dst, i):
            copy = pltpu.make_async_copy(src, dst, local_sem.at[i])
            copy.start()
            return copy

        def send(src, dst, peer):
            i = counter[0]
            counter[0] += 1
            copy = pltpu.make_async_remote_copy(
                src_ref=src,
                dst_ref=dst,
                send_sem=send_sem.at[i],
                recv_sem=recv_sem.at[i],
                device_id=peer,
                device_id_type=MESH,
            )
            copy.start()
            sent.append(copy)
            return copy

        def far_copy(b):
            return pltpu.make_async_remote_copy(
                src_ref=x_ref.at[0, b],
                dst_ref=xp_ref.at[0, b],
                send_sem=send_sem.at[15 + b],
                recv_sem=recv_sem.at[15 + b],
                device_id=far_peer,
                device_id_type=MESH,
            )

        def near_copy(b):
            return pltpu.make_async_remote_copy(
                src_ref=xp_ref.at[0, b],
                dst_ref=xp_ref.at[1, b],
                send_sem=send_sem.at[15 + blocks + b],
                recv_sem=recv_sem.at[15 + blocks + b],
                device_id=sibling_peer,
                device_id_type=MESH,
            )

        sent = []
        quarters = (member, member + 2, 1 - member, 3 - member)
        fills = [
            local(t_ref.at[pl.ds(blocks * pair, blocks), quarters[2 * s + e]], x_ref.at[s, :, e], 2 * s + e)
            for s in range(2)
            for e in range(2)
        ]
        pack_piece(query_ref, key_ref, value_ref, out_ref, a_ref)
        fill_a = local(a_ref, wa_ref.at[0, z, x], 4)
        pl.semaphore_wait(barrier, 5)
        a_next = send(a_ref, wa_ref.at[0, z, x], next_peer)
        a_far = send(a_ref, wa_ref.at[0, z, x], far_peer)
        far = send(small_ref, far_ref, y_peer)
        b_ref[0] = up_ref[...]
        b_ref[1] = down_ref[...]
        fill_b = local(b_ref, wb_ref.at[0, :, z, x], 5)
        b_far = send(b_ref, wb_ref.at[0, :, z, x], far_peer)
        for fill in fills:
            fill.wait()
        lax.fori_loop(0, 4 * blocks, turned, 0)
        a_far.wait_recv()
        a_pass = send(wa_ref.at[0, z_far, x], wa_ref.at[0, z_far, x], next_peer)
        b_next = send(b_ref, wb_ref.at[0, :, z, x], next_peer)
        far_copy(0).start()
        half = a_ref.shape[0] // 2
        up, low = pl.ds(0, half), pl.ds(half, half)
        fill_a.wait()
        a_next.wait_recv()
        a_pass.wait_recv()
        a_x = send(wa_ref.at[0, :, x, up], wa_ref.at[0, :, x, up], x_peer)
        a_y = send(wa_ref.at[0, :, x, low], wa_ref.at[1, :, x, low], y_peer)
        b_far.wait_recv()
        b_pass = send(wb_ref.at[0, :, z_far, x], wb_ref.at[0, :, z_far, x], next_peer)
        for b in range(1, blocks):
            far_copy(b).start()
        a_x.wait_recv()
        a_xy = send(wa_ref.at[0, :, :, up], wa_ref.at[1, :, :, up], y_peer)
        a_y.wait_recv()
        a_yx = send(wa_ref.at[:, :, x, low], wa_ref.at[:, :, x, low], x_peer)
        fill_b.wait()
        b_next.wait_recv()
        b_pass.wait_recv()
        b_x = send(wb_ref.at[0, 0, :, x], wb_ref.at[0, 0, :, x], x_peer)
        b_y = send(wb_ref.at[0, 1, :, x], wb_ref.at[1, 1, :, x], y_peer)
        far.wait_recv()
        a_xy.wait_recv()
        a_yx.wait_recv()
        bias, swapped = bias_of()

        def own_block(b, carry):
            forward_own(b, x_ref, wa_ref, bias, q_ref, k_ref, v_ref)
            return carry

    lax.fori_loop(0, blocks, own_block, 0)
    lax.fori_loop(0, blocks, listed, 0)
    if comm:

        def attend_block(b, carry):
            far_copy(b).wait_recv()
            near = near_copy(b)
            near.start()
            near.wait_recv()
            forward_attend(b, xp_ref, wa_ref, bias, swapped, q_ref, k_ref, v_ref, ku_ref, vu_ref, o_ref)
            return carry

        lax.fori_loop(0, 1, attend_block, 0)
        b_x.wait_recv()
        b_xy = send(wb_ref.at[0, 0], wb_ref.at[1, 0], y_peer)
        b_y.wait_recv()
        b_yx = send(wb_ref.at[:, 1, :, x], wb_ref.at[:, 1, :, x], x_peer)
        lax.fori_loop(1, blocks, attend_block, 0)
        b_xy.wait_recv()
        b_yx.wait_recv()
        for copy in sent:
            copy.wait_send()
        for b in range(blocks):
            far_copy(b).wait_send()
            near_copy(b).wait_send()
    else:

        def attend_block(b, carry):
            forward_attend(b, xp_ref, wa_ref, bias, swapped, q_ref, k_ref, v_ref, ku_ref, vu_ref, o_ref)
            return carry

        lax.fori_loop(0, blocks, attend_block, 0)


def vmem_spec():
    return pl.BlockSpec(memory_space=pltpu.VMEM)


def any_spec():
    return pl.BlockSpec(memory_space=pl.ANY)


def forward(tokens, weights, small, listed, member, pair):
    n = lax.axis_size("dp")
    block_count, block_rows, width = tokens.shape
    blocks, quarter = block_count // 2, block_rows // 4
    slots = listed.shape[1]
    cap = slots // 4
    lanes = 6 * HD
    tokens = tokens.reshape(block_count, 4, quarter, width)
    query, key, value, out_weight, up_weight, down_weight = weights
    piece_rows, hidden = up_weight.shape
    rows_shape = (2, blocks, 2, quarter, width)

    def out(*shape, dtype=BF16):
        return jax.ShapeDtypeStruct(shape, dtype)

    dense = (2, blocks, 2 * quarter, lanes)
    tail = [out(width, 2 * blocks * 2 * quarter)] + [out(*dense)] * 5 + [
        out(2, blocks, 2 * cap, lanes),
        out(blocks, slots, slots),
        out(blocks, slots, quarter),
    ]
    params = dict(vmem_limit_bytes=60 * 2**20, has_side_effects=True)
    if n == 8:
        shapes = [
            out(2, 4, 2, piece_rows, 12 * HD),
            out(2, 2, 4, 2, piece_rows, hidden),
            out(*rows_shape),
            *tail,
            out(*small.shape, dtype=F32),
        ]
        specs = [vmem_spec()] * len(shapes)
        specs[1] = any_spec()
        results = pl.pallas_call(
            functools.partial(forward_kernel, True),
            out_shape=shapes,
            in_specs=[vmem_spec()] * 6 + [any_spec()] + [vmem_spec()] * 2,
            out_specs=specs,
            scratch_shapes=[
                pltpu.VMEM((piece_rows, 12 * HD), BF16),
                pltpu.VMEM((2, piece_rows, hidden), BF16),
                pltpu.VMEM(rows_shape, BF16),
                pltpu.VMEM(dense, BF16),
                pltpu.SemaphoreType.DMA((6,)),
                pltpu.SemaphoreType.DMA((15 + 2 * blocks,)),
                pltpu.SemaphoreType.DMA((15 + 2 * blocks,)),
            ],
            compiler_params=pltpu.CompilerParams(collective_id=1, **params),
        )(*weights, tokens, small, listed)
        w_attn, w_feed, rows, *rest, far = results
    else:
        mine = pick(tokens.reshape(2, blocks, 2, 2, quarter, width), pair)
        rows = jnp.stack((pick(mine, member, 2), pick(mine, 1 - member, 2)))
        out_t = out_weight.T
        first, last = slice(0, 2 * HD), slice(2 * HD, 3 * HD)
        piece_a = jnp.concatenate(
            [part[:, first] for part in (query, key, value)]
            + [part[:, last] for part in (query, key, value, out_t)]
            + [out_t[:, first]],
            axis=1,
        )
        w_attn = gather(piece_a, True)
        w_feed = jnp.stack([gather(piece, True) for piece in (up_weight, down_weight)], axis=1)
        far = across(small)
        shapes = tail
        rest = pl.pallas_call(
            functools.partial(forward_kernel, False),
            out_shape=shapes,
            in_specs=[vmem_spec()] * 6,
            out_specs=[vmem_spec()] * len(shapes),
            scratch_shapes=[pltpu.VMEM(dense, BF16)],
            compiler_params=pltpu.CompilerParams(vmem_limit_bytes=60 * 2**20),
        )(w_attn.reshape(2, width, -1), rows, partner(rows), small, far, listed)
    w_attn = w_attn.reshape(2, width, -1)
    w_feed = w_feed.reshape(2, 2, width, -1)
    return (w_attn, w_feed, rows, *rest, far)


OUT_BIAS, FIRST_GAIN, FIRST_SHIFT, DOWN_BIAS, SECOND_GAIN, SECOND_SHIFT = range(4, 10)


def picked(chosen, rows):
    high = rows.astype(BF16)
    rest = (rows - high.astype(F32)).astype(BF16)
    return mm(chosen, high) + mm(chosen, rest)


def column_sum(rows):
    return jnp.sum(rows, axis=0, keepdims=True)


def middle_kernel(
    wa_ref, wf_in, x_in, attn_ref, select_ref, picks_ref, grads_in, small_ref, far_ref, qc_ref,
    y_ref, gb_ref, da_ref, db_ref, df_ref, vec_ref, qf_ref,
    wf, xs, gs, wo, ao, hid, hl, hc, one_c, pre, act, feeds, ft_out, ft_in, rows_ref, ds, dfd, turned_h, turned_d,
    d_act, d_pre, term, dt_out, dt_in, acc, local_sem, send_sem, recv_sem,
):
    blocks, half, width = hid.shape
    quarter = half // 2
    cap = df_ref.shape[1] // 2
    own = blocks * 2 * cap
    head = lax.axis_index("head")
    member, pair = lax.rem(head, 2), lax.div(head, 2)
    sibling_peer = {"head": 2 * pair + 1 - member}
    y_peer = {"head": lax.rem(head + 2, 4)}
    devices = lax.axis_size("dp")
    partner_peer = {"dp": lax.rem(lax.axis_index("dp") + devices // 2, devices)}
    barrier = pltpu.get_barrier_semaphore()
    for peer in (sibling_peer, y_peer, partner_peer):
        pl.semaphore_signal(barrier, inc=1, device_id=peer, device_id_type=MESH)
    sent = []

    def remote(src, dst, peer, i):
        return pltpu.make_async_remote_copy(
            src_ref=src,
            dst_ref=dst,
            send_sem=send_sem.at[i],
            recv_sem=recv_sem.at[i],
            device_id=peer,
            device_id_type=MESH,
        )

    def send(src, dst, peer):
        copy = remote(src, dst, peer, 2 * blocks + len(sent))
        copy.start()
        sent.append(copy)
        return copy

    def local(src, dst, i):
        copy = pltpu.make_async_copy(src, dst, local_sem.at[i])
        copy.start()
        return copy

    def hidden_copy(b):
        return remote(hl.at[0, b], hl.at[1, b], sibling_peer, b)

    def feed_copy(b):
        return remote(ft_out.at[b], ft_in.at[b], sibling_peer, blocks + b)

    def vector(i):
        return small_ref[i : i + 1, :]

    up_biases = (small_ref, far_ref)

    fill_x = local(x_in.at[0], xs, 0)
    fill_w = local(wf_in, wf, 1)
    fill_g = local(grads_in.at[pl.ds(blocks * pair, blocks)], gs, 2)
    pl.semaphore_wait(barrier, 3)
    far_queries = send(qc_ref, qf_ref, partner_peer)
    other_rows = send(attn_ref.at[1], ao, sibling_peer)
    for p in range(2):
        wo[0, :, 128 * p : 128 * (p + 1)] = wa_ref[p, :, 640:768]
    wo[0, :, 256:384] = highs_joined(
        wa_ref[0, :, 512:640].astype(F32), wa_ref[1, :, 512:640].astype(F32)
    ).astype(BF16)
    other_weights = send(wo.at[0], wo.at[1], sibling_peer)

    def branch_own(b, carry):
        feeds[b] = mm_t(attn_ref[0, b], wo[0])
        return carry

    lax.fori_loop(0, blocks, branch_own, 0)
    acc[...] = jnp.zeros_like(acc)
    fill_x.wait()
    other_rows.wait_recv()
    other_weights.wait_recv()

    def first_norm(b, carry):
        rows = xs[b].reshape(half, width).astype(F32) + feeds[b] + mm_t(ao[b], wo[1]) + vector(OUT_BIAS)
        hidden = norm_parts(rows)[0] * vector(FIRST_GAIN) + vector(FIRST_SHIFT)
        low = hidden.astype(BF16)
        hid[b] = hidden
        hl[0, b] = low
        hidden_copy(b).start()
        for e in range(2):
            at, run = slice(cap * e, cap * (e + 1)), slice(quarter * e, quarter * (e + 1))
            chosen = select_ref[b, at, :]
            one_c[b, at, :] = picked(chosen, rows[run])
            hc[0, b, at, :] = mm(chosen, low[run]).astype(BF16)
        return carry

    lax.fori_loop(0, blocks, first_norm, 0)
    other_listed = send(hc.at[0], hc.at[1], sibling_peer)
    fill_w.wait()

    def feed(s, b):
        out = 0.0
        for p in range(2):
            for i in range(3):
                units = slice(width // 3 * i, width // 3 * (i + 1))
                t = mm(hl[s, b], wf[p, 0, :, units]) + up_biases[p][3:4, units]
                low = (t * gaussian_parts(t)[0]).astype(BF16)
                out = out + mm_t(low, wf[p, 1, :, units])
        return out

    def feed_other(b, carry):
        hidden_copy(b).wait_recv()
        ft_out[b] = feed(1, b).astype(BF16)
        feed_copy(b).start()
        return carry

    lax.fori_loop(0, blocks, feed_other, 0)

    def feed_own(b, carry):
        feeds[b] = feed(0, b)
        return carry

    lax.fori_loop(0, blocks, feed_own, 0)
    fill_g.wait()

    def second_norm(b, carry):
        feed_copy(b).wait_recv()
        rows = hid[b] + feeds[b] + ft_in[b].astype(F32) + vector(DOWN_BIAS)
        out = (norm_parts(rows)[0] * vector(SECOND_GAIN) + vector(SECOND_SHIFT)).astype(BF16)
        listed = []
        for e in range(2):
            at, run = slice(cap * e, cap * (e + 1)), slice(quarter * e, quarter * (e + 1))
            rows_ref[e, b] = out[run]
            listed.append(picked(select_ref[b, at, :], rows[run]))
        normed, inverse = norm_parts(jnp.concatenate(listed, axis=0))
        grad_y = mm(picks_ref[b, 0 : 2 * cap, :], gs[b])
        d_second = norm_back(grad_y, normed, inverse, vector(SECOND_GAIN))
        d_feed = d_second.astype(BF16)
        ds[b] = d_second
        dfd[0, b] = d_feed
        acc[3:4] += column_sum(d_feed.astype(F32))
        acc[4:5] += column_sum(grad_y * normed)
        acc[5:6] += column_sum(grad_y)
        return carry

    lax.fori_loop(0, blocks, second_norm, 0)
    other_d = send(dfd.at[0], dfd.at[1], sibling_peer)
    moved = send(rows_ref.at[1 - pair], y_ref.at[pair], y_peer)
    kept = local(rows_ref.at[pair], y_ref.at[pair], 3)

    other_listed.wait_recv()

    def turn(ref, out):
        flat = ref[...].reshape(2 * own, width)
        for i in range(2 * own // 128):
            out[:, 128 * i : 128 * (i + 1)] = flat[128 * i : 128 * (i + 1)].T

    turn(hc, turned_h)
    other_d.wait_recv()
    turn(dfd, turned_d)

    for p in range(2):
        pre[...] = mm(hc[...].reshape(2 * own, width), wf[p, 0]) + up_biases[p][3:4, :]
        d_act[...] = mm(dfd[...].reshape(2 * own, width), wf[p, 1])

        def back_rows_of(i, total):
            at = pl.ds(pl.multiple_of(16 * i, 16), 16)
            t = pre[at, :]
            cdf, bell = gaussian_parts(t)
            act[p, at, :] = (t * cdf).astype(BF16)
            d = (d_act[at, :] * (cdf + t * (bell * (0.5 / jnp.pi) ** 0.5))).astype(BF16)
            d_pre[p, at, :] = d
            d = d.astype(F32)
            return total + (d[0:8] + d[8:16])

        total = lax.fori_loop(0, 2 * own // 16, back_rows_of, jnp.zeros((8, width), F32))
        acc[6 + p : 7 + p] = column_sum(total)
        part = mm_t(d_pre[p], wf[p, 0])
        if p == 0:
            term[...] = part
        else:
            part = part + term[...]
            dt_out[...] = part[own:].astype(BF16)
            other_term = send(dt_out, dt_in, sibling_peer)
            term[0:own] = part[:own]

    gb_ref[0, 0] = mm(turned_h[...], d_pre[0]).astype(BF16)
    other_term.wait_recv()

    def first_back(b, carry):
        at = pl.ds(pl.multiple_of(2 * cap * b, 2 * cap), 2 * cap)
        d_hidden = ds[b] + term[at, :] + dt_in[at, :].astype(F32)
        normed, inverse = norm_parts(one_c[b])
        d_first = norm_back(d_hidden, normed, inverse, vector(FIRST_GAIN))
        d_branch = d_first.astype(BF16)
        df_ref[b] = d_first
        db_ref[0, b] = d_branch
        acc[0:1] += column_sum(d_branch.astype(F32))
        acc[1:2] += column_sum(d_hidden * normed)
        acc[2:3] += column_sum(d_hidden)
        return carry

    lax.fori_loop(0, blocks, first_back, 0)
    other_branch = send(db_ref.at[0], db_ref.at[1], sibling_peer)
    gb_ref[0, 1] = mm(turned_d[...], act[0]).astype(BF16)
    gb_ref[1, 0] = mm(turned_h[...], d_pre[1]).astype(BF16)
    gb_ref[1, 1] = mm(turned_d[...], act[1]).astype(BF16)
    tiles = width // 128
    vec_ref[...] = jnp.zeros_like(vec_ref)
    for t in range(tiles):
        lanes = slice(128 * t, 128 * (t + 1))
        for i in range(6):
            vec_ref[tiles * i + t : tiles * i + t + 1, :] = acc[i : i + 1, lanes]
        for h in range(4):
            mine = jnp.where(head == h, acc[6:7, lanes], 0.0)
            other = jnp.where(lax.rem(head + 2, 4) == h, acc[7:8, lanes], 0.0)
            at = tiles * (6 + h) + t
            vec_ref[at : at + 1, :] = mine + other
    other_branch.wait_recv()
    for s in range(2):
        da = mm(db_ref[s].reshape(own, width), wo[0])
        da_ref[s] = da.astype(BF16).reshape(da_ref.shape[1:])
    kept.wait()
    moved.wait_recv()
    far_queries.wait_recv()
    for copy in sent:
        copy.wait_send()
    for b in range(blocks):
        hidden_copy(b).wait_send()
        feed_copy(b).wait_send()


def middle(w_attn, w_feed, x_rows, attention, select, picks, out_grad, small, far, q_compact):
    _, blocks, block_half, lanes = attention.shape
    width = w_attn.shape[1]
    quarter = block_half // 2
    listed = select.shape[1] // 2
    own = blocks * listed

    def out(*shape, dtype=BF16):
        return jax.ShapeDtypeStruct(shape, dtype)

    def room(*shape, dtype=BF16):
        return pltpu.VMEM(shape, dtype)

    in_specs = [vmem_spec()] * 10
    for i in (1, 2, 6):
        in_specs[i] = any_spec()
    return pl.pallas_call(
        middle_kernel,
        out_shape=[
            out(2, blocks, quarter, width),
            out(*w_feed.shape),
            out(2, blocks, listed, lanes),
            out(2, blocks, listed, width),
            out(blocks, listed, width, dtype=F32),
            out(64, 128, dtype=F32),
            out(*q_compact.shape),
        ],
        in_specs=in_specs,
        out_specs=[vmem_spec()] * 7,
        scratch_shapes=[
            room(*w_feed.shape),
            room(blocks, 2, quarter, width),
            room(blocks, *out_grad.shape[1:]),
            room(2, width, lanes),
            room(blocks, block_half, lanes),
            room(blocks, block_half, width, dtype=F32),
            room(2, blocks, block_half, width),
            room(2, blocks, listed, width),
            room(blocks, listed, width, dtype=F32),
            room(2 * own, width, dtype=F32),
            room(2, 2 * own, width),
            room(blocks, block_half, width, dtype=F32),
            room(blocks, block_half, width),
            room(blocks, block_half, width),
            room(2, blocks, quarter, width),
            room(blocks, listed, width, dtype=F32),
            room(2, blocks, listed, width),
            room(width, 2 * own),
            room(width, 2 * own),
            room(2 * own, width, dtype=F32),
            room(2, 2 * own, width),
            room(2 * own, width, dtype=F32),
            room(own, width),
            room(own, width),
            room(8, width, dtype=F32),
            pltpu.SemaphoreType.DMA((4,)),
            pltpu.SemaphoreType.DMA((2 * blocks + 8,)),
            pltpu.SemaphoreType.DMA((2 * blocks + 8,)),
        ],
        compiler_params=pltpu.CompilerParams(
            collective_id=3, vmem_limit_bytes=60 * 2**20, has_side_effects=True
        ),
    )(w_attn, w_feed, x_rows, attention, select, picks, out_grad, small, far, q_compact)


def back_queries(b, qc_ref, g_ref, ku_ref, vu_ref, select_ref, o_ref, dt_ref, oc_ref, total_ref):
    rows = ku_ref.shape[2] * 2
    slots = qc_ref.shape[2] * 2
    cap = slots // 4
    quarter = rows // 4
    select = select_ref[b]
    tiles = []
    for t in range(3):
        lanes = slice(128 * t, 128 * (t + 1))
        q = qc_ref[:, b, :, lanes].reshape(slots, 128)
        g = g_ref[:, b, :, lanes].reshape(slots, 128)
        k = ku_ref[:, b, :, lanes].reshape(rows, 128)
        v = vu_ref[:, b, :, lanes].reshape(rows, 128)
        outs = []
        for mask, one in zip(lane_masks(SCALE), lane_masks(1.0)):
            s = mm_t(q * mask, k)
            raised = jnp.exp(s - jnp.max(s, axis=-1, keepdims=True))
            probs = raised / jnp.sum(raised, axis=-1, keepdims=True)
            d_probs = mm_t(g * one, v)
            inner = jnp.sum(d_probs * probs, axis=-1, keepdims=True)
            d_scores = (probs * (d_probs - inner)).astype(BF16)
            outs.append(mm(d_scores, k) * SCALE)
        tile = pair_lanes(outs).astype(BF16)
        total_ref[0:1, lanes] += jnp.sum(tile.astype(F32), axis=0, keepdims=True)
        tiles.append(tile)
    for s in range(2):
        for e in range(2):
            at = (2 * s + e) * cap
            chosen = select[at : at + cap]
            own = slice(quarter * e, quarter * (e + 1))
            dense = [t_mm(chosen, tile[at : at + cap]) for tile in tiles]
            dt_ref[0, s, b, own, 0:128] = dense[0].astype(BF16)
            dt_ref[1, s, b, own, 0:128] = dense[1].astype(BF16)
            lane = lax.broadcasted_iota(jnp.int32, dense[2].shape, 1)
            for p in range(2):
                last = dense[2] if p == 0 else pltpu.roll(dense[2], HD, 1)
                dt_ref[p, s, b, own, 384:512] = jnp.where(lane < HD, last, 0.0).astype(BF16)
            rows_o = mm(chosen, o_ref[s, b, own, :])
            at_o = slice(cap * e, cap * (e + 1))
            lane = lax.broadcasted_iota(jnp.int32, (cap, 128), 1)
            for p in range(2):
                oc_ref[p, s, b, at_o, 128:256] = rows_o[:, 128 * p : 128 * (p + 1)].astype(BF16)
                last = rows_o[:, 256:384] if p == 1 else pltpu.roll(rows_o[:, 256:384], HD, 1)
                oc_ref[p, s, b, at_o, 0:128] = jnp.where(lane < HD, 0.0, last).astype(BF16)


def back_keys(b, swapped, qc_ref, g_ref, qf_ref, gf_ref, k_ref, v_ref, dt_ref, total_ref):
    rows = k_ref.shape[2] * 2
    slots = qc_ref.shape[2] * 2
    for t in range(3):
        lanes = slice(128 * t, 128 * (t + 1))
        take_far = swapped[t] > 0.5

        def chosen(near, far):
            near = near[:, b, :, lanes].reshape(slots, 128).astype(F32)
            far = far[:, b, :, lanes].reshape(slots, 128).astype(F32)
            return jnp.where(take_far, far, near).astype(BF16)

        q, g = chosen(qc_ref, qf_ref), chosen(g_ref, gf_ref)
        k = k_ref[:, b, :, lanes].reshape(rows, 128)
        v = v_ref[:, b, :, lanes].reshape(rows, 128)
        d_keys, d_values = [], []
        for mask, one in zip(lane_masks(SCALE), lane_masks(1.0)):
            s = mm_t(k, q * mask)
            raised = jnp.exp(s - jnp.max(s, axis=0, keepdims=True))
            probs = raised / jnp.sum(raised, axis=0, keepdims=True)
            d_probs = mm_t(v, g * one)
            inner = jnp.sum(d_probs * probs, axis=0, keepdims=True)
            d_scores = (probs * (d_probs - inner)).astype(BF16)
            d_keys.append(mm(d_scores, q) * SCALE)
            d_values.append(mm(probs.astype(BF16), g))
        dk, dv = pair_lanes(d_keys), pair_lanes(d_values)
        total_ref[1:2, lanes] += jnp.sum(dv.astype(BF16).astype(F32), axis=0, keepdims=True)
        half = (2, rows // 2, 128)
        if t < 2:
            dt_ref[t, :, b, :, 128:256] = dk.astype(BF16).reshape(half)
            dt_ref[t, :, b, :, 256:384] = dv.astype(BF16).reshape(half)
        else:
            lane = lax.broadcasted_iota(jnp.int32, dk.shape, 1)
            for p in range(2):
                last = pltpu.roll(dk, HD, 1) if p == 0 else dk
                before = dt_ref[p, :, b, :, 384:512].reshape(rows, 128).astype(F32)
                dt_ref[p, :, b, :, 384:512] = (
                    jnp.where(lane < HD, before, last).astype(BF16).reshape(half)
                )
                last = dv if p == 0 else pltpu.roll(dv, HD, 1)
                dt_ref[p, :, b, :, 512:640] = (
                    jnp.where(lane < HD, last, 0.0).astype(BF16).reshape(half)
                )


def back_weights(p, xt_ref, dt_ref, db_ref, oc_ref, ga_ref):
    width = xt_ref.shape[0]
    shape = ga_ref.shape[1:-1] + (128,)
    listed = db_ref.shape[0] * db_ref.shape[1] * db_ref.shape[2]
    d_branch = db_ref[...].reshape(listed, width)
    outs = mm(xt_ref[...], dt_ref[p].reshape(xt_ref.shape[1], 640))
    extra = t_mm(d_branch, oc_ref[p].reshape(listed, 256))
    for i in range(6):
        if i < 4:
            tile = outs[:, 128 * i : 128 * (i + 1)]
        elif i == 4:
            tile = outs[:, 512:640] + extra[:, 0:128]
        else:
            tile = extra[:, 128:256]
        ga_ref[p, ..., 128 * i : 128 * (i + 1)] = tile.astype(BF16).reshape(shape)


def back_rows(s, b, wa_ref, dt_ref):
    rows, width = dt_ref.shape[3], wa_ref.shape[-1]
    out = 0.0
    for p in range(2):
        w = wa_ref[p].reshape(-1, wa_ref.shape[-1])
        out = out + mm_t(dt_ref[p, s, b], w[:, 0:640])
    return out


def bias_totals(member, pair, total_ref):
    lane = lax.broadcasted_iota(jnp.int32, (1, 128), 1)
    line = lax.broadcasted_iota(jnp.int32, (8, 128), 0)
    first = jnp.zeros((8, 128), F32)
    second = jnp.zeros((8, 128), F32)
    for i in range(2):
        last = total_ref[i : i + 1, 256:384]
        for p in range(2):
            place = 4 * i + 2 * (pair if p == 0 else 1 - pair) + member
            tile = total_ref[i : i + 1, 128 * p : 128 * (p + 1)]
            third = last if p == 0 else pltpu.roll(last, HD, 1)
            first = first + jnp.where(line == place, tile, 0.0)
            second = second + jnp.where(line == place, jnp.where(lane < HD, third, 0.0), 0.0)
    return first, second


def store_vectors(total, refs):
    at = 0
    rows = total.shape[0] - 16
    for ref in refs[:7]:
        for t in range(ref.shape[0] // 128):
            ref[128 * t : 128 * (t + 1)] = total[at]
            at += 1
    for i, ref in enumerate(refs[7:]):
        for h in (0, 2):
            line = rows + 4 * i + h
            one, two = total[line : line + 1], total[line + 1 : line + 2]
            one_last, two_last = total[line + 8 : line + 9], total[line + 9 : line + 10]
            tiles = (one, halves_joined(one_last, two), highs_joined(two, pltpu.roll(two_last, HD, 1)))
            for t, tile in enumerate(tiles):
                at = 192 * h + 128 * t
                ref[at : at + 128] = tile[0]


def back_kernel(comm, *refs):
    if comm:
        (
            gb_ref, qf_ref, qc_ref, g_ref, k_ref, v_ref, ku_ref, vu_ref, o_ref, xt_ref, wa_ref,
            select_ref, small_ref, far_ref, db_ref, df_ref, vec_ref,
            gx_ref, gq_ref, gk_ref, gv_ref, go_ref, gu_ref, gd_ref,
            v1_ref, v2_ref, v3_ref, v4_ref, v5_ref, v6_ref, v7_ref, v8_ref, v9_ref,
            dt_ref, oc_ref, ga_ref, total_ref, gf_ref, term_ref, near_ref, rows_ref,
            b1_up, b1_low, b2, b3, a1_up, a1_low, a2, a3, vec1, vec4,
            local_sem, send_sem, recv_sem,
        ) = refs
    else:
        (
            qf_ref, gf_ref, qc_ref, g_ref, k_ref, v_ref, ku_ref, vu_ref, o_ref, xt_ref, wa_ref,
            select_ref, small_ref, far_ref, db_ref,
            ga_ref, term_ref, both_ref,
            dt_ref, oc_ref, total_ref,
        ) = refs
    blocks = k_ref.shape[1]
    head = lax.axis_index("head")
    member, pair = lax.rem(head, 2), lax.div(head, 2)
    swapped = head_tiles(heads_repeated(small_ref[2:3]), heads_repeated(far_ref[2:3]))
    total_ref[...] = jnp.zeros_like(total_ref)

    def queries(b, carry):
        back_queries(b, qc_ref, g_ref, ku_ref, vu_ref, select_ref, o_ref, dt_ref, oc_ref, total_ref)
        return carry

    def keys(b, carry):
        back_keys(b, swapped, qc_ref, g_ref, qf_ref, gf_ref, k_ref, v_ref, dt_ref, total_ref)
        return carry

    def weights(p, carry):
        back_weights(p, xt_ref, dt_ref, db_ref, oc_ref, ga_ref)
        return carry

    if not comm:
        lax.fori_loop(0, blocks, queries, 0)
        lax.fori_loop(0, blocks, keys, 0)
        lax.fori_loop(0, 2, weights, 0)

        def rows(i, carry):
            s, b = lax.div(i, blocks), lax.rem(i, blocks)
            term_ref[s, b] = back_rows(s, b, wa_ref, dt_ref)
            return carry

        lax.fori_loop(0, 2 * blocks, rows, 0)
        both_ref[0:8], both_ref[8:16] = bias_totals(member, pair, total_ref)
        return

    index = lax.axis_index("dp")
    z, x = lax.div(index, 2), lax.rem(index, 2)
    x_peer = {"dp": 2 * z + 1 - x}
    y_peer = {"head": lax.rem(head + 2, 4)}
    sibling_peer = {"head": 2 * pair + 1 - member}
    z_peers = [{"dp": lax.rem(index + 2 * k, 8)} for k in (1, 2, 3)]
    z_to = [lax.rem(z + k, 4) for k in (1, 2, 3)]
    barrier = pltpu.get_barrier_semaphore()
    for peer in [x_peer, y_peer, sibling_peer] + z_peers:
        pl.semaphore_signal(barrier, inc=1, device_id=peer, device_id_type=MESH)
    pl.semaphore_wait(barrier, 6)
    sent = []

    def send(src, dst, peer):
        i = len(sent)
        copy = pltpu.make_async_remote_copy(
            src_ref=src,
            dst_ref=dst,
            send_sem=send_sem.at[i],
            recv_sem=recv_sem.at[i],
            device_id=peer,
            device_id_type=MESH,
        )
        copy.start()
        sent.append(copy)
        return copy

    def plus(a, b):
        return (a.astype(F32) + b.astype(F32)).astype(BF16)

    def first_phase(up_other, low_other, up_buffer, low_buffer):
        return send(up_other, up_buffer, y_peer), send(low_other, low_buffer, x_peer)

    far_g = send(g_ref, gf_ref, z_peers[1])
    b_up = send(gb_ref.at[1, 0], b1_up, y_peer)
    b_low = send(gb_ref.at[:, 1, :, 1 - x], b1_low, x_peer)
    lax.fori_loop(0, blocks, queries, 0)
    far_g.wait_recv()
    lax.fori_loop(0, blocks, keys, 0)

    vec_rows = vec_ref.shape[0]
    vec1[0, 0:vec_rows] = vec_ref[...]
    vec1[0, vec_rows : vec_rows + 8], vec1[0, vec_rows + 8 : vec_rows + 16] = bias_totals(
        member, pair, total_ref
    )
    v_sib = send(vec1.at[0], vec1.at[1], sibling_peer)

    halves = gb_ref.shape[2]

    def add_up(i, carry):
        b1_up[i] = plus(b1_up[i], gb_ref[0, 0, i])
        return carry

    def add_low(i, carry):
        for p in range(2):
            b1_low[p, i] = plus(b1_low[p, i], gb_ref[p, 1, i, x])
        return carry

    b_up.wait_recv()
    lax.fori_loop(0, halves, add_up, 0)
    b_up = send(b1_up.at[:, 1 - x], b2.at[0], x_peer)
    b_low.wait_recv()
    lax.fori_loop(0, halves, add_low, 0)
    b_low = send(b1_low.at[1], b2.at[1], y_peer)
    v_sib.wait_recv()
    vec1[2] = vec1[0] + vec1[1]
    v_y = send(vec1.at[2], vec1.at[3], y_peer)

    lax.fori_loop(0, 2, weights, 0)
    half = ga_ref.shape[3] // 2
    up, low = slice(0, half), slice(half, 2 * half)
    a_up = send(ga_ref.at[1, :, :, pl.ds(0, half)], a1_up, y_peer)
    a_low = send(ga_ref.at[:, :, 1 - x, pl.ds(half, half)], a1_low, x_peer)

    def rows_other(b, carry):
        term_ref[b] = back_rows(1, b, wa_ref, dt_ref).astype(BF16)
        return carry

    lax.fori_loop(0, blocks, rows_other, 0)
    term = send(term_ref, near_ref, sibling_peer)

    b_up.wait_recv()
    b_low.wait_recv()

    def add_second(i, carry):
        b2[0, i] = plus(b2[0, i], b1_up[i, x])
        b2[1, i] = plus(b2[1, i], b1_low[0, i])
        return carry

    lax.fori_loop(0, halves, add_second, 0)
    b_z = [send(b2.at[:, to], b3.at[k], peer) for k, (to, peer) in enumerate(zip(z_to, z_peers))]
    v_y.wait_recv()
    vec1[4] = vec1[2] + vec1[3]
    v_x = send(vec1.at[4], vec1.at[5], x_peer)

    a_up.wait_recv()

    def a_add_up(i, carry):
        a1_up[i] = plus(a1_up[i], ga_ref[0, i, :, up])
        return carry

    lax.fori_loop(0, halves, a_add_up, 0)
    a_up = send(a1_up.at[:, 1 - x], a2.at[0], x_peer)
    a_low.wait_recv()

    def a_add_low(i, carry):
        for p in range(2):
            a1_low[p, i] = plus(a1_low[p, i], ga_ref[p, i, x, low])
        return carry

    lax.fori_loop(0, halves, a_add_low, 0)
    a_low = send(a1_low.at[1], a2.at[1], y_peer)

    cap = df_ref.shape[1] // 2
    quarter = rows_ref.shape[2]
    term.wait_recv()

    def rows_own(b, carry):
        own = back_rows(0, b, wa_ref, dt_ref) + near_ref[b].astype(F32)
        for e in range(2):
            first = df_ref[b, cap * e : cap * (e + 1), :]
            high = first.astype(BF16)
            rest = (first - high.astype(F32)).astype(BF16)
            chosen = select_ref[b, cap * e : cap * (e + 1), :]
            spread = t_mm(chosen, high) + t_mm(chosen, rest)
            rows_ref[e, b] = (own[quarter * e : quarter * (e + 1)] + spread).astype(BF16)
        return carry

    lax.fori_loop(0, blocks, rows_own, 0)
    moved = send(rows_ref.at[1 - pair], gx_ref.at[pair], y_peer)
    kept = pltpu.make_async_copy(rows_ref.at[pair], gx_ref.at[pair], local_sem.at[0])
    kept.start()
    v_x.wait_recv()
    vec1[6] = vec1[4] + vec1[5]
    own_vec = pltpu.make_async_copy(vec1.at[6], vec4.at[z], local_sem.at[1])
    own_vec.start()
    v_z = [send(vec1.at[6], vec4.at[z], peer) for peer in z_peers]

    a_up.wait_recv()
    a_low.wait_recv()

    def a_add_second(i, carry):
        a2[0, i] = plus(a2[0, i], a1_up[i, x])
        a2[1, i] = plus(a2[1, i], a1_low[0, i])
        return carry

    lax.fori_loop(0, halves, a_add_second, 0)
    a_z = [send(a2.at[:, to], a3.at[k], peer) for k, (to, peer) in enumerate(zip(z_to, z_peers))]

    for copy in b_z:
        copy.wait_recv()
    for t in range(2):
        total = b2[t, z].astype(F32)
        for k in range(3):
            total = total + b3[k, t].astype(F32)
        if t == 0:
            gu_ref[...] = total
        else:
            gd_ref[...] = total
    own_vec.wait()
    for copy in v_z:
        copy.wait_recv()
    store_vectors(
        (vec4[0] + vec4[1]) + (vec4[2] + vec4[3]),
        (v1_ref, v2_ref, v3_ref, v4_ref, v5_ref, v6_ref, v7_ref, v8_ref, v9_ref),
    )
    for copy in a_z:
        copy.wait_recv()
    halves_of_a = []
    for t in range(2):
        total = a2[t, z].astype(F32)
        for k in range(3):
            total = total + a3[k, t].astype(F32)
        halves_of_a.append(total)
    total = jnp.concatenate(halves_of_a, axis=0)
    last = total[:, 384:512], total[:, 512:640]
    seconds = [pltpu.roll(tile, HD, 1) for tile in last]
    for ref, i, tile in ((gq_ref, 0, last[0]), (gk_ref, 1, seconds[0]), (gv_ref, 2, last[1])):
        ref[:, 0:128] = total[:, 128 * i : 128 * (i + 1)]
        ref[:, 128:192] = tile[:, 0:HD]
    go_ref[0:128, :] = total[:, 640:768].T
    go_ref[128:192, :] = seconds[1].T[0:HD, :]
    kept.wait()
    moved.wait_recv()
    for copy in sent:
        copy.wait_send()


def backward(gb, q_far, q_compact, d_attention, keys, values, keys_used, values_used, attention, rows_t, w_attn, select, small, far, d_branch, d_first, vectors):
    n = lax.axis_size("dp")
    _, blocks, block_half, lanes = keys.shape
    width = rows_t.shape[0]
    quarter = block_half // 2
    piece = width // n
    slots = select.shape[1]
    vec_rows = vectors.shape[0] + 16
    sizes = [width] * 6 + [4 * width] + [width] * 2

    def out(*shape, dtype=BF16):
        return jax.ShapeDtypeStruct(shape, dtype)

    compact = (2, blocks, slots // 2, lanes)
    scratch = [
        pltpu.VMEM((2, 2, blocks, block_half, 640), BF16),
        pltpu.VMEM((2, 2, blocks, slots // 2, 256), BF16),
    ]
    shared = (q_compact, d_attention, keys, values, keys_used, values_used, attention, rows_t, w_attn, select, small, far, d_branch)
    if n == 8:
        half = piece // 2
        return pl.pallas_call(
            functools.partial(back_kernel, True),
            out_shape=[
                out(2, blocks, quarter, width),
                out(piece, width // 4, dtype=F32),
                out(piece, width // 4, dtype=F32),
                out(piece, width // 4, dtype=F32),
                out(width // 4, piece, dtype=F32),
                out(piece, width, dtype=F32),
                out(piece, width, dtype=F32),
            ]
            + [out(size, dtype=F32) for size in sizes],
            in_specs=[vmem_spec()] * 17,
            out_specs=[vmem_spec()] * (7 + len(sizes)),
            scratch_shapes=scratch
            + [
                pltpu.VMEM((2, 4, 2, piece, width), BF16),
                pltpu.VMEM((8, lanes), F32),
                pltpu.VMEM(compact, BF16),
                pltpu.VMEM((blocks, block_half, width), BF16),
                pltpu.VMEM((blocks, block_half, width), BF16),
                pltpu.VMEM((2, blocks, quarter, width), BF16),
                pltpu.VMEM((4, 2, piece, width), BF16),
                pltpu.VMEM((2, 4, piece, width), BF16),
                pltpu.VMEM((2, 4, piece, width), BF16),
                pltpu.VMEM((3, 2, piece, width), BF16),
                pltpu.VMEM((4, 2, half, width), BF16),
                pltpu.VMEM((2, 4, half, width), BF16),
                pltpu.VMEM((2, 4, half, width), BF16),
                pltpu.VMEM((3, 2, half, width), BF16),
                pltpu.VMEM((7, vec_rows, 128), F32),
                pltpu.VMEM((4, vec_rows, 128), F32),
                pltpu.SemaphoreType.DMA((2,)),
                pltpu.SemaphoreType.DMA((24,)),
                pltpu.SemaphoreType.DMA((24,)),
            ],
            compiler_params=pltpu.CompilerParams(
                collective_id=2, vmem_limit_bytes=62 * 2**20, has_side_effects=True
            ),
        )(gb.reshape(2, 2, 4, 2, piece, width), q_far, *shared, d_first, vectors)
    ga, term, both = pl.pallas_call(
        functools.partial(back_kernel, False),
        out_shape=[
            out(2, 1, 1, width, width),
            out(2, blocks, block_half, width, dtype=F32),
            out(16, 128, dtype=F32),
        ],
        in_specs=[vmem_spec()] * 15,
        out_specs=[vmem_spec()] * 3,
        scratch_shapes=scratch + [pltpu.VMEM((8, lanes), F32)],
        compiler_params=pltpu.CompilerParams(vmem_limit_bytes=62 * 2**20),
    )(q_far, partner(d_attention), *shared)
    pair = lax.axis_index("head") // 2
    cap = slots // 4
    chosen = select[:, : 2 * cap].reshape(blocks, 2, cap, quarter).astype(F32)
    spread = jnp.einsum(
        "bekr,bekw->berw",
        chosen,
        d_first.reshape(blocks, 2, cap, width),
        precision=lax.Precision.HIGHEST,
    )
    own = term[0].reshape(spread.shape) + sibling(term[1].astype(BF16)).astype(F32).reshape(spread.shape)
    own = (own + spread).astype(BF16)
    grad_x = ordered(pair, pick(own, pair, 1), across(pick(own, 1 - pair, 1)))
    pieces = (2, n, piece, width)
    s_attn = reduce_scatter(ga.reshape(pieces), True)
    s_feed = jnp.stack([reduce_scatter(gb[:, i].reshape(pieces), True) for i in range(2)])
    summed = lax.psum(jnp.concatenate((vectors, both)), ("dp", "head"))
    whole, ends, start = summed.reshape(-1), [], 0
    for size in sizes[:7]:
        ends.append(whole[start : start + size])
        start += size
    last = summed[vectors.shape[0] :].reshape(2, 2, 4, 128)
    ends += [
        jnp.concatenate((last[0, i], last[1, i, :, :HD]), axis=-1).reshape(-1) for i in range(2)
    ]

    def columns_of(i, j, second):
        at = 128 * j + HD * second
        return jnp.concatenate((s_attn[:, 128 * i : 128 * (i + 1)], s_attn[:, at : at + HD]), axis=1)

    return (
        grad_x,
        columns_of(0, 3, 0),
        columns_of(1, 3, 1),
        columns_of(2, 4, 0),
        columns_of(5, 4, 1).T,
        s_feed[0],
        s_feed[1],
        *ends,
    )


def deliver_kernel(*refs):
    count = (len(refs) - 1) // 2
    copies = [
        pltpu.make_async_copy(refs[i], refs[count + i], refs[-1].at[i]) for i in range(count)
    ]
    for copy in copies:
        copy.start()
    for copy in copies:
        copy.wait()


def deliver(arrays):
    return pl.pallas_call(
        deliver_kernel,
        out_shape=[jax.ShapeDtypeStruct(array.shape, array.dtype) for array in arrays],
        in_specs=[vmem_spec()] * len(arrays),
        out_specs=[any_spec()] * len(arrays),
        scratch_shapes=[pltpu.SemaphoreType.DMA((len(arrays),))],
    )(*arrays)


def per_device(
    tokens,
    query_weight,
    query_bias,
    key_weight,
    value_weight,
    value_bias,
    out_weight,
    out_bias,
    first_gain,
    first_shift,
    up_weight,
    up_bias,
    down_weight,
    down_bias,
    second_gain,
    second_shift,
    block_order,
    masked_rows,
    out_grad,
):
    block_count, block_rows, width = tokens.shape
    quarter = block_rows // 4
    hidden_piece = up_weight.shape[1]
    head = lax.axis_index("head")
    c, p = head % 2, head // 2

    lines = (
        query_bias,
        value_bias,
        block_order.astype(F32),
        up_bias,
        out_bias,
        first_gain,
        first_shift,
        down_bias,
        second_gain,
        second_shift,
    )
    flat = []
    for vector in lines:
        flat += [vector, jnp.zeros((hidden_piece - vector.shape[0],), F32)]
    flat.append(jnp.zeros((6 * hidden_piece,), F32))
    small = jnp.concatenate(flat).reshape(16, hidden_piece)
    (
        w_attn, w_feed, x_rows, rows_t, attention, keys, values, keys_used, values_used, q_compact, picks_b, select_b, small_far,
    ) = forward(
        tokens,
        (query_weight, key_weight, value_weight, out_weight, up_weight, down_weight.T),
        small,
        masked_rows,
        c,
        p,
    )

    out_y, gb, d_attention, d_branch_all, d_first, flat, q_far = middle(
        w_attn, w_feed, x_rows, attention, select_b, picks_b, out_grad, small, small_far, q_compact
    )
    grad_x, g_query, g_key, g_value, g_out, g_up, g_down, *ends = backward(
        gb, q_far, q_compact, d_attention, keys, values, keys_used, values_used, attention, rows_t, w_attn, select_b,
        small, small_far, d_branch_all, d_first, flat,
    )
    (
        v_out_bias, v_first_gain, v_first_shift, v_down_bias, v_second_gain, v_second_shift, v_up_bias, v_query_bias, v_value_bias,
        out_y, grad_x, g_query, g_key, g_value, g_out, g_up, g_down,
    ) = deliver((*ends, out_y, grad_x, g_query, g_key, g_value, g_out, g_up, g_down))

    out_y = out_y.reshape(block_count, quarter, width)
    grad_x = grad_x.reshape(block_count, quarter, width)

    return (
        out_y,
        grad_x,
        g_query,
        v_query_bias,
        g_key,
        g_value,
        v_value_bias,
        g_out,
        v_out_bias,
        v_first_gain,
        v_first_shift,
        g_up,
        v_up_bias,
        g_down.T,
        v_down_bias,
        v_second_gain,
        v_second_shift,
    )


def solution(mesh):
    in_specs = (
        P("dp", None, None),
        P("dp", "head"),
        P("head"),
        P("dp", "head"),
        P("dp", "head"),
        P("head"),
        P("head", "dp"),
        P(),
        P(),
        P(),
        P("dp", "head"),
        P("head"),
        P("head", "dp"),
        P(),
        P(),
        P(),
        P("head"),
        P("dp", None),
        P("dp", None, None),
    )
    out_specs = (
        P("dp", "head", None),
        P("dp", "head", None),
        P("dp", "head"),
        P(),
        P("dp", "head"),
        P("dp", "head"),
        P(),
        P("head", "dp"),
        P(),
        P(),
        P(),
        P("dp", "head"),
        P(),
        P("head", "dp"),
        P(),
        P(),
        P(),
    )
    return jax.shard_map(
        per_device, mesh=mesh, in_specs=in_specs, out_specs=out_specs, check_vma=False
    )
```
